32 devices in a mesh: grp: 4 (over y, x), seq: 8 (over z, core).
Axes of the slice: x: 2, y: 2, z: 4, core: 2. Of those that a mesh axis runs over, the one named last changes fastest.
Arguments:
- tokens: bfloat16 [20480, 1024], P(('grp', 'seq')), may hold values from -6 to 6
- cotangent: bfloat16 [20480, 1024], P(('grp', 'seq')), may hold values from -6 to 6
- query_key_value_weight: bfloat16 [3145728], P(('grp', 'seq')), may hold values from -0.1875 to 0.1875
- attention_out_weight: bfloat16 [1048576], P(('grp', 'seq')), may hold values from -1.5 to 1.5
- feedforward_in_weight: bfloat16 [4194304], P(('grp', 'seq')), may hold values from -0.1875 to 0.1875
- feedforward_out_weight: bfloat16 [4194304], P(('grp', 'seq')), may hold values from -0.09375 to 0.09375
- layer_norm_gains: float32 [2, 1024], replicated, may hold values from 0.25 to 1.75
- biases: float32 [10240], replicated, may hold values from -1.75 to 1.75
- adapter_down_matrices: bfloat16 [917504], P(('grp', 'seq')), may hold values from -0.1875 to 0.1875
- adapter_up_matrices: bfloat16 [1179648], P(('grp', 'seq')), may hold values from -0.75 to 0.75
- adapter_of_continuation: int32 [32, 1], P(('grp', 'seq')), may hold values from 0 to 7
Outputs:
- activations: bfloat16 [20480, 1024], P(('grp', 'seq'))
- input_grad: float32 [20480, 1024], P(('grp', 'seq'))
- down_grad: float32 [917504], P(('grp', 'seq'))
- up_grad: float32 [1179648], P(('grp', 'seq'))
The draws below stay inside these ranges and needn't reach their ends.
Inputs may be any that keep to these rules, and one draw needn't show every extreme that they name: `adapter_of_continuation`: every one of the 8 adapters is named by some continuation.
All inputs are finite; a program needn't handle non-finite values.
Results may differ from the reference program's by a relative error of at most 0.012.
Values may be sent and summed in bfloat16 or wider, within the bound.
A program may use at most 256 MiB of HBM per device.

```python
import jax
import jax.numpy as jnp
from jax import lax

MODEL_WIDTH = 1024
HEADS = 16
HEAD_DIM = 64
HIDDEN_UNITS = 4096
ADAPTER_RANK = 16
ADAPTER_COUNT = 8
GROUPS = 4
SPLITS = 8
PB = 128
PROMPT = 1024
ROWS_DEV = 640
KEYS = 1536
CONTS = 32
TOKENS = 20480


def block_levels(rng, shape, shards, low, top_value):
    gain, own = 1.0, jax.random.fold_in(rng, 6)
    for axis_at, shards_of in shards:
        heights = jnp.exp(jax.random.uniform(jax.random.fold_in(own, axis_at), (shards_of,), jnp.float32, low / len(shards), top_value / len(shards)))
        gain = gain * jnp.repeat(heights, shape[axis_at] // shards_of).reshape([-1 if axis == axis_at else 1 for axis in range(len(shape))])
    return gain


def picks_of(own_key, rows, count, top, lift):
    sequence = jax.random.permutation(jax.random.fold_in(own_key, 1), count)
    pull = sequence
    for power in range(3):
        pull = pull * pull // count
    pull = pull * lift // count
    chance = jax.random.randint(jax.random.fold_in(own_key, 2), (rows, count), 0, 4096) + pull
    holders = jax.random.permutation(jax.random.fold_in(own_key, 3), rows)[jnp.arange(count) % rows]
    chance = jnp.where(jnp.arange(rows)[:, None] == holders[None, :], 1 << 14, chance)
    merit = chance * count + jnp.arange(count)
    return lax.top_k(merit.astype(jnp.int32), top)[1].astype(jnp.int32)


def gaussian(own_key, shape, width, most, split=(), held_as=jnp.bfloat16):
    drawn = jax.random.normal(own_key, shape, jnp.float32) * width
    if len(split) > 0:
        drawn = block_levels(own_key, shape, split, -0.22, 0.18) * drawn
    return jnp.clip(drawn, min=-most, max=most).astype(held_as)


def setup_inputs(seed: int = 0) -> dict:
    streams_of = jax.random.split(jax.random.key(seed), 12)
    tokens = gaussian(streams_of[0], (TOKENS, MODEL_WIDTH), 1.0, 6.0, ((0, 32),))
    cotangent = gaussian(streams_of[1], (TOKENS, MODEL_WIDTH), 1.0, 6.0, ((0, 32),))
    query_key_value_weight = gaussian(streams_of[2], (3 * MODEL_WIDTH * MODEL_WIDTH,), MODEL_WIDTH ** -0.5, 0.1875, ((0, 32),))
    attention_out_weight = gaussian(streams_of[3], (MODEL_WIDTH * MODEL_WIDTH,), (MODEL_WIDTH // 64) ** -0.5, 1.5, ((0, 32),))
    feedforward_in_weight = gaussian(streams_of[4], (MODEL_WIDTH * HIDDEN_UNITS,), MODEL_WIDTH ** -0.5, 0.1875, ((0, 32),))
    feedforward_out_weight = gaussian(streams_of[5], (HIDDEN_UNITS * MODEL_WIDTH,), HIDDEN_UNITS ** -0.5, 0.09375, ((0, 32),))
    layer_norm_gains = jnp.clip(1.0 + 0.15 * jax.random.normal(streams_of[6], (2, MODEL_WIDTH), jnp.float32), 0.25, 1.75)
    biases = gaussian(streams_of[7], (6 * MODEL_WIDTH + HIDDEN_UNITS,), 0.3, 1.75, (), jnp.float32)
    adapter_down_matrices = gaussian(streams_of[8], (ADAPTER_COUNT * (3 * MODEL_WIDTH + HIDDEN_UNITS) * ADAPTER_RANK,), MODEL_WIDTH ** -0.5, 0.1875, ((0, 32),))
    adapter_up_matrices = gaussian(streams_of[9], (ADAPTER_COUNT * ADAPTER_RANK * (5 * MODEL_WIDTH + HIDDEN_UNITS),), (4 * ADAPTER_RANK) ** -0.5, 0.75, ((0, 32),))
    adapter_of_continuation = picks_of(streams_of[10], CONTS, ADAPTER_COUNT, 1, 1024)
    return {"tokens": tokens, "cotangent": cotangent, "query_key_value_weight": query_key_value_weight, "attention_out_weight": attention_out_weight, "feedforward_in_weight": feedforward_in_weight, "feedforward_out_weight": feedforward_out_weight, "layer_norm_gains": layer_norm_gains, "biases": biases, "adapter_down_matrices": adapter_down_matrices, "adapter_up_matrices": adapter_up_matrices, "adapter_of_continuation": adapter_of_continuation}


@jax.custom_vjp
def low_rank_state(v):
    return lax.optimization_barrier(v.astype(jnp.bfloat16)).astype(jnp.float32)

@jax.custom_vjp
def low_rank_gradient(v):
    return v

def low_keep(v):
    return (low_rank_state(v), None)

def low_pass(kept, grad):
    return (grad,)

def back_keep(v):
    return (v, None)

def back_low(kept, grad):
    return (low_rank_state(grad),)
low_rank_state.defvjp(low_keep, low_pass)
low_rank_gradient.defvjp(back_keep, back_low)
EPSILON = 1e-05
NEGATIVE = -1e+30

def matrix_multiply(left_side, right_side):
    return jnp.dot(left_side, right_side, precision=lax.Precision.HIGHEST, preferred_element_type=jnp.float32)

def layer_norm(values, gain_vec, shift_vec):
    row_mean = lax.optimization_barrier(jnp.mean(values, axis=-1, keepdims=True))
    centred = values - row_mean
    row_var = lax.optimization_barrier(jnp.mean(centred * centred, axis=-1, keepdims=True))
    return centred * lax.rsqrt(row_var + EPSILON) * gain_vec + shift_vec

def adapter_pieces(every_down_matrix, every_up_matrix, adapter_index):
    down_rows = lax.dynamic_index_in_dim(every_down_matrix, adapter_index, 0, keepdims=False)
    up_cols = lax.dynamic_index_in_dim(every_up_matrix, adapter_index, 0, keepdims=False)
    return (down_rows[:MODEL_WIDTH], down_rows[MODEL_WIDTH:2 * MODEL_WIDTH], down_rows[2 * MODEL_WIDTH:3 * MODEL_WIDTH], down_rows[3 * MODEL_WIDTH:], up_cols[:, :3 * MODEL_WIDTH], up_cols[:, 3 * MODEL_WIDTH:4 * MODEL_WIDTH], up_cols[:, 4 * MODEL_WIDTH:4 * MODEL_WIDTH + HIDDEN_UNITS], up_cols[:, 4 * MODEL_WIDTH + HIDDEN_UNITS:])

def continuation_token_rows():
    return (jnp.arange(ROWS_DEV, dtype=jnp.int32) >= PB).astype(jnp.float32)[:, None]

def visible(seq_index):
    row_ids = jnp.arange(ROWS_DEV, dtype=jnp.int32)[:, None]
    col_ids = jnp.arange(KEYS, dtype=jnp.int32)[None, :]
    in_prompt = col_ids < PROMPT
    prompt_seen = in_prompt & (col_ids <= seq_index * PB + row_ids)
    later_seen = in_prompt | (col_ids - PROMPT <= row_ids - PB)
    return jnp.where(row_ids < PB, prompt_seen, later_seen)

def first_section(token_block, adapter_index, every_down_matrix, every_up_matrix, frozen):
    frozen_query_key_value, frozen_attention_out, frozen_feedforward_in, frozen_feedforward_out, gains_all, every_bias = frozen
    adapter_sections = adapter_pieces(every_down_matrix, every_up_matrix, adapter_index)
    normalized_rows = low_rank_state(layer_norm(token_block, gains_all[0], every_bias[:MODEL_WIDTH]))
    query_key_value_bias = jnp.concatenate([every_bias[2 * MODEL_WIDTH:3 * MODEL_WIDTH], jnp.zeros((MODEL_WIDTH,), jnp.float32), every_bias[3 * MODEL_WIDTH:4 * MODEL_WIDTH]])
    query_key_value_inner = low_rank_state(low_rank_gradient(matrix_multiply(normalized_rows, adapter_sections[0])))
    mixed_query_key_value = matrix_multiply(normalized_rows, frozen_query_key_value) + query_key_value_bias + continuation_token_rows() * matrix_multiply(query_key_value_inner, adapter_sections[4])
    return low_rank_state(low_rank_gradient(mixed_query_key_value))

def attend(qkv_block, seq_index, prompt_keys, prompt_values):
    query_all = qkv_block[:, :MODEL_WIDTH].reshape(ROWS_DEV, HEADS, HEAD_DIM)
    all_keys = jnp.concatenate([prompt_keys, qkv_block[PB:, MODEL_WIDTH:2 * MODEL_WIDTH]], 0).reshape(KEYS, HEADS, HEAD_DIM)
    all_values = jnp.concatenate([prompt_values, qkv_block[PB:, 2 * MODEL_WIDTH:]], 0).reshape(KEYS, HEADS, HEAD_DIM)
    scores = low_rank_gradient(jnp.einsum('qhd,khd->hqk', query_all, all_keys, precision=lax.Precision.HIGHEST) * 0.125)
    scores = jnp.where(visible(seq_index)[None], scores, NEGATIVE)
    row_max = lax.optimization_barrier(jnp.max(scores, axis=2, keepdims=True))
    exp_scores = jnp.exp(scores - row_max)
    probs = exp_scores / lax.optimization_barrier(jnp.sum(exp_scores, axis=2, keepdims=True))
    attention_context = jnp.einsum('hqk,khd->qhd', low_rank_state(probs), all_values, precision=lax.Precision.HIGHEST)
    return low_rank_state(low_rank_gradient(attention_context.reshape(ROWS_DEV, MODEL_WIDTH)))

def second_section(token_block, attention_context, adapter_index, every_down_matrix, every_up_matrix, frozen):
    frozen_query_key_value, frozen_attention_out, frozen_feedforward_in, frozen_feedforward_out, gains_all, every_bias = frozen
    adapter_sections = adapter_pieces(every_down_matrix, every_up_matrix, adapter_index)
    section_marker = continuation_token_rows()
    attention_out_inner = low_rank_state(low_rank_gradient(matrix_multiply(attention_context, adapter_sections[1])))
    attention_output = low_rank_gradient(matrix_multiply(attention_context, frozen_attention_out) + every_bias[4 * MODEL_WIDTH:5 * MODEL_WIDTH] + section_marker * matrix_multiply(attention_out_inner, adapter_sections[5]))
    hidden = token_block + attention_output
    normalized_rows = low_rank_state(layer_norm(hidden, gains_all[1], every_bias[MODEL_WIDTH:2 * MODEL_WIDTH]))
    feedforward_in_inner = low_rank_state(low_rank_gradient(matrix_multiply(normalized_rows, adapter_sections[2])))
    before_activation = low_rank_gradient(matrix_multiply(normalized_rows, frozen_feedforward_in) + every_bias[6 * MODEL_WIDTH:] + section_marker * matrix_multiply(feedforward_in_inner, adapter_sections[6]))
    activated_hidden = low_rank_state(jax.nn.gelu(before_activation, approximate=True))
    feedforward_out_inner = low_rank_state(low_rank_gradient(matrix_multiply(activated_hidden, adapter_sections[3])))
    adapter_branch = low_rank_gradient(matrix_multiply(activated_hidden, frozen_feedforward_out) + every_bias[5 * MODEL_WIDTH:6 * MODEL_WIDTH] + section_marker * matrix_multiply(feedforward_out_inner, adapter_sections[7]))
    return hidden + adapter_branch

def group_forward(tokens_group, every_down_matrix, every_up_matrix, ids_group, frozen):
    first_fn = jax.checkpoint(first_section)
    qkv_all = lax.map(lambda operands: first_fn(operands[0], operands[1], every_down_matrix, every_up_matrix, frozen), (tokens_group, ids_group))
    prompt_keys = qkv_all[:, :PB, MODEL_WIDTH:2 * MODEL_WIDTH].reshape(PROMPT, MODEL_WIDTH)
    prompt_values = qkv_all[:, :PB, 2 * MODEL_WIDTH:].reshape(PROMPT, MODEL_WIDTH)
    mixer_fn = jax.checkpoint(attend)
    attention_context = lax.map(lambda operands: mixer_fn(operands[0], operands[1], prompt_keys, prompt_values), (qkv_all, jnp.arange(SPLITS, dtype=jnp.int32)))
    second_fn = jax.checkpoint(second_section)
    return lax.map(lambda operands: second_fn(operands[0], operands[1], operands[2], every_down_matrix, every_up_matrix, frozen), (tokens_group, attention_context, ids_group))

def reference(tokens, cotangent, query_key_value_weight, attention_out_weight, feedforward_in_weight, feedforward_out_weight, layer_norm_gains, biases, adapter_down_matrices, adapter_up_matrices, adapter_of_continuation):
    frozen = (query_key_value_weight.astype(jnp.float32).reshape(MODEL_WIDTH, 3 * MODEL_WIDTH), attention_out_weight.astype(jnp.float32).reshape(MODEL_WIDTH, MODEL_WIDTH), feedforward_in_weight.astype(jnp.float32).reshape(MODEL_WIDTH, HIDDEN_UNITS), feedforward_out_weight.astype(jnp.float32).reshape(HIDDEN_UNITS, MODEL_WIDTH), layer_norm_gains, biases)
    every_down_matrix = adapter_down_matrices.astype(jnp.float32).reshape(ADAPTER_COUNT, 3 * MODEL_WIDTH + HIDDEN_UNITS, ADAPTER_RANK)
    every_up_matrix = adapter_up_matrices.astype(jnp.float32).reshape(ADAPTER_COUNT, ADAPTER_RANK, 5 * MODEL_WIDTH + HIDDEN_UNITS)
    tokens_all = tokens.astype(jnp.float32).reshape(GROUPS, SPLITS, ROWS_DEV, MODEL_WIDTH)
    cotangent_all = cotangent.astype(jnp.float32).reshape(GROUPS, SPLITS, ROWS_DEV, MODEL_WIDTH)
    ids_all = adapter_of_continuation.reshape(GROUPS, SPLITS).astype(jnp.int32)

    def per_group(totals, operands):
        tokens_group, cotangent_group, ids_group = operands
        result, pull_back = jax.vjp(lambda token_vals, down_vals, up_vals: group_forward(token_vals, down_vals, up_vals, ids_group, frozen), tokens_group, every_down_matrix, every_up_matrix)
        grad_tokens, grad_down, grad_up = pull_back(cotangent_group)
        return ((totals[0] + grad_down, totals[1] + grad_up), (result.astype(jnp.bfloat16), grad_tokens))
    start_sums = (jnp.zeros((ADAPTER_COUNT, 3 * MODEL_WIDTH + HIDDEN_UNITS, ADAPTER_RANK), jnp.float32), jnp.zeros((ADAPTER_COUNT, ADAPTER_RANK, 5 * MODEL_WIDTH + HIDDEN_UNITS), jnp.float32))
    sums_out, outputs = lax.scan(per_group, start_sums, (tokens_all, cotangent_all, ids_all))
    activations = outputs[0].reshape(TOKENS, MODEL_WIDTH)
    input_grad = outputs[1].reshape(TOKENS, MODEL_WIDTH)
    return (activations, input_grad, sums_out[0].reshape(-1), sums_out[1].reshape(-1))
```

```python
import functools

import jax
import jax.numpy as jnp
from jax import lax
from jax.experimental import pallas as pl
from jax.experimental.pallas import tpu as pltpu
from jax.sharding import PartitionSpec as P

MODEL_WIDTH = 1024
HEADS = 16
HEAD_DIM = 64
HIDDEN_UNITS = 4096
ADAPTER_RANK = 16
ADAPTER_COUNT = 8
CONT_LEN = 512


EPSILON = 1e-05
NEGATIVE = -1e30


def product(left_side, right_side):
    return jnp.dot(left_side, right_side, preferred_element_type=jnp.float32)


def product_tn(left_side, right_side):
    return lax.dot_general(
        left_side, right_side, (((0,), (0,)), ((), ())), preferred_element_type=jnp.float32
    )


def product_nt(left_side, right_side):
    return lax.dot_general(
        left_side, right_side, (((1,), (1,)), ((), ())), preferred_element_type=jnp.float32
    )


def layer_norm(values, gain_vec, shift_vec):
    row_mean = jnp.mean(values, axis=-1, keepdims=True)
    centred = values - row_mean
    row_var = jnp.mean(centred * centred, axis=-1, keepdims=True)
    return centred * lax.rsqrt(row_var + EPSILON) * gain_vec + shift_vec


def unpack_sections(pieces, adapter_index):
    qkv_flat, out_flat, fc_flat, proj_flat, down_flat, up_flat = pieces
    every_down_matrix = down_flat.reshape(
        ADAPTER_COUNT, 3 * MODEL_WIDTH + HIDDEN_UNITS, ADAPTER_RANK
    )
    every_up_matrix = up_flat.reshape(ADAPTER_COUNT, ADAPTER_RANK, 5 * MODEL_WIDTH + HIDDEN_UNITS)
    down_rows = lax.dynamic_index_in_dim(every_down_matrix, adapter_index, 0, keepdims=False)
    up_cols = lax.dynamic_index_in_dim(every_up_matrix, adapter_index, 0, keepdims=False)
    weight_matrices = (
        qkv_flat.reshape(MODEL_WIDTH, 3 * MODEL_WIDTH),
        out_flat.reshape(MODEL_WIDTH, MODEL_WIDTH),
        fc_flat.reshape(MODEL_WIDTH, HIDDEN_UNITS),
        proj_flat.reshape(HIDDEN_UNITS, MODEL_WIDTH),
    )
    adapter_sections = (
        down_rows[:MODEL_WIDTH],
        down_rows[MODEL_WIDTH : 2 * MODEL_WIDTH],
        down_rows[2 * MODEL_WIDTH : 3 * MODEL_WIDTH],
        down_rows[3 * MODEL_WIDTH :],
        up_cols[:, : 3 * MODEL_WIDTH],
        up_cols[:, 3 * MODEL_WIDTH : 4 * MODEL_WIDTH],
        up_cols[:, 4 * MODEL_WIDTH : 4 * MODEL_WIDTH + HIDDEN_UNITS],
        up_cols[:, 4 * MODEL_WIDTH + HIDDEN_UNITS :],
    )
    return (weight_matrices, adapter_sections)


def visible(row_count, prompt_rows, prompt_total, key_count, seq_index):
    row_ids = jnp.arange(row_count, dtype=jnp.int32)[:, None]
    col_ids = jnp.arange(key_count, dtype=jnp.int32)[None, :]
    in_prompt = col_ids < prompt_total
    prompt_seen = in_prompt & (col_ids <= seq_index * prompt_rows + row_ids)
    later_seen = in_prompt | (col_ids - prompt_total <= row_ids - prompt_rows)
    return jnp.where(row_ids < prompt_rows, prompt_seen, later_seen)


def split_heads(values):
    return values.reshape(values.shape[0], HEADS, HEAD_DIM).transpose(1, 0, 2)


def merge_heads(values):
    return values.transpose(1, 0, 2).reshape(values.shape[1], HEADS * HEAD_DIM)


MESH = pl.DeviceIdType.MESH
SCALE2 = 0.125 * 1.4426950408889634
VMEM_LIMIT = 60 << 20


def gather_stages(groups, sizes, chunks, ins, outs, sems):
    grp_n, seq_n = groups
    z_n, y_n = seq_n // 2, grp_n // 2
    z_sem, x_sem, y_sem, d_sem, p_sem, s_sem, l_sem = sems
    g, s = lax.axis_index("grp"), lax.axis_index("seq")
    core, z = lax.rem(s, 2), s // 2
    gx, gy = lax.rem(g, 2), g // 2
    partner = (g, z * 2 + 1 - core)
    other_x = gy * 2 + 1 - gx
    x_next = (other_x, s)
    far_z = [lax.rem(z + d, z_n) for d in range(1, z_n)]
    far_y = [lax.rem(gy + d, y_n) for d in range(1, y_n)]
    y_next = [(y * 2 + gx, s) for y in far_y]

    def enter():
        peers = [partner, x_next] + y_next + [(g, far * 2 + core) for far in far_z]
        barrier = pltpu.get_barrier_semaphore()
        for peer in peers:
            pl.semaphore_signal(barrier, inc=1, device_id=peer, device_id_type=MESH)
        pl.semaphore_wait(barrier, len(peers))

    def place(ch, gg, ss):
        arr, row, rows, full = chunks[ch]
        block = gg * seq_n + ss if full else ss
        return outs[arr].at[pl.ds(pl.multiple_of(block * sizes[arr] + row, 16), rows)]

    def send(ch, src, gg, ss, sem, device):
        pltpu.make_async_remote_copy(
            src_ref=src,
            dst_ref=place(ch, gg, ss),
            send_sem=s_sem.at[ch],
            recv_sem=sem,
            device_id=device,
            device_id_type=MESH,
        ).start()

    def drain(ch, sem, count=1):
        arr, _, rows, _ = chunks[ch]
        block = outs[arr].at[pl.ds(0, count * rows)]
        pltpu.make_async_copy(block, block, sem).wait()

    def own(ch):
        arr, row, rows, full = chunks[ch]
        src = ins[arr].at[pl.ds(row, rows)]
        for far in far_z:
            send(ch, src, g, s, z_sem.at[ch, z], (g, far * 2 + core))
        if full:
            send(ch, src, g, s, x_sem.at[ch, z], x_next)
            for peer in y_next:
                send(ch, src, g, s, y_sem.at[ch, gy, z], peer)
        send(ch, src, g, s, p_sem.at[ch], partner)
        pltpu.make_async_copy(src, place(ch, g, s), l_sem.at[ch]).start()

    def line(ch):
        for far in far_z:
            drain(ch, z_sem.at[ch, far])
            from_s = far * 2 + core
            src = place(ch, g, from_s)
            if chunks[ch][3]:
                send(ch, src, g, from_s, x_sem.at[ch, far], x_next)
                for peer in y_next:
                    send(ch, src, g, from_s, y_sem.at[ch, gy, far], peer)
            send(ch, src, g, from_s, p_sem.at[ch], partner)

    def side(ch):
        if not chunks[ch][3]:
            return
        for far in range(z_n):
            from_s = far * 2 + core
            drain(ch, x_sem.at[ch, far])
            src = place(ch, other_x, from_s)
            if far % 2 == 0:
                for peer in y_next:
                    send(ch, src, other_x, from_s, d_sem.at[ch, gy, far], peer)
            send(ch, src, other_x, from_s, p_sem.at[ch], partner)
            for y in far_y:
                drain(ch, y_sem.at[ch, y, far])
                from_g = y * 2 + gx
                src = place(ch, from_g, from_s)
                if far % 2 == 1:
                    send(ch, src, from_g, from_s, d_sem.at[ch, y, far], x_next)
                send(ch, src, from_g, from_s, p_sem.at[ch], partner)

    def corner(ch):
        if not chunks[ch][3]:
            return
        for far in range(z_n):
            from_s = far * 2 + core
            for y in far_y:
                drain(ch, d_sem.at[ch, y, far])
                from_g = y * 2 + 1 - gx
                src = place(ch, from_g, from_s)
                send(ch, src, from_g, from_s, p_sem.at[ch], partner)

    def finish(ch):
        blocks, sends = z_n, 2 * z_n - 1
        if chunks[ch][3]:
            blocks = z_n * grp_n
            sends += z_n * y_n
            sends += z_n * (y_n - 1)
            sends += z_n * (2 * y_n - 1)
        drain(ch, p_sem.at[ch], blocks)
        drain(ch, s_sem.at[ch], sends)
        drain(ch, l_sem.at[ch])

    steps = (own, line, side, corner)

    def tick(t):
        for lag, step in enumerate(steps):
            if 0 <= t - lag < len(chunks):
                step(t - lag)

    def close():
        for ch in range(len(chunks)):
            finish(ch)

    return enter, tick, close, len(chunks) + len(steps) - 1


def gather_plan(groups, arrays, fulls, splits):
    grp_n, seq_n = groups
    chunks = []
    for i, array in enumerate(arrays):
        rows = array.shape[0] // splits[i]
        chunks += [(i, j * rows, rows, fulls[i]) for j in range(splits[i])]
    shapes = [
        jax.ShapeDtypeStruct(((grp_n if full else 1) * seq_n * a.shape[0], a.shape[1]), a.dtype)
        for a, full in zip(arrays, fulls)
    ]
    dma, count = pltpu.SemaphoreType.DMA, len(chunks)
    sems = [
        dma((count, seq_n // 2)),
        dma((count, seq_n // 2)),
        dma((count, grp_n // 2, seq_n // 2)),
        dma((count, grp_n // 2, seq_n // 2)),
        dma((count,)),
        dma((count,)),
        dma((count,)),
    ]
    return [a.shape[0] for a in arrays], chunks, shapes, sems


def gather_arrays(groups, arrays, fulls, splits, collective_id):
    sizes, chunks, shapes, sems = gather_plan(groups, arrays, fulls, splits)
    count = len(arrays)

    def kernel(*refs):
        enter, tick, close, ticks = gather_stages(
            groups, sizes, chunks, refs[:count], refs[count : 2 * count], refs[2 * count :]
        )
        enter()
        for t in range(ticks):
            tick(t)
        close()

    return pl.pallas_call(
        kernel,
        out_shape=shapes,
        in_specs=[pl.BlockSpec(memory_space=pltpu.VMEM)] * count,
        out_specs=[pl.BlockSpec(memory_space=pl.ANY)] * count,
        scratch_shapes=sems,
        compiler_params=pltpu.CompilerParams(collective_id=collective_id, has_side_effects=True),
    )(*arrays)


def dot_nt(left, right):
    return lax.dot_general(
        left, right, (((1,), (1,)), ((), ())), preferred_element_type=jnp.float32
    )


def dot_nn(left, right):
    return lax.dot_general(
        left, right, (((1,), (0,)), ((), ())), preferred_element_type=jnp.float32
    )


def stacked_heads(pair):
    first = lax.broadcasted_iota(jnp.int32, pair.shape, 1) < HEAD_DIM
    zero = jnp.zeros_like(pair)
    return jnp.concatenate([jnp.where(first, pair, zero), jnp.where(first, zero, pair)], 0)


def row_groups(prompt_rows, prompt_total, later_rows):
    block = min(256, later_rows)
    return [(prompt_rows + i, block, prompt_total + i) for i in range(0, later_rows, block)]


def attention_forward(sizes, q_ref, k_ref, v_ref, ctx_ref, lse_ref, wide_ref):
    prompt_rows, prompt_total, later_rows = sizes
    seq = lax.axis_index("seq")
    wide_ref[:, :128] = v_ref[...]
    wide_ref[:, 128:] = jnp.ones((prompt_total + later_rows, 128), jnp.bfloat16)

    def finish(start, rows, row_max, summed):
        total = summed[:, 128:]
        mixed = summed[:, :128] / total
        log_total = row_max * SCALE2 + jnp.log2(total)
        first = lax.broadcasted_iota(jnp.int32, (rows, 128), 1) < HEAD_DIM
        ctx_ref[start : start + rows] = jnp.where(first, mixed[:rows], mixed[rows:]).astype(
            jnp.bfloat16
        )
        lse_ref[start : start + rows] = jnp.where(first, log_total[:rows], log_total[rows:])

    for start, rows, free in row_groups(prompt_rows, prompt_total, later_rows):
        queries = stacked_heads(q_ref[start : start + rows])
        open_scores = dot_nt(queries, k_ref[:free])
        edge_scores = dot_nt(queries, k_ref[free : free + rows])
        row = lax.broadcasted_iota(jnp.int32, (rows, rows), 0)
        key = lax.broadcasted_iota(jnp.int32, (rows, rows), 1)
        seen = key <= row
        edge_scores = jnp.where(jnp.concatenate([seen, seen], 0), edge_scores, NEGATIVE)
        row_max = jnp.maximum(
            jnp.max(open_scores, 1, keepdims=True), jnp.max(edge_scores, 1, keepdims=True)
        )
        scaled = row_max * SCALE2
        open_p = jnp.exp2(open_scores * SCALE2 - scaled).astype(jnp.bfloat16)
        edge_p = jnp.exp2(edge_scores * SCALE2 - scaled).astype(jnp.bfloat16)
        summed = dot_nn(open_p, wide_ref[:free]) + dot_nn(edge_p, wide_ref[free : free + rows])
        finish(start, rows, row_max, summed)
    scores = dot_nt(stacked_heads(q_ref[:prompt_rows]), k_ref[:prompt_total])
    row = lax.broadcasted_iota(jnp.int32, (prompt_rows, prompt_total), 0)
    key = lax.broadcasted_iota(jnp.int32, (prompt_rows, prompt_total), 1)
    seen = key <= row + seq * prompt_rows
    scores = jnp.where(jnp.concatenate([seen, seen], 0), scores, NEGATIVE)
    row_max = jnp.max(scores, 1, keepdims=True)
    p = jnp.exp2(scores * SCALE2 - row_max * SCALE2).astype(jnp.bfloat16)
    finish(0, prompt_rows, row_max, dot_nn(p, wide_ref[:prompt_total]))


def attention_backward(
    sizes, q_ref, k_ref, v_ref, d_ref, ctx_ref, lse_ref, dq_ref, dk_ref, dv_ref, k_sum, v_sum
):
    prompt_rows, prompt_total, later_rows = sizes
    seq = lax.axis_index("seq")
    keys_t = k_ref[...].astype(jnp.float32).T.astype(jnp.bfloat16)
    lse_t = lse_ref[...].T
    weighed_t = (d_ref[...].astype(jnp.float32) * ctx_ref[...].astype(jnp.float32)).T
    deltas = [
        jnp.sum(weighed_t[:HEAD_DIM], 0, keepdims=True),
        jnp.sum(weighed_t[HEAD_DIM:], 0, keepdims=True),
    ]
    totals = [lse_t[0:1], lse_t[HEAD_DIM : HEAD_DIM + 1]]

    def group(start, rows, count, mask):
        queries = stacked_heads(q_ref[start : start + rows])
        grads = stacked_heads(d_ref[start : start + rows])
        total = jnp.concatenate([t[:, start : start + rows] for t in totals], 1)
        delta = jnp.concatenate([t[:, start : start + rows] for t in deltas], 1)
        p = mask(jnp.exp2(dot_nt(k_ref[:count], queries) * SCALE2 - total))
        d_scores = (p * (dot_nt(v_ref[:count], grads) - delta)).astype(jnp.bfloat16)
        dq_t = dot_nn(keys_t[:, :count], d_scores)
        first = lax.broadcasted_iota(jnp.int32, (128, rows), 0) < HEAD_DIM
        dq = jnp.where(first, dq_t[:, :rows], dq_t[:, rows:]).T * 0.125
        dq_ref[start : start + rows] = dq.astype(jnp.bfloat16)
        return dot_nn(d_scores, queries), dot_nn(p.astype(jnp.bfloat16), grads)

    def causal(free, rows):
        def mask(p):
            key = lax.broadcasted_iota(jnp.int32, (rows, rows), 0)
            row = lax.broadcasted_iota(jnp.int32, (rows, rows), 1)
            seen = key <= row
            edge = jnp.where(jnp.concatenate([seen, seen], 1), p[free:], 0.0)
            return jnp.concatenate([p[:free], edge], 0)

        return mask

    def prompt_mask(p):
        key = lax.broadcasted_iota(jnp.int32, (prompt_total, prompt_rows), 0)
        row = lax.broadcasted_iota(jnp.int32, (prompt_total, prompt_rows), 1)
        seen = key <= row + seq * prompt_rows
        return jnp.where(jnp.concatenate([seen, seen], 1), p, 0.0)

    groups = row_groups(prompt_rows, prompt_total, later_rows)
    start, rows, free = groups[-1]
    k_sum[...], v_sum[...] = group(start, rows, free + rows, causal(free, rows))
    for start, rows, free in groups[:-1]:
        d_keys, d_values = group(start, rows, free + rows, causal(free, rows))
        k_sum[: free + rows] += d_keys
        v_sum[: free + rows] += d_values
    d_keys, d_values = group(0, prompt_rows, prompt_total, prompt_mask)
    k_sum[:prompt_total] += d_keys
    v_sum[:prompt_total] += d_values
    dk_ref[...] = (k_sum[...] * 0.125).astype(jnp.bfloat16)
    dv_ref[...] = v_sum[...].astype(jnp.bfloat16)


def attend_and_gather(groups, q, kv, arrays, splits, collective_id):
    rows, keys, pairs = q.shape[0], kv.shape[0], q.shape[1] // 128
    sizes = (rows - CONT_LEN, keys - CONT_LEN, CONT_LEN)
    lengths, chunks, shapes, sems = gather_plan(groups, arrays, [True] * len(arrays), splits)
    count = len(arrays)

    def kernel(q_ref, k_ref, v_ref, *refs):
        ins, refs = refs[:count], refs[count:]
        ctx_ref, lse_ref, outs, wide_ref, sem_refs = (
            refs[0],
            refs[1],
            refs[2 : 2 + count],
            refs[2 + count],
            refs[3 + count :],
        )
        enter, tick, close, ticks = gather_stages(groups, lengths, chunks, ins, outs, sem_refs)
        step = pl.program_id(0)
        for i in range(pairs):

            @pl.when(step == i)
            def _():
                if i == 0:
                    enter()
                if i < ticks:
                    tick(i)

        attention_forward(sizes, q_ref, k_ref, v_ref, ctx_ref, lse_ref, wide_ref)

        @pl.when(step == pairs - 1)
        def _():
            for t in range(pairs, ticks):
                tick(t)
            close()

    def pair(i):
        return (0, i)

    return pl.pallas_call(
        kernel,
        grid=(pairs,),
        in_specs=[
            pl.BlockSpec((rows, 128), pair),
            pl.BlockSpec((keys, 128), pair),
            pl.BlockSpec((keys, 128), lambda i: (0, pairs + i)),
        ]
        + [pl.BlockSpec(memory_space=pltpu.VMEM)] * count,
        out_specs=[pl.BlockSpec((rows, 128), pair)] * 2
        + [pl.BlockSpec(memory_space=pl.ANY)] * count,
        out_shape=[
            jax.ShapeDtypeStruct(q.shape, jnp.bfloat16),
            jax.ShapeDtypeStruct(q.shape, jnp.float32),
        ]
        + shapes,
        scratch_shapes=[pltpu.VMEM((keys, 256), jnp.bfloat16)] + sems,
        compiler_params=pltpu.CompilerParams(
            collective_id=collective_id, has_side_effects=True, vmem_limit_bytes=VMEM_LIMIT
        ),
    )(q, kv, kv, *arrays)


def adapter_scratch(rows):
    dma = pltpu.SemaphoreType.DMA
    return [
        pltpu.VMEM((2, rows, 128), jnp.bfloat16),
        pltpu.VMEM((16, 128), jnp.bfloat16),
        pltpu.VMEM((3, 4, rows, 128), jnp.bfloat16),
        pltpu.VMEM((3, 4, rows, 128), jnp.bfloat16),
        pltpu.VMEM((4, rows, 128), jnp.float32),
        pltpu.VMEM((3, rows, 128), jnp.bfloat16),
        pltpu.VMEM((3, rows, 128), jnp.bfloat16),
        dma((3,)),
        dma((3,)),
        dma((3,)),
        dma((3,)),
        dma((3,)),
        dma((3,)),
    ]


def adapter_stages(term_ref, id_ref, out_ref, scratch):
    from_core, other_id, to_grp, from_grp, total, to_z, from_z = scratch[:7]
    a_send, a_recv, g_send, g_recv, z_send, z_recv = scratch[7:]
    g, s = lax.axis_index("grp"), lax.axis_index("seq")
    core, z = lax.rem(s, 2), s // 2
    other = 1 - core
    partner = (g, z * 2 + other)
    grps = [lax.rem(g + d, 4) for d in range(1, 4)]
    lines = [lax.rem(z + d, 4) for d in range(1, 4)]

    def enter():
        peers = [partner] + [(far, s) for far in grps] + [(g, far * 2 + core) for far in lines]
        barrier = pltpu.get_barrier_semaphore()
        for peer in peers:
            pl.semaphore_signal(barrier, inc=1, device_id=peer, device_id_type=MESH)
        pl.semaphore_wait(barrier, len(peers))

    def remote(src, dst, send_sem, recv_sem, device):
        return pltpu.make_async_remote_copy(
            src_ref=src,
            dst_ref=dst,
            send_sem=send_sem,
            recv_sem=recv_sem,
            device_id=device,
            device_id_type=MESH,
        )

    copies_a = [
        remote(term_ref.at[i * 2 + other], from_core.at[i], a_send.at[i], a_recv.at[i], partner)
        for i in range(2)
    ] + [remote(id_ref, other_id, a_send.at[2], a_recv.at[2], partner)]
    copies_g = [
        remote(to_grp.at[d], from_grp.at[d], g_send.at[d], g_recv.at[d], (grps[d], s))
        for d in range(3)
    ]
    copies_z = [
        remote(to_z.at[d], from_z.at[d], z_send.at[d], z_recv.at[d], (g, lines[d] * 2 + core))
        for d in range(3)
    ]

    def start(copies):
        for copy in copies:
            copy.start()

    def wait(copies):
        for copy in copies:
            copy.wait()

    def select():
        wait(copies_a)
        mine = id_ref[0:1].astype(jnp.float32)
        theirs = other_id[0:1].astype(jnp.float32)
        for d, grp in enumerate(grps + [g]):
            for slot in range(4):
                adapter = (grp * 2 + slot // 2).astype(jnp.float32)
                own_term = term_ref[(slot % 2) * 2 + core].astype(jnp.float32)
                other_term = from_core[slot % 2].astype(jnp.float32)
                picked = jnp.where(mine == adapter, own_term, 0.0) + jnp.where(
                    theirs == adapter, other_term, 0.0
                )
                if d < 3:
                    to_grp[d, slot] = picked.astype(jnp.bfloat16)
                else:
                    total[slot] = picked

    def add_grps():
        wait(copies_g)
        for slot in range(4):
            total[slot] += sum(from_grp[d, slot].astype(jnp.float32) for d in range(3))
        for d in range(3):
            to_z[d] = total[lines[d]].astype(jnp.bfloat16)

    def add_lines():
        wait(copies_z)
        out_ref[...] = total[z] + sum(from_z[d].astype(jnp.float32) for d in range(3))

    return (
        enter,
        lambda: start(copies_a),
        select,
        lambda: start(copies_g),
        add_grps,
        lambda: start(copies_z),
        add_lines,
    )


def attend_back_and_reduce(q, kv, d_ctx, ctx, lse, term, ident, collective_id):
    rows, keys, pairs = q.shape[0], kv.shape[0], q.shape[1] // 128
    sizes = (rows - CONT_LEN, keys - CONT_LEN, CONT_LEN)
    term_rows = term.shape[1]

    def kernel(q_ref, k_ref, v_ref, d_ref, ctx_ref, lse_ref, term_ref, id_ref, *refs):
        dq_ref, dk_ref, dv_ref, out_ref, k_sum, v_sum = refs[:6]
        enter, send_core, select, send_grp, add_grps, send_z, add_lines = adapter_stages(
            term_ref, id_ref, out_ref, refs[6:]
        )
        step = pl.program_id(0)

        @pl.when(step == 0)
        def _():
            enter()
            send_core()

        @pl.when(step == 1)
        def _():
            select()

        @pl.when(step == 2)
        def _():
            send_grp()

        @pl.when(step == pairs - 2)
        def _():
            add_grps()

        attention_backward(
            sizes,
            q_ref,
            k_ref,
            v_ref,
            d_ref,
            ctx_ref,
            lse_ref,
            dq_ref,
            dk_ref,
            dv_ref,
            k_sum,
            v_sum,
        )

        @pl.when(step == pairs - 2)
        def _():
            send_z()

        @pl.when(step == pairs - 1)
        def _():
            add_lines()

    def pair(i):
        return (0, i)

    row_spec = pl.BlockSpec((rows, 128), pair)
    key_spec = pl.BlockSpec((keys, 128), pair)
    whole = pl.BlockSpec(memory_space=pltpu.VMEM)
    return pl.pallas_call(
        kernel,
        grid=(pairs,),
        in_specs=[
            row_spec,
            key_spec,
            pl.BlockSpec((keys, 128), lambda i: (0, pairs + i)),
            row_spec,
            row_spec,
            row_spec,
            whole,
            whole,
        ],
        out_specs=[row_spec, key_spec, key_spec, whole],
        out_shape=[
            jax.ShapeDtypeStruct(q.shape, jnp.bfloat16),
            jax.ShapeDtypeStruct((keys, q.shape[1]), jnp.bfloat16),
            jax.ShapeDtypeStruct((keys, q.shape[1]), jnp.bfloat16),
            jax.ShapeDtypeStruct((term_rows, 128), jnp.float32),
        ],
        scratch_shapes=[pltpu.VMEM((keys, 128), jnp.float32)] * 2 + adapter_scratch(term_rows),
        compiler_params=pltpu.CompilerParams(
            collective_id=collective_id, has_side_effects=True, vmem_limit_bytes=VMEM_LIMIT
        ),
    )(q, kv, kv, d_ctx, ctx, lse, term, ident)


def last_exchange(rows_term, term, ident, collective_id):
    blocks, cols = rows_term.shape[0], rows_term.shape[3]
    rows = rows_term.shape[2]
    term_rows = term.shape[1]
    dma = pltpu.SemaphoreType.DMA

    def kernel(x_ref, term_ref, id_ref, sum_ref, out_ref, pair_in, to_line, from_line, *refs):
        p_send, p_recv, l_send, l_recv = refs[:4]
        enter, send_core, select, send_grp, add_grps, send_z, add_lines = adapter_stages(
            term_ref, id_ref, out_ref, refs[4:]
        )
        g, s = lax.axis_index("grp"), lax.axis_index("seq")
        core, z = lax.rem(s, 2), s // 2
        far_z = [lax.rem(z + d, blocks) for d in range(1, blocks)]
        across = pltpu.make_async_remote_copy(
            src_ref=x_ref.at[:, 1 - core],
            dst_ref=pair_in,
            send_sem=p_send,
            recv_sem=p_recv,
            device_id=(g, z * 2 + 1 - core),
            device_id_type=MESH,
        )
        along = [
            pltpu.make_async_remote_copy(
                src_ref=to_line.at[d],
                dst_ref=from_line.at[d],
                send_sem=l_send.at[d],
                recv_sem=l_recv.at[d],
                device_id=(g, far * 2 + core),
                device_id_type=MESH,
            )
            for d, far in enumerate(far_z)
        ]
        enter()
        send_core()
        across.start()
        select()
        send_grp()
        across.wait()
        for d, far in enumerate(far_z):
            both = x_ref[far, core].astype(jnp.float32) + pair_in[far].astype(jnp.float32)
            to_line[d] = both.astype(jnp.bfloat16)
            along[d].start()
        add_grps()
        send_z()
        total = x_ref[z, core].astype(jnp.float32) + pair_in[z].astype(jnp.float32)
        for d, copy in enumerate(along):
            copy.wait()
            total = total + from_line[d].astype(jnp.float32)
        sum_ref[...] = total
        add_lines()

    whole = pl.BlockSpec(memory_space=pltpu.VMEM)
    return pl.pallas_call(
        kernel,
        in_specs=[whole] * 3,
        out_specs=[whole] * 2,
        out_shape=[
            jax.ShapeDtypeStruct((rows, cols), jnp.float32),
            jax.ShapeDtypeStruct((term_rows, 128), jnp.float32),
        ],
        scratch_shapes=[
            pltpu.VMEM((blocks, rows, cols), jnp.bfloat16),
            pltpu.VMEM((blocks - 1, rows, cols), jnp.bfloat16),
            pltpu.VMEM((blocks - 1, rows, cols), jnp.bfloat16),
            dma,
            dma,
            dma((blocks - 1,)),
            dma((blocks - 1,)),
        ]
        + adapter_scratch(term_rows),
        compiler_params=pltpu.CompilerParams(
            collective_id=collective_id, has_side_effects=True, vmem_limit_bytes=VMEM_LIMIT
        ),
    )(rows_term, term, ident)


def local_general(
    tokens,
    cotangent,
    query_key_value_weight,
    attention_out_weight,
    feedforward_in_weight,
    feedforward_out_weight,
    layer_norm_gains,
    biases,
    adapter_down_matrices,
    adapter_up_matrices,
    adapter_of_continuation,
):
    row_count = tokens.shape[0]
    prompt_rows = row_count - CONT_LEN
    prompt_total = prompt_rows * lax.axis_size("seq")
    key_count = prompt_total + CONT_LEN
    seq_index = lax.axis_index("seq")
    adapter_index = adapter_of_continuation[0, 0]
    weight_shards = (
        query_key_value_weight,
        attention_out_weight,
        feedforward_in_weight,
        feedforward_out_weight,
        adapter_down_matrices,
        adapter_up_matrices,
    )
    gathered_rows = (
        lax.all_gather(weight_shards[0], ("grp", "seq"), axis=0, tiled=True),
        lax.all_gather(weight_shards[1], ("grp", "seq"), axis=0, tiled=True),
        lax.all_gather(weight_shards[2], ("grp", "seq"), axis=0, tiled=True),
        lax.all_gather(weight_shards[3], ("grp", "seq"), axis=0, tiled=True),
        lax.all_gather(weight_shards[4], ("grp", "seq"), axis=0, tiled=True),
        lax.all_gather(weight_shards[5], ("grp", "seq"), axis=0, tiled=True),
    )
    weight_matrices, adapter_sections = unpack_sections(gathered_rows, adapter_index)
    frozen_query_key_value, frozen_attention_out, frozen_feedforward_in, frozen_feedforward_out = (
        weight_matrices
    )
    (
        down_query_key_value,
        down_attention_out,
        down_feedforward_in,
        down_feedforward_out,
        up_query_key_value,
        up_attention_out,
        up_feedforward_in,
        up_feedforward_out,
    ) = adapter_sections
    shift_one = biases[:MODEL_WIDTH]
    shift_two = biases[MODEL_WIDTH : 2 * MODEL_WIDTH]
    query_key_value_bias = jnp.concatenate(
        [
            biases[2 * MODEL_WIDTH : 3 * MODEL_WIDTH],
            jnp.zeros((MODEL_WIDTH,), jnp.float32),
            biases[3 * MODEL_WIDTH : 4 * MODEL_WIDTH],
        ]
    )
    bias_out = biases[4 * MODEL_WIDTH : 5 * MODEL_WIDTH]
    bias_proj = biases[5 * MODEL_WIDTH : 6 * MODEL_WIDTH]
    bias_fc = biases[6 * MODEL_WIDTH :]
    inputs = tokens.astype(jnp.float32)
    normed_one = layer_norm(inputs, layer_norm_gains[0], shift_one).astype(jnp.bfloat16)
    inner_one = product(normed_one[prompt_rows:], down_query_key_value).astype(jnp.bfloat16)
    mixed_query_key_value = product(normed_one, frozen_query_key_value) + query_key_value_bias
    mixed_query_key_value = mixed_query_key_value.at[prompt_rows:].add(
        product(inner_one, up_query_key_value)
    )
    qkv_rows = mixed_query_key_value.astype(jnp.bfloat16)
    prompt_keys, prompt_values = (
        lax.all_gather(
            qkv_rows[:prompt_rows, MODEL_WIDTH : 2 * MODEL_WIDTH], "seq", axis=0, tiled=True
        ),
        lax.all_gather(qkv_rows[:prompt_rows, 2 * MODEL_WIDTH :], "seq", axis=0, tiled=True),
    )
    all_keys = jnp.concatenate(
        [prompt_keys, qkv_rows[prompt_rows:, MODEL_WIDTH : 2 * MODEL_WIDTH]], 0
    )
    all_values = jnp.concatenate([prompt_values, qkv_rows[prompt_rows:, 2 * MODEL_WIDTH :]], 0)
    allowed = visible(row_count, prompt_rows, prompt_total, key_count, seq_index)
    query_heads = split_heads(qkv_rows[:, :MODEL_WIDTH])
    key_heads = split_heads(all_keys)
    value_heads = split_heads(all_values)

    def forward_head(operands):
        query_head, key_head, value_head = operands
        scores = jnp.where(allowed, product_nt(query_head, key_head) * 0.125, NEGATIVE)
        row_max = jnp.max(scores, axis=1, keepdims=True)
        exp_scores = jnp.exp(scores - row_max)
        exp_total = jnp.sum(exp_scores, axis=1, keepdims=True)
        weights = (exp_scores / exp_total).astype(jnp.bfloat16)
        return (product(weights, value_head), (row_max + jnp.log(exp_total))[:, 0])

    head_contexts, log_total = lax.map(forward_head, (query_heads, key_heads, value_heads))
    attention_context = merge_heads(head_contexts).astype(jnp.bfloat16)
    inner_two = product(attention_context[prompt_rows:], down_attention_out).astype(jnp.bfloat16)
    attention_output = product(attention_context, frozen_attention_out) + bias_out
    attention_output = attention_output.at[prompt_rows:].add(product(inner_two, up_attention_out))
    hidden = inputs + attention_output
    normed_two = layer_norm(hidden, layer_norm_gains[1], shift_two).astype(jnp.bfloat16)
    inner_three = product(normed_two[prompt_rows:], down_feedforward_in).astype(jnp.bfloat16)
    before_activation = product(normed_two, frozen_feedforward_in) + bias_fc
    before_activation = before_activation.at[prompt_rows:].add(
        product(inner_three, up_feedforward_in)
    )
    activated_hidden = jax.nn.gelu(before_activation, approximate=True).astype(jnp.bfloat16)
    inner_four = product(activated_hidden[prompt_rows:], down_feedforward_out).astype(jnp.bfloat16)
    adapter_branch = product(activated_hidden, frozen_feedforward_out) + bias_proj
    adapter_branch = adapter_branch.at[prompt_rows:].add(product(inner_four, up_feedforward_out))
    outputs = (hidden + adapter_branch).astype(jnp.bfloat16)
    weight_matrices, adapter_sections = unpack_sections(
        (
            lax.all_gather(weight_shards[0], ("grp", "seq"), axis=0, tiled=True),
            lax.all_gather(weight_shards[1], ("grp", "seq"), axis=0, tiled=True),
            lax.all_gather(weight_shards[2], ("grp", "seq"), axis=0, tiled=True),
            lax.all_gather(weight_shards[3], ("grp", "seq"), axis=0, tiled=True),
            lax.all_gather(weight_shards[4], ("grp", "seq"), axis=0, tiled=True),
            lax.all_gather(weight_shards[5], ("grp", "seq"), axis=0, tiled=True),
        ),
        adapter_index,
    )
    frozen_query_key_value, frozen_attention_out, frozen_feedforward_in, frozen_feedforward_out = (
        weight_matrices
    )
    (
        down_query_key_value,
        down_attention_out,
        down_feedforward_in,
        down_feedforward_out,
        up_query_key_value,
        up_attention_out,
        up_feedforward_in,
        up_feedforward_out,
    ) = adapter_sections
    grad_inner_four = product_nt(cotangent[prompt_rows:], up_feedforward_out).astype(jnp.bfloat16)
    grad_act = product_nt(cotangent, frozen_feedforward_out)
    grad_act = grad_act.at[prompt_rows:].add(product_nt(grad_inner_four, down_feedforward_out))
    gelu_pull = jax.vjp(lambda field: jax.nn.gelu(field, approximate=True), before_activation)[1]
    grad_pre = gelu_pull(grad_act)[0].astype(jnp.bfloat16)
    grad_inner_three = product_nt(grad_pre[prompt_rows:], up_feedforward_in).astype(jnp.bfloat16)
    grad_normed_two = product_nt(grad_pre, frozen_feedforward_in)
    grad_normed_two = grad_normed_two.at[prompt_rows:].add(
        product_nt(grad_inner_three, down_feedforward_in)
    )
    second_pull = jax.vjp(lambda field: layer_norm(field, layer_norm_gains[1], shift_two), hidden)[
        1
    ]
    grad_hidden = cotangent.astype(jnp.float32) + second_pull(grad_normed_two)[0]
    grad_attn = grad_hidden.astype(jnp.bfloat16)
    grad_inner_two = product_nt(grad_attn[prompt_rows:], up_attention_out).astype(jnp.bfloat16)
    grad_context = product_nt(grad_attn, frozen_attention_out)
    grad_context = (
        grad_context.at[prompt_rows:]
        .add(product_nt(grad_inner_two, down_attention_out))
        .astype(jnp.bfloat16)
    )

    def backward_head(operands):
        query_head, key_head, value_head, grad_head, total_head = operands
        scores = jnp.where(allowed, product_nt(query_head, key_head) * 0.125, NEGATIVE)
        prob_full = jnp.exp(scores - total_head[:, None])
        weights = prob_full.astype(jnp.bfloat16)
        grad_weights = product_nt(grad_head, value_head)
        row_delta = jnp.sum(prob_full * grad_weights, axis=1, keepdims=True)
        grad_scores = (prob_full * (grad_weights - row_delta)).astype(jnp.bfloat16)
        return (
            product(grad_scores, key_head) * 0.125,
            product_tn(grad_scores, query_head) * 0.125,
            product_tn(weights, grad_head),
        )

    grad_q, grad_k, grad_v = lax.map(
        backward_head, (query_heads, key_heads, value_heads, split_heads(grad_context), log_total)
    )
    grad_query = merge_heads(grad_q)
    grad_keys = merge_heads(grad_k)
    grad_values = merge_heads(grad_v)
    own_keys, own_values = (
        lax.psum_scatter(
            grad_keys[:prompt_total].astype(jnp.bfloat16), "seq", scatter_dimension=0, tiled=True
        ).astype(jnp.float32),
        lax.psum_scatter(
            grad_values[:prompt_total].astype(jnp.bfloat16), "seq", scatter_dimension=0, tiled=True
        ).astype(jnp.float32),
    )
    grad_qkv = jnp.concatenate(
        [
            grad_query,
            jnp.concatenate([own_keys, grad_keys[prompt_total:]], 0),
            jnp.concatenate([own_values, grad_values[prompt_total:]], 0),
        ],
        1,
    ).astype(jnp.bfloat16)
    grad_inner_one = product_nt(grad_qkv[prompt_rows:], up_query_key_value).astype(jnp.bfloat16)
    grad_normed_one = product_nt(grad_qkv, frozen_query_key_value)
    grad_normed_one = grad_normed_one.at[prompt_rows:].add(
        product_nt(grad_inner_one, down_query_key_value)
    )
    first_pull = jax.vjp(lambda field: layer_norm(field, layer_norm_gains[0], shift_one), inputs)[1]
    input_grad = grad_hidden + first_pull(grad_normed_one)[0]
    down_term = jnp.concatenate(
        [
            product_tn(normed_one[prompt_rows:], grad_inner_one),
            product_tn(attention_context[prompt_rows:], grad_inner_two),
            product_tn(normed_two[prompt_rows:], grad_inner_three),
            product_tn(activated_hidden[prompt_rows:], grad_inner_four),
        ],
        0,
    )
    up_term = jnp.concatenate(
        [
            product_tn(inner_one, grad_qkv[prompt_rows:]),
            product_tn(inner_two, grad_attn[prompt_rows:]),
            product_tn(inner_three, grad_pre[prompt_rows:]),
            product_tn(inner_four, cotangent[prompt_rows:]),
        ],
        1,
    )
    select = (jnp.arange(ADAPTER_COUNT, dtype=jnp.int32) == adapter_index).astype(jnp.float32)
    down_grad, up_grad = (
        lax.psum_scatter(
            (select[:, None, None] * down_term[None]).reshape(-1),
            ("grp", "seq"),
            scatter_dimension=0,
            tiled=True,
        ),
        lax.psum_scatter(
            (select[:, None, None] * up_term[None]).reshape(-1),
            ("grp", "seq"),
            scatter_dimension=0,
            tiled=True,
        ),
    )
    return (outputs, input_grad, down_grad, up_grad)


def fast(
    tokens,
    cotangent,
    query_key_value_weight,
    attention_out_weight,
    feedforward_in_weight,
    feedforward_out_weight,
    layer_norm_gains,
    biases,
    adapter_down_matrices,
    adapter_up_matrices,
    adapter_of_continuation,
):
    groups = (lax.axis_size("grp"), lax.axis_size("seq"))
    prompt_rows = tokens.shape[0] - CONT_LEN
    prompt_total = prompt_rows * groups[1]
    down_rows = 3 * MODEL_WIDTH + HIDDEN_UNITS
    up_cols = 5 * MODEL_WIDTH + HIDDEN_UNITS
    adapter_index = adapter_of_continuation[0, 0]
    shift_one = biases[:MODEL_WIDTH]
    shift_two = biases[MODEL_WIDTH : 2 * MODEL_WIDTH]
    bias_q = biases[2 * MODEL_WIDTH : 3 * MODEL_WIDTH]
    bias_kv = jnp.concatenate(
        [jnp.zeros((MODEL_WIDTH,), jnp.float32), biases[3 * MODEL_WIDTH : 4 * MODEL_WIDTH]]
    )
    bias_out = biases[4 * MODEL_WIDTH : 5 * MODEL_WIDTH]
    bias_proj = biases[5 * MODEL_WIDTH : 6 * MODEL_WIDTH]
    bias_fc = biases[6 * MODEL_WIDTH :]

    prompt_tokens, w_qkv, downs, ups = gather_arrays(
        groups,
        [
            tokens[:prompt_rows],
            query_key_value_weight.reshape(-1, 3 * MODEL_WIDTH),
            adapter_down_matrices.reshape(-1, 128),
            adapter_up_matrices.reshape(-1, 128),
        ],
        [False, True, True, True],
        [1, 2, 1, 1],
        1,
    )
    down_all = lax.dynamic_index_in_dim(
        downs.reshape(ADAPTER_COUNT, -1, 128), adapter_index, 0, keepdims=False
    ).reshape(down_rows, ADAPTER_RANK)
    up_all = lax.dynamic_index_in_dim(
        ups.reshape(ADAPTER_COUNT, -1, 128), adapter_index, 0, keepdims=False
    ).reshape(ADAPTER_RANK, up_cols)
    down_qkv = down_all[:MODEL_WIDTH]
    down_out = down_all[MODEL_WIDTH : 2 * MODEL_WIDTH]
    down_fc = down_all[2 * MODEL_WIDTH : 3 * MODEL_WIDTH]
    down_proj = down_all[3 * MODEL_WIDTH :]
    up_qkv = up_all[:, : 3 * MODEL_WIDTH]
    up_out = up_all[:, 3 * MODEL_WIDTH : 4 * MODEL_WIDTH]
    up_fc = up_all[:, 4 * MODEL_WIDTH : 4 * MODEL_WIDTH + HIDDEN_UNITS]
    up_proj = up_all[:, 4 * MODEL_WIDTH + HIDDEN_UNITS :]

    inputs = tokens.astype(jnp.float32)
    normed_own = layer_norm(inputs, layer_norm_gains[0], shift_one).astype(jnp.bfloat16)
    normed_prompt = layer_norm(
        prompt_tokens.astype(jnp.float32), layer_norm_gains[0], shift_one
    ).astype(jnp.bfloat16)
    normed_later = normed_own[prompt_rows:]
    normed_keys = jnp.concatenate([normed_prompt, normed_later], 0)
    inner_one = product(normed_later, down_qkv).astype(jnp.bfloat16)
    queries = product(normed_own, w_qkv[:, :MODEL_WIDTH]) + bias_q
    queries = queries.at[prompt_rows:].add(product(inner_one, up_qkv[:, :MODEL_WIDTH]))
    queries = queries.astype(jnp.bfloat16)
    keys_values = product(normed_keys, w_qkv[:, MODEL_WIDTH:]) + bias_kv
    keys_values = keys_values.at[prompt_total:].add(product(inner_one, up_qkv[:, MODEL_WIDTH:]))
    keys_values = keys_values.astype(jnp.bfloat16)

    context, log_total, w_out, w_fc, w_proj = attend_and_gather(
        groups,
        queries,
        keys_values,
        [
            attention_out_weight.reshape(-1, MODEL_WIDTH),
            feedforward_in_weight.reshape(-1, HIDDEN_UNITS),
            feedforward_out_weight.reshape(-1, MODEL_WIDTH),
        ],
        [1, 2, 2],
        2,
    )

    inner_two = product(context[prompt_rows:], down_out).astype(jnp.bfloat16)
    attention_output = product(context, w_out) + bias_out
    attention_output = attention_output.at[prompt_rows:].add(product(inner_two, up_out))
    hidden = inputs + attention_output
    normed_two = layer_norm(hidden, layer_norm_gains[1], shift_two).astype(jnp.bfloat16)
    inner_three = product(normed_two[prompt_rows:], down_fc).astype(jnp.bfloat16)
    before_activation = product(normed_two, w_fc) + bias_fc
    before_activation = before_activation.at[prompt_rows:].add(product(inner_three, up_fc))
    activated = jax.nn.gelu(before_activation, approximate=True).astype(jnp.bfloat16)
    inner_four = product(activated[prompt_rows:], down_proj).astype(jnp.bfloat16)
    branch = product(activated, w_proj) + bias_proj
    branch = branch.at[prompt_rows:].add(product(inner_four, up_proj))
    outputs = (hidden + branch).astype(jnp.bfloat16)

    later_cotangent = cotangent[prompt_rows:]
    grad_inner_four = product_nt(later_cotangent, up_proj).astype(jnp.bfloat16)
    grad_act = product_nt(cotangent, w_proj)
    grad_act = grad_act.at[prompt_rows:].add(product_nt(grad_inner_four, down_proj))
    gelu_pull = jax.vjp(lambda field: jax.nn.gelu(field, approximate=True), before_activation)[1]
    grad_pre = gelu_pull(grad_act)[0].astype(jnp.bfloat16)
    grad_inner_three = product_nt(grad_pre[prompt_rows:], up_fc).astype(jnp.bfloat16)
    grad_normed_two = product_nt(grad_pre, w_fc)
    grad_normed_two = grad_normed_two.at[prompt_rows:].add(product_nt(grad_inner_three, down_fc))
    second_pull = jax.vjp(lambda field: layer_norm(field, layer_norm_gains[1], shift_two), hidden)[
        1
    ]
    grad_hidden = cotangent.astype(jnp.float32) + second_pull(grad_normed_two)[0]
    grad_attn = grad_hidden.astype(jnp.bfloat16)
    grad_inner_two = product_nt(grad_attn[prompt_rows:], up_out).astype(jnp.bfloat16)
    grad_context = product_nt(grad_attn, w_out)
    grad_context = (
        grad_context.at[prompt_rows:]
        .add(product_nt(grad_inner_two, down_out))
        .astype(jnp.bfloat16)
    )

    down_early = jnp.concatenate(
        [
            jnp.zeros((MODEL_WIDTH, ADAPTER_RANK), jnp.float32),
            product_tn(context[prompt_rows:], grad_inner_two),
            product_tn(normed_two[prompt_rows:], grad_inner_three),
            product_tn(activated[prompt_rows:], grad_inner_four),
        ],
        0,
    ).astype(jnp.bfloat16)
    up_early = jnp.concatenate(
        [
            product_tn(inner_two, grad_attn[prompt_rows:]),
            product_tn(inner_three, grad_pre[prompt_rows:]),
            product_tn(inner_four, later_cotangent),
        ],
        1,
    ).astype(jnp.bfloat16)
    early_term = jnp.concatenate(
        [down_early.reshape(4, -1, 128), up_early.reshape(4, -1, 128)], 1
    )
    ident = jnp.full((16, 128), adapter_index, jnp.int32).astype(jnp.bfloat16)

    grad_q, grad_k, grad_v, early = attend_back_and_reduce(
        queries, keys_values, grad_context, context, log_total, early_term, ident, 3
    )

    w_q, w_k, w_v = (
        w_qkv[:, :MODEL_WIDTH],
        w_qkv[:, MODEL_WIDTH : 2 * MODEL_WIDTH],
        w_qkv[:, 2 * MODEL_WIDTH :],
    )
    rows_term = (
        product_nt(grad_k[:prompt_total], w_k) + product_nt(grad_v[:prompt_total], w_v)
    ).astype(jnp.bfloat16)
    grad_later = jnp.concatenate(
        [grad_q[prompt_rows:], grad_k[prompt_total:], grad_v[prompt_total:]], 1
    )
    grad_inner_one = product_nt(grad_later, up_qkv).astype(jnp.bfloat16)
    down_late = product_tn(normed_later, grad_inner_one).astype(jnp.bfloat16)
    up_late = product_tn(inner_one, grad_later).astype(jnp.bfloat16)
    down_late = jnp.concatenate(
        [
            down_late.reshape(1, -1, 128),
            jnp.zeros((3, MODEL_WIDTH * ADAPTER_RANK // 128, 128), jnp.bfloat16),
        ],
        0,
    )
    late_term = jnp.concatenate([down_late, up_late.reshape(4, -1, 128)], 1)
    prompt_sum, late = last_exchange(
        rows_term.reshape(groups[1] // 2, 2, prompt_rows, MODEL_WIDTH), late_term, ident, 4
    )
    later_normed_grad = product_nt(grad_later, w_qkv) + product_nt(grad_inner_one, down_qkv)
    prompt_normed_grad = product_nt(grad_q[:prompt_rows], w_q) + prompt_sum
    grad_normed_one = jnp.concatenate([prompt_normed_grad, later_normed_grad], 0)
    first_pull = jax.vjp(lambda field: layer_norm(field, layer_norm_gains[0], shift_one), inputs)[1]
    input_grad = grad_hidden + first_pull(grad_normed_one)[0]

    split = down_rows * ADAPTER_RANK // 4 // 128
    late_split = MODEL_WIDTH * ADAPTER_RANK // 128
    down_grad = early[:split].at[:late_split].add(late[:late_split]).reshape(-1)
    up_grad = jnp.concatenate(
        [
            late[late_split:].reshape(ADAPTER_RANK // 4, -1),
            early[split:].reshape(ADAPTER_RANK // 4, -1),
        ],
        1,
    ).reshape(-1)
    return (outputs, input_grad, down_grad, up_grad)


def solution(mesh):
    placed = (
        P(("grp", "seq"), None),
        P(("grp", "seq"), None),
        P(("grp", "seq")),
        P(("grp", "seq")),
        P(("grp", "seq")),
        P(("grp", "seq")),
        P(),
        P(),
        P(("grp", "seq")),
        P(("grp", "seq")),
        P(("grp", "seq"), None),
    )
    fits = mesh.shape["grp"] == 4 and mesh.shape["seq"] == 8
    return jax.shard_map(
        fast if fits else local_general,
        mesh=mesh,
        in_specs=placed,
        out_specs=(
            P(("grp", "seq"), None),
            P(("grp", "seq"), None),
            P(("grp", "seq")),
            P(("grp", "seq")),
        ),
        check_vma=False,
    )
```

```python
import functools

import jax
import jax.numpy as jnp
from jax import lax
from jax.experimental import pallas as pl
from jax.experimental.pallas import tpu as pltpu
from jax.sharding import PartitionSpec as P

MODEL_WIDTH = 1024
HEADS = 16
HEAD_DIM = 64
HIDDEN_UNITS = 4096
ADAPTER_RANK = 16
ADAPTER_COUNT = 8
CONT_LEN = 512


EPSILON = 1e-05
NEGATIVE = -1e30


def product(left_side, right_side):
    return jnp.dot(left_side, right_side, preferred_element_type=jnp.float32)


def product_tn(left_side, right_side):
    return lax.dot_general(
        left_side, right_side, (((0,), (0,)), ((), ())), preferred_element_type=jnp.float32
    )


def product_nt(left_side, right_side):
    return lax.dot_general(
        left_side, right_side, (((1,), (1,)), ((), ())), preferred_element_type=jnp.float32
    )


def layer_norm(values, gain_vec, shift_vec):
    row_mean = jnp.mean(values, axis=-1, keepdims=True)
    centred = values - row_mean
    row_var = jnp.mean(centred * centred, axis=-1, keepdims=True)
    return centred * lax.rsqrt(row_var + EPSILON) * gain_vec + shift_vec


def unpack_sections(pieces, adapter_index):
    qkv_flat, out_flat, fc_flat, proj_flat, down_flat, up_flat = pieces
    every_down_matrix = down_flat.reshape(
        ADAPTER_COUNT, 3 * MODEL_WIDTH + HIDDEN_UNITS, ADAPTER_RANK
    )
    every_up_matrix = up_flat.reshape(ADAPTER_COUNT, ADAPTER_RANK, 5 * MODEL_WIDTH + HIDDEN_UNITS)
    down_rows = lax.dynamic_index_in_dim(every_down_matrix, adapter_index, 0, keepdims=False)
    up_cols = lax.dynamic_index_in_dim(every_up_matrix, adapter_index, 0, keepdims=False)
    weight_matrices = (
        qkv_flat.reshape(MODEL_WIDTH, 3 * MODEL_WIDTH),
        out_flat.reshape(MODEL_WIDTH, MODEL_WIDTH),
        fc_flat.reshape(MODEL_WIDTH, HIDDEN_UNITS),
        proj_flat.reshape(HIDDEN_UNITS, MODEL_WIDTH),
    )
    adapter_sections = (
        down_rows[:MODEL_WIDTH],
        down_rows[MODEL_WIDTH : 2 * MODEL_WIDTH],
        down_rows[2 * MODEL_WIDTH : 3 * MODEL_WIDTH],
        down_rows[3 * MODEL_WIDTH :],
        up_cols[:, : 3 * MODEL_WIDTH],
        up_cols[:, 3 * MODEL_WIDTH : 4 * MODEL_WIDTH],
        up_cols[:, 4 * MODEL_WIDTH : 4 * MODEL_WIDTH + HIDDEN_UNITS],
        up_cols[:, 4 * MODEL_WIDTH + HIDDEN_UNITS :],
    )
    return (weight_matrices, adapter_sections)


def visible(row_count, prompt_rows, prompt_total, key_count, seq_index):
    row_ids = jnp.arange(row_count, dtype=jnp.int32)[:, None]
    col_ids = jnp.arange(key_count, dtype=jnp.int32)[None, :]
    in_prompt = col_ids < prompt_total
    prompt_seen = in_prompt & (col_ids <= seq_index * prompt_rows + row_ids)
    later_seen = in_prompt | (col_ids - prompt_total <= row_ids - prompt_rows)
    return jnp.where(row_ids < prompt_rows, prompt_seen, later_seen)


def split_heads(values):
    return values.reshape(values.shape[0], HEADS, HEAD_DIM).transpose(1, 0, 2)


def merge_heads(values):
    return values.transpose(1, 0, 2).reshape(values.shape[1], HEADS * HEAD_DIM)


MESH = pl.DeviceIdType.MESH
SCALE2 = 0.125 * 1.4426950408889634
VMEM_LIMIT = 60 << 20


def gather_stages(groups, sizes, chunks, ins, outs, sems):
    grp_n, seq_n = groups
    z_n, y_n = seq_n // 2, grp_n // 2
    z_sem, x_sem, y_sem, d_sem, p_sem, s_sem, l_sem = sems
    g, s = lax.axis_index("grp"), lax.axis_index("seq")
    core, z = lax.rem(s, 2), s // 2
    gx, gy = lax.rem(g, 2), g // 2
    partner = (g, z * 2 + 1 - core)
    other_x = gy * 2 + 1 - gx
    x_next = (other_x, s)
    far_z = [lax.rem(z + d, z_n) for d in range(1, z_n)]
    far_y = [lax.rem(gy + d, y_n) for d in range(1, y_n)]
    y_next = [(y * 2 + gx, s) for y in far_y]

    def enter():
        peers = [partner, x_next] + y_next + [(g, far * 2 + core) for far in far_z]
        barrier = pltpu.get_barrier_semaphore()
        for peer in peers:
            pl.semaphore_signal(barrier, inc=1, device_id=peer, device_id_type=MESH)
        pl.semaphore_wait(barrier, len(peers))

    def place(ch, gg, ss):
        arr, row, rows, full = chunks[ch]
        block = gg * seq_n + ss if full else ss
        return outs[arr].at[pl.ds(pl.multiple_of(block * sizes[arr] + row, 16), rows)]

    def send(ch, src, gg, ss, sem, device):
        pltpu.make_async_remote_copy(
            src_ref=src,
            dst_ref=place(ch, gg, ss),
            send_sem=s_sem.at[ch],
            recv_sem=sem,
            device_id=device,
            device_id_type=MESH,
        ).start()

    def drain(ch, sem, count=1):
        arr, _, rows, _ = chunks[ch]
        block = outs[arr].at[pl.ds(0, count * rows)]
        pltpu.make_async_copy(block, block, sem).wait()

    def own(ch):
        arr, row, rows, full = chunks[ch]
        src = ins[arr].at[pl.ds(row, rows)]
        for far in far_z:
            send(ch, src, g, s, z_sem.at[ch, z], (g, far * 2 + core))
        if full:
            send(ch, src, g, s, x_sem.at[ch, z], x_next)
            for peer in y_next:
                send(ch, src, g, s, y_sem.at[ch, gy, z], peer)
        send(ch, src, g, s, p_sem.at[ch], partner)
        pltpu.make_async_copy(src, place(ch, g, s), l_sem.at[ch]).start()

    def line(ch):
        for far in far_z:
            drain(ch, z_sem.at[ch, far])
            from_s = far * 2 + core
            src = place(ch, g, from_s)
            if chunks[ch][3]:
                send(ch, src, g, from_s, x_sem.at[ch, far], x_next)
                for peer in y_next:
                    send(ch, src, g, from_s, y_sem.at[ch, gy, far], peer)
            send(ch, src, g, from_s, p_sem.at[ch], partner)

    def side(ch):
        if not chunks[ch][3]:
            return
        for far in range(z_n):
            from_s = far * 2 + core
            drain(ch, x_sem.at[ch, far])
            src = place(ch, other_x, from_s)
            if far % 2 == 0:
                for peer in y_next:
                    send(ch, src, other_x, from_s, d_sem.at[ch, gy, far], peer)
            send(ch, src, other_x, from_s, p_sem.at[ch], partner)
            for y in far_y:
                drain(ch, y_sem.at[ch, y, far])
                from_g = y * 2 + gx
                src = place(ch, from_g, from_s)
                if far % 2 == 1:
                    send(ch, src, from_g, from_s, d_sem.at[ch, y, far], x_next)
                send(ch, src, from_g, from_s, p_sem.at[ch], partner)

    def corner(ch):
        if not chunks[ch][3]:
            return
        for far in range(z_n):
            from_s = far * 2 + core
            for y in far_y:
                drain(ch, d_sem.at[ch, y, far])
                from_g = y * 2 + 1 - gx
                src = place(ch, from_g, from_s)
                send(ch, src, from_g, from_s, p_sem.at[ch], partner)

    def ready(ch):
        drain(ch, p_sem.at[ch], z_n * grp_n if chunks[ch][3] else z_n)
        drain(ch, l_sem.at[ch])

    def finish(ch):
        sends = 2 * z_n - 1
        if chunks[ch][3]:
            sends += z_n * y_n
            sends += z_n * (y_n - 1)
            sends += z_n * (2 * y_n - 1)
        drain(ch, s_sem.at[ch], sends)

    steps = (own, line, side, corner)

    def tick(t):
        for lag, step in enumerate(steps):
            if 0 <= t - lag < len(chunks):
                step(t - lag)

    return enter, tick, ready, finish


def gather_plan(groups, shards, splits):
    grp_n, seq_n = groups
    chunks, shapes = [], []
    for i, (rows, cols, full) in enumerate(shards):
        part = rows // splits[i]
        chunks += [(i, j * part, part, full) for j in range(splits[i])]
        total = (grp_n if full else 1) * seq_n * rows
        shapes.append(jax.ShapeDtypeStruct((total, cols), jnp.bfloat16))
    dma, count = pltpu.SemaphoreType.DMA, len(chunks)
    sems = [
        dma((count, seq_n // 2)),
        dma((count, seq_n // 2)),
        dma((count, grp_n // 2, seq_n // 2)),
        dma((count, grp_n // 2, seq_n // 2)),
        dma((count,)),
        dma((count,)),
        dma((count,)),
    ]
    return [rows for rows, _, _ in shards], chunks, shapes, sems


def dot_nt(left, right):
    return lax.dot_general(
        left, right, (((1,), (1,)), ((), ())), preferred_element_type=jnp.float32
    )


def dot_nn(left, right):
    return lax.dot_general(
        left, right, (((1,), (0,)), ((), ())), preferred_element_type=jnp.float32
    )


def stacked_heads(pair):
    first = lax.broadcasted_iota(jnp.int32, pair.shape, 1) < HEAD_DIM
    zero = jnp.zeros_like(pair)
    return jnp.concatenate([jnp.where(first, pair, zero), jnp.where(first, zero, pair)], 0)


def row_groups(prompt_rows, prompt_total, later_rows):
    block = min(256, later_rows)
    return [(prompt_rows + i, block, prompt_total + i) for i in range(0, later_rows, block)]


def attention_forward(sizes, q_ref, k_ref, v_ref, ctx_ref, lse_ref, wide_ref):
    prompt_rows, prompt_total, later_rows = sizes
    seq = lax.axis_index("seq")
    wide_ref[:, :128] = v_ref[...]
    wide_ref[:, 128:] = jnp.ones((prompt_total + later_rows, 128), jnp.bfloat16)

    def finish(start, rows, row_max, summed):
        total = summed[:, 128:]
        mixed = summed[:, :128] / total
        log_total = row_max * SCALE2 + jnp.log2(total)
        first = lax.broadcasted_iota(jnp.int32, (rows, 128), 1) < HEAD_DIM
        ctx_ref[start : start + rows] = jnp.where(first, mixed[:rows], mixed[rows:]).astype(
            jnp.bfloat16
        )
        lse_ref[start : start + rows] = jnp.where(first, log_total[:rows], log_total[rows:])

    for start, rows, free in row_groups(prompt_rows, prompt_total, later_rows):
        queries = stacked_heads(q_ref[start : start + rows])
        open_scores = dot_nt(queries, k_ref[:free])
        edge_scores = dot_nt(queries, k_ref[free : free + rows])
        row = lax.broadcasted_iota(jnp.int32, (rows, rows), 0)
        key = lax.broadcasted_iota(jnp.int32, (rows, rows), 1)
        seen = key <= row
        edge_scores = jnp.where(jnp.concatenate([seen, seen], 0), edge_scores, NEGATIVE)
        row_max = jnp.maximum(
            jnp.max(open_scores, 1, keepdims=True), jnp.max(edge_scores, 1, keepdims=True)
        )
        scaled = row_max * SCALE2
        open_p = jnp.exp2(open_scores * SCALE2 - scaled).astype(jnp.bfloat16)
        edge_p = jnp.exp2(edge_scores * SCALE2 - scaled).astype(jnp.bfloat16)
        summed = dot_nn(open_p, wide_ref[:free]) + dot_nn(edge_p, wide_ref[free : free + rows])
        finish(start, rows, row_max, summed)
    scores = dot_nt(stacked_heads(q_ref[:prompt_rows]), k_ref[:prompt_total])
    row = lax.broadcasted_iota(jnp.int32, (prompt_rows, prompt_total), 0)
    key = lax.broadcasted_iota(jnp.int32, (prompt_rows, prompt_total), 1)
    seen = key <= row + seq * prompt_rows
    scores = jnp.where(jnp.concatenate([seen, seen], 0), scores, NEGATIVE)
    row_max = jnp.max(scores, 1, keepdims=True)
    p = jnp.exp2(scores * SCALE2 - row_max * SCALE2).astype(jnp.bfloat16)
    finish(0, prompt_rows, row_max, dot_nn(p, wide_ref[:prompt_total]))


def attention_backward(
    sizes, q_ref, k_ref, v_ref, d_ref, ctx_ref, lse_ref, dq_ref, dk_ref, dv_ref, k_sum, v_sum
):
    prompt_rows, prompt_total, later_rows = sizes
    seq = lax.axis_index("seq")
    keys_t = k_ref[...].astype(jnp.float32).T.astype(jnp.bfloat16)
    lse_t = lse_ref[...].T
    weighed_t = (d_ref[...].astype(jnp.float32) * ctx_ref[...].astype(jnp.float32)).T
    deltas = [
        jnp.sum(weighed_t[:HEAD_DIM], 0, keepdims=True),
        jnp.sum(weighed_t[HEAD_DIM:], 0, keepdims=True),
    ]
    totals = [lse_t[0:1], lse_t[HEAD_DIM : HEAD_DIM + 1]]

    def group(start, rows, count, mask):
        queries = stacked_heads(q_ref[start : start + rows])
        grads = stacked_heads(d_ref[start : start + rows])
        total = jnp.concatenate([t[:, start : start + rows] for t in totals], 1)
        delta = jnp.concatenate([t[:, start : start + rows] for t in deltas], 1)
        p = mask(jnp.exp2(dot_nt(k_ref[:count], queries) * SCALE2 - total))
        d_scores = (p * (dot_nt(v_ref[:count], grads) - delta)).astype(jnp.bfloat16)
        dq_t = dot_nn(keys_t[:, :count], d_scores)
        first = lax.broadcasted_iota(jnp.int32, (128, rows), 0) < HEAD_DIM
        dq = jnp.where(first, dq_t[:, :rows], dq_t[:, rows:]).T * 0.125
        dq_ref[start : start + rows] = dq.astype(jnp.bfloat16)
        return dot_nn(d_scores, queries), dot_nn(p.astype(jnp.bfloat16), grads)

    def causal(free, rows):
        def mask(p):
            key = lax.broadcasted_iota(jnp.int32, (rows, rows), 0)
            row = lax.broadcasted_iota(jnp.int32, (rows, rows), 1)
            seen = key <= row
            edge = jnp.where(jnp.concatenate([seen, seen], 1), p[free:], 0.0)
            return jnp.concatenate([p[:free], edge], 0)

        return mask

    def prompt_mask(p):
        key = lax.broadcasted_iota(jnp.int32, (prompt_total, prompt_rows), 0)
        row = lax.broadcasted_iota(jnp.int32, (prompt_total, prompt_rows), 1)
        seen = key <= row + seq * prompt_rows
        return jnp.where(jnp.concatenate([seen, seen], 1), p, 0.0)

    groups = row_groups(prompt_rows, prompt_total, later_rows)
    start, rows, free = groups[-1]
    k_sum[...], v_sum[...] = group(start, rows, free + rows, causal(free, rows))
    for start, rows, free in groups[:-1]:
        d_keys, d_values = group(start, rows, free + rows, causal(free, rows))
        k_sum[: free + rows] += d_keys
        v_sum[: free + rows] += d_values
    d_keys, d_values = group(0, prompt_rows, prompt_total, prompt_mask)
    k_sum[:prompt_total] += d_keys
    v_sum[:prompt_total] += d_values
    dk_ref[...] = (k_sum[...] * 0.125).astype(jnp.bfloat16)
    dv_ref[...] = v_sum[...].astype(jnp.bfloat16)


UP_SECTIONS = (3 * MODEL_WIDTH, MODEL_WIDTH, HIDDEN_UNITS, MODEL_WIDTH)
UP_STARTS = (0, 768, 1024, 2048)
QUARTER = (3 * MODEL_WIDTH + HIDDEN_UNITS) // 4
UP_QUARTER = sum(UP_SECTIONS) // 4
TILE = 256


def normalize_rows(read, write, count, gain, shift):
    def body(i, carry):
        start = pl.multiple_of(i * 128, 128)
        values = read(start)
        centred = values - jnp.mean(values, axis=1, keepdims=True)
        var = jnp.mean(centred * centred, axis=1, keepdims=True)
        write(start, (centred * lax.rsqrt(var + EPSILON) * gain + shift).astype(jnp.bfloat16))
        return carry

    lax.fori_loop(0, count // 128, body, 0)


def spread_rank(inner):
    rank = lax.broadcasted_iota(jnp.int32, (ADAPTER_RANK, 64), 0)
    col = lax.broadcasted_iota(jnp.int32, (ADAPTER_RANK, 64), 1)
    parts = []
    for j in range(4):
        chosen = (col == (rank // 4) * 16 + (rank % 4) * 4 + j).astype(jnp.bfloat16)
        parts.append(dot_nn(inner, chosen).astype(jnp.bfloat16))
    return parts


def forward_and_gather(groups, ident, tokens, gains, biases, shards, collective_id):
    rows = tokens.shape[0]
    prompt_rows = rows - CONT_LEN
    prompt_total = prompt_rows * groups[1]
    keys = prompt_total + CONT_LEN
    sizes = (prompt_rows, prompt_total, CONT_LEN)
    width, hidden_units = MODEL_WIDTH, HIDDEN_UNITS
    pairs = width // 128
    plan = [(prompt_rows, width, False)] + [(a.shape[0], a.shape[1], True) for a in shards]
    splits = [1, 1, 1, 2, 1, 2, 2]
    lengths, chunks, gathered, sems = gather_plan(groups, plan, splits)
    count = len(plan)
    dma = pltpu.SemaphoreType.DMA

    def kernel(id_ref, tokens_ref, gains_ref, bias_ref, *refs):
        ins = (tokens_ref,) + refs[: count - 1]
        refs = refs[count - 1 :]
        q_out, kv_out, ctx_out, lse_out, h_out, n_out, f_out, gl_out, u_out = refs[:9]
        outs, refs = refs[9 : 9 + count], refs[9 + count :]
        (
            prompt_v,
            norm_v,
            weight_v,
            w_out_v,
            q_v,
            kv_v,
            wide_v,
            ctx_v,
            lse_v,
            h_v,
            n_v,
            gl_v,
            f_v,
            downs_v,
            ups_v,
            down_v,
            up_v,
            spread_v,
            in_sem,
            out_sem,
            f_sem,
        ) = refs[:21]
        enter, tick, ready, finish = gather_stages(groups, lengths, chunks, ins, outs, refs[21:])
        adapter = id_ref[0, 0]
        seq = lax.axis_index("seq")

        def load(arr, dst, sem):
            copy = pltpu.make_async_copy(outs[arr], dst, in_sem.at[sem])
            copy.start()
            return copy

        stores = []

        def store(src, dst):
            copy = pltpu.make_async_copy(src, dst, out_sem.at[len(stores)])
            copy.start()
            stores.append(copy)

        def bias(start, size):
            return bias_ref[:, pl.ds(pl.multiple_of(start, 128), size)]

        def read_tokens(start):
            at = pl.multiple_of(start + prompt_rows, 128)
            return tokens_ref[pl.ds(at, 128)].astype(jnp.float32)

        def write_later(start, values):
            norm_v[pl.ds(pl.multiple_of(start + prompt_total, 128), 128)] = values

        def read_prompt(start):
            return prompt_v[pl.ds(start, 128)].astype(jnp.float32)

        def write_prompt(start, values):
            norm_v[pl.ds(start, 128)] = values

        def read_hidden(start):
            return h_v[pl.ds(start, 128)]

        def write_hidden(start, values):
            n_v[pl.ds(start, 128)] = values

        def inner(which, values, first, size):
            low = dot_nt(values, down_v[:, first : first + size]).astype(jnp.bfloat16)
            u_out[which] = low
            for j, part in enumerate(spread_rank(low)):
                spread_v[j] = part

        enter()
        tick(0)
        shift_one = bias_ref[:, :width]
        normalize_rows(read_tokens, write_later, CONT_LEN, gains_ref[0:1], shift_one)
        tick(1)
        ready(0)
        load(0, prompt_v, 0).wait()
        normalize_rows(read_prompt, write_prompt, prompt_total, gains_ref[0:1], shift_one)
        tick(2)
        tick(3)
        tick(4)
        ready(1)
        copy_down = load(1, downs_v, 1)
        tick(5)
        ready(2)
        copy_up = load(2, ups_v, 2)
        copy_down.wait()
        copy_up.wait()
        row = lax.broadcasted_iota(jnp.int32, (64, downs_v.shape[0]), 0)
        col = lax.broadcasted_iota(jnp.int32, (64, downs_v.shape[0]), 1)
        chosen = (col == row + adapter * 64).astype(jnp.bfloat16)
        for part in range(4):
            rows_of = chosen[part * 16 : (part + 1) * 16]
            down_v[:, part * QUARTER : (part + 1) * QUARTER] = dot_nn(rows_of, downs_v[...]).astype(
                jnp.bfloat16
            )
        up_v[...] = dot_nn(chosen, ups_v[...]).astype(jnp.bfloat16)
        inner(0, norm_v[prompt_total:], 0, width)
        tick(6)
        tick(7)
        ready(3)
        ready(4)
        load_qkv = pltpu.make_async_copy(outs[3], weight_v.at[:, : 3 * width], in_sem.at[3])
        load_qkv.start()
        load_qkv.wait()

        def later_tile(i):
            at = pl.multiple_of(i * TILE, TILE)
            weight = weight_v[:, pl.ds(at, TILE)]
            up = up_v[:, pl.ds(pl.multiple_of(lax.rem(i, 3) * TILE, TILE), TILE)]
            later = dot_nn(norm_v[prompt_total:], weight) + dot_nn(spread_v[i // 3], up)
            return at, weight, later

        def key_tile(i, carry):
            at, weight, later = later_tile(i)
            shift = jnp.where(i >= 8, bias(at + width, TILE), 0.0)
            to = pl.ds(pl.multiple_of(at - width, TILE), TILE)
            kv_v[prompt_total:, to] = (later + shift).astype(jnp.bfloat16)
            early = dot_nn(norm_v[:prompt_total], weight)
            kv_v[:prompt_total, to] = (early + shift).astype(jnp.bfloat16)
            return carry

        def query_tile(i, carry):
            at, weight, later = later_tile(i)
            shift = bias(at + 2 * width, TILE)
            to = pl.ds(at, TILE)
            q_v[prompt_rows:, to] = (later + shift).astype(jnp.bfloat16)
            mine = norm_v[pl.ds(pl.multiple_of(seq * prompt_rows, 128), prompt_rows)]
            q_v[:prompt_rows, to] = (dot_nn(mine, weight) + shift).astype(jnp.bfloat16)
            return carry

        lax.fori_loop(4, 12, key_tile, 0)
        store(kv_v, kv_out)
        tick(8)
        ready(5)
        load_out = load(4, w_out_v, 4)
        lax.fori_loop(0, 4, query_tile, 0)
        store(q_v, q_out)

        def attend(i, carry):
            cols = pl.ds(pl.multiple_of(i * 128, 128), 128)
            values = pl.ds(pl.multiple_of(i * 128 + width, 128), 128)

            @pl.when(i == pairs // 2)
            def _():
                tick(9)

            attention_forward(
                sizes,
                q_v.at[:, cols],
                kv_v.at[:, cols],
                kv_v.at[:, values],
                ctx_v.at[:, cols],
                lse_v.at[:, cols],
                wide_v,
            )
            return carry

        lax.fori_loop(0, pairs, attend, 0)
        store(ctx_v, ctx_out)
        store(lse_v, lse_out)
        tick(10)
        ready(6)
        ready(7)
        load_fc = load(5, weight_v, 5)
        load_out.wait()
        inner(1, ctx_v[prompt_rows:], width, width)
        for j in range(4):
            cols = slice(j * TILE, (j + 1) * TILE)
            mixed = dot_nn(ctx_v[...], w_out_v[:, cols]) + bias_ref[
                :, 4 * width + j * TILE : 4 * width + (j + 1) * TILE
            ]
            mixed = tokens_ref[:, cols].astype(jnp.float32) + mixed
            extra = dot_nn(spread_v[j], up_v[:, UP_STARTS[1] : UP_STARTS[1] + TILE])
            h_v[:prompt_rows, cols] = mixed[:prompt_rows]
            h_v[prompt_rows:, cols] = mixed[prompt_rows:] + extra
        store(h_v, h_out)
        normalize_rows(
            read_hidden, write_hidden, rows, gains_ref[1:2], bias_ref[:, width : 2 * width]
        )
        store(n_v, n_out)
        inner(2, n_v[prompt_rows:], 2 * width, width)
        load_fc.wait()

        def put_f(i, slot):
            to = pl.ds(pl.multiple_of(i * TILE, TILE), TILE)
            return pltpu.make_async_copy(f_v.at[slot], f_out.at[:, to], f_sem.at[slot])

        tiles = hidden_units // TILE

        def hidden_tile(i, carry):
            at = pl.multiple_of(i * TILE, TILE)
            cols = pl.ds(at, TILE)
            slot = lax.rem(i, 2)

            @pl.when(i == tiles // 2)
            def _():
                tick(11)

            @pl.when(i >= 2)
            def _():
                put_f(i - 2, slot).wait()

            wide = dot_nn(n_v[...], weight_v[:, cols]) + bias(at + 6 * width, TILE)
            up = up_v[
                :, pl.ds(pl.multiple_of(UP_STARTS[2] + lax.rem(i, 4) * TILE, TILE), TILE)
            ]
            extra = dot_nn(spread_v[i // 4], up)
            later = wide[prompt_rows:] + extra
            f_v[slot, :prompt_rows] = wide[:prompt_rows]
            f_v[slot, prompt_rows:] = later
            put_f(i, slot).start()
            gl_v[:prompt_rows, cols] = gelu_tanh(wide[:prompt_rows]).astype(jnp.bfloat16)
            gl_v[prompt_rows:, cols] = gelu_tanh(later).astype(jnp.bfloat16)
            return carry

        lax.fori_loop(0, tiles, hidden_tile, 0)
        put_f(tiles - 2, 0).wait()
        put_f(tiles - 1, 1).wait()
        store(gl_v, gl_out)
        tick(12)
        ready(8)
        ready(9)
        for ch in range(len(chunks)):
            finish(ch)
        for copy in stores:
            copy.wait()

    bf, f32 = jnp.bfloat16, jnp.float32
    vmem = pl.BlockSpec(memory_space=pltpu.VMEM)
    hbm = pl.BlockSpec(memory_space=pl.ANY)
    return pl.pallas_call(
        kernel,
        in_specs=[pl.BlockSpec(memory_space=pltpu.SMEM)] + [vmem] * (2 + count),
        out_specs=[hbm] * 8 + [vmem] + [hbm] * count,
        out_shape=[
            jax.ShapeDtypeStruct((rows, width), bf),
            jax.ShapeDtypeStruct((keys, 2 * width), bf),
            jax.ShapeDtypeStruct((rows, width), bf),
            jax.ShapeDtypeStruct((rows, width), f32),
            jax.ShapeDtypeStruct((rows, width), f32),
            jax.ShapeDtypeStruct((rows, width), bf),
            jax.ShapeDtypeStruct((rows, hidden_units), f32),
            jax.ShapeDtypeStruct((rows, hidden_units), bf),
            jax.ShapeDtypeStruct((3, CONT_LEN, ADAPTER_RANK), bf),
        ]
        + gathered,
        scratch_shapes=[
            pltpu.VMEM((prompt_total, width), bf),
            pltpu.VMEM((keys, width), bf),
            pltpu.VMEM((width, hidden_units), bf),
            pltpu.VMEM((width, width), bf),
            pltpu.VMEM((rows, width), bf),
            pltpu.VMEM((keys, 2 * width), bf),
            pltpu.VMEM((keys, 256), bf),
            pltpu.VMEM((rows, width), bf),
            pltpu.VMEM((rows, width), f32),
            pltpu.VMEM((rows, width), f32),
            pltpu.VMEM((rows, width), bf),
            pltpu.VMEM((rows, hidden_units), bf),
            pltpu.VMEM((2, rows, TILE), f32),
            pltpu.VMEM(gathered[1].shape, bf),
            pltpu.VMEM(gathered[2].shape, bf),
            pltpu.VMEM((ADAPTER_RANK, 4 * QUARTER), bf),
            pltpu.VMEM((64, UP_QUARTER), bf),
            pltpu.VMEM((4, CONT_LEN, 64), bf),
            dma((6,)),
            dma((8,)),
            dma((2,)),
        ]
        + sems,
        compiler_params=pltpu.CompilerParams(
            collective_id=collective_id, has_side_effects=True, vmem_limit_bytes=VMEM_LIMIT
        ),
    )(ident, tokens, gains, biases, *shards)


def gelu_tanh(field):
    inner = 0.7978845608028654 * (field + 0.044715 * field * field * field)
    return 0.5 * field * (1.0 + jnp.tanh(inner))


def adapter_scratch(cols):
    dma = pltpu.SemaphoreType.DMA
    return [
        pltpu.VMEM((2, 16, cols), jnp.bfloat16),
        pltpu.VMEM((16, 128), jnp.bfloat16),
        pltpu.VMEM((3, 4, 16, cols), jnp.bfloat16),
        pltpu.VMEM((3, 4, 16, cols), jnp.bfloat16),
        pltpu.VMEM((4, 16, cols), jnp.float32),
        pltpu.VMEM((3, 16, cols), jnp.bfloat16),
        pltpu.VMEM((3, 16, cols), jnp.bfloat16),
        dma((3,)),
        dma((3,)),
        dma((3,)),
        dma((3,)),
        dma((3,)),
        dma((3,)),
    ]


def adapter_stages(term_ref, id_ref, out_ref, scratch):
    from_core, other_id, to_grp, from_grp, total, to_z, from_z = scratch[:7]
    a_send, a_recv, g_send, g_recv, z_send, z_recv = scratch[7:]
    g, s = lax.axis_index("grp"), lax.axis_index("seq")
    core, z = lax.rem(s, 2), s // 2
    other = 1 - core
    partner = (g, z * 2 + other)
    grps = [lax.rem(g + d, 4) for d in range(1, 4)]
    lines = [lax.rem(z + d, 4) for d in range(1, 4)]

    def enter():
        peers = [partner] + [(far, s) for far in grps] + [(g, far * 2 + core) for far in lines]
        barrier = pltpu.get_barrier_semaphore()
        for peer in peers:
            pl.semaphore_signal(barrier, inc=1, device_id=peer, device_id_type=MESH)
        pl.semaphore_wait(barrier, len(peers))

    def remote(src, dst, send_sem, recv_sem, device):
        return pltpu.make_async_remote_copy(
            src_ref=src,
            dst_ref=dst,
            send_sem=send_sem,
            recv_sem=recv_sem,
            device_id=device,
            device_id_type=MESH,
        )

    copies_a = [
        remote(term_ref.at[i * 2 + other], from_core.at[i], a_send.at[i], a_recv.at[i], partner)
        for i in range(2)
    ] + [remote(id_ref, other_id, a_send.at[2], a_recv.at[2], partner)]
    copies_g = [
        remote(to_grp.at[d], from_grp.at[d], g_send.at[d], g_recv.at[d], (grps[d], s))
        for d in range(3)
    ]
    copies_z = [
        remote(to_z.at[d], from_z.at[d], z_send.at[d], z_recv.at[d], (g, lines[d] * 2 + core))
        for d in range(3)
    ]

    def start(copies):
        for copy in copies:
            copy.start()

    def wait(copies):
        for copy in copies:
            copy.wait()

    def select():
        wait(copies_a)
        mine = id_ref[0:1, 0:1].astype(jnp.float32)
        theirs = other_id[0:1, 0:1].astype(jnp.float32)
        for d, grp in enumerate(grps + [g]):
            for slot in range(4):
                adapter = (grp * 2 + slot // 2).astype(jnp.float32)
                own_term = term_ref[(slot % 2) * 2 + core].astype(jnp.float32)
                other_term = from_core[slot % 2].astype(jnp.float32)
                picked = jnp.where(mine == adapter, own_term, 0.0) + jnp.where(
                    theirs == adapter, other_term, 0.0
                )
                if d < 3:
                    to_grp[d, slot] = picked.astype(jnp.bfloat16)
                else:
                    total[slot] = picked

    def add_grps():
        wait(copies_g)
        for slot in range(4):
            total[slot] += sum(from_grp[d, slot].astype(jnp.float32) for d in range(3))
        for d in range(3):
            to_z[d] = total[lines[d]].astype(jnp.bfloat16)

    def add_lines():
        wait(copies_z)
        out_ref[...] = total[z] + sum(from_z[d].astype(jnp.float32) for d in range(3))

    return (
        enter,
        lambda: start(copies_a),
        select,
        lambda: start(copies_g),
        add_grps,
        lambda: start(copies_z),
        add_lines,
    )


def attend_back_and_reduce(q, kv, d_ctx, ctx, lse, term, ident, collective_id):
    rows, keys, pairs = q.shape[0], kv.shape[0], q.shape[1] // 128
    sizes = (rows - CONT_LEN, keys - CONT_LEN, CONT_LEN)
    term_cols = term.shape[2]

    def kernel(q_ref, k_ref, v_ref, d_ref, ctx_ref, lse_ref, term_ref, id_ref, *refs):
        dq_ref, dk_ref, dv_ref, out_ref, k_sum, v_sum = refs[:6]
        enter, send_core, select, send_grp, add_grps, send_z, add_lines = adapter_stages(
            term_ref, id_ref, out_ref, refs[6:]
        )
        step = pl.program_id(0)

        @pl.when(step == 0)
        def _():
            enter()
            send_core()

        attention_backward(
            sizes,
            q_ref,
            k_ref,
            v_ref,
            d_ref,
            ctx_ref,
            lse_ref,
            dq_ref,
            dk_ref,
            dv_ref,
            k_sum,
            v_sum,
        )

        @pl.when(step == 0)
        def _():
            select()
            send_grp()

        @pl.when(step == pairs - 4)
        def _():
            add_grps()
            send_z()

        @pl.when(step == pairs - 1)
        def _():
            add_lines()

    def pair(i):
        return (0, i)

    row_spec = pl.BlockSpec((rows, 128), pair)
    key_spec = pl.BlockSpec((keys, 128), pair)
    whole = pl.BlockSpec(memory_space=pltpu.VMEM)
    return pl.pallas_call(
        kernel,
        grid=(pairs,),
        in_specs=[
            row_spec,
            key_spec,
            pl.BlockSpec((keys, 128), lambda i: (0, pairs + i)),
            row_spec,
            row_spec,
            row_spec,
            whole,
            whole,
        ],
        out_specs=[row_spec, key_spec, key_spec, whole],
        out_shape=[
            jax.ShapeDtypeStruct(q.shape, jnp.bfloat16),
            jax.ShapeDtypeStruct((keys, q.shape[1]), jnp.bfloat16),
            jax.ShapeDtypeStruct((keys, q.shape[1]), jnp.bfloat16),
            jax.ShapeDtypeStruct((16, term_cols), jnp.float32),
        ],
        scratch_shapes=[pltpu.VMEM((keys, 128), jnp.float32)] * 2 + adapter_scratch(term_cols),
        compiler_params=pltpu.CompilerParams(
            collective_id=collective_id, has_side_effects=True, vmem_limit_bytes=VMEM_LIMIT
        ),
    )(q, kv, kv, d_ctx, ctx, lse, term, ident)


def last_exchange(rows_term, term, ident, collective_id):
    blocks, cols = rows_term.shape[0], rows_term.shape[3]
    rows = rows_term.shape[2]
    term_cols = term.shape[2]
    dma = pltpu.SemaphoreType.DMA

    def kernel(x_ref, term_ref, id_ref, sum_ref, out_ref, pair_in, to_line, from_line, *refs):
        p_send, p_recv, l_send, l_recv = refs[:4]
        enter, send_core, select, send_grp, add_grps, send_z, add_lines = adapter_stages(
            term_ref, id_ref, out_ref, refs[4:]
        )
        g, s = lax.axis_index("grp"), lax.axis_index("seq")
        core, z = lax.rem(s, 2), s // 2
        far_z = [lax.rem(z + d, blocks) for d in range(1, blocks)]
        across = pltpu.make_async_remote_copy(
            src_ref=x_ref.at[:, 1 - core],
            dst_ref=pair_in,
            send_sem=p_send,
            recv_sem=p_recv,
            device_id=(g, z * 2 + 1 - core),
            device_id_type=MESH,
        )
        along = [
            pltpu.make_async_remote_copy(
                src_ref=to_line.at[d],
                dst_ref=from_line.at[d],
                send_sem=l_send.at[d],
                recv_sem=l_recv.at[d],
                device_id=(g, far * 2 + core),
                device_id_type=MESH,
            )
            for d, far in enumerate(far_z)
        ]
        enter()
        send_core()
        across.start()
        select()
        send_grp()
        across.wait()
        for d, far in enumerate(far_z):
            both = x_ref[far, core].astype(jnp.float32) + pair_in[far].astype(jnp.float32)
            to_line[d] = both.astype(jnp.bfloat16)
            along[d].start()
        add_grps()
        send_z()
        total = x_ref[z, core].astype(jnp.float32) + pair_in[z].astype(jnp.float32)
        for d, copy in enumerate(along):
            copy.wait()
            total = total + from_line[d].astype(jnp.float32)
        sum_ref[...] = total
        add_lines()

    whole = pl.BlockSpec(memory_space=pltpu.VMEM)
    return pl.pallas_call(
        kernel,
        in_specs=[whole] * 3,
        out_specs=[whole] * 2,
        out_shape=[
            jax.ShapeDtypeStruct((rows, cols), jnp.float32),
            jax.ShapeDtypeStruct((16, term_cols), jnp.float32),
        ],
        scratch_shapes=[
            pltpu.VMEM((blocks, rows, cols), jnp.bfloat16),
            pltpu.VMEM((blocks - 1, rows, cols), jnp.bfloat16),
            pltpu.VMEM((blocks - 1, rows, cols), jnp.bfloat16),
            dma,
            dma,
            dma((blocks - 1,)),
            dma((blocks - 1,)),
        ]
        + adapter_scratch(term_cols),
        compiler_params=pltpu.CompilerParams(
            collective_id=collective_id, has_side_effects=True, vmem_limit_bytes=VMEM_LIMIT
        ),
    )(rows_term, term, ident)


def local_general(
    tokens,
    cotangent,
    query_key_value_weight,
    attention_out_weight,
    feedforward_in_weight,
    feedforward_out_weight,
    layer_norm_gains,
    biases,
    adapter_down_matrices,
    adapter_up_matrices,
    adapter_of_continuation,
):
    row_count = tokens.shape[0]
    prompt_rows = row_count - CONT_LEN
    prompt_total = prompt_rows * lax.axis_size("seq")
    key_count = prompt_total + CONT_LEN
    seq_index = lax.axis_index("seq")
    adapter_index = adapter_of_continuation[0, 0]
    weight_shards = (
        query_key_value_weight,
        attention_out_weight,
        feedforward_in_weight,
        feedforward_out_weight,
        adapter_down_matrices,
        adapter_up_matrices,
    )
    gathered_rows = (
        lax.all_gather(weight_shards[0], ("grp", "seq"), axis=0, tiled=True),
        lax.all_gather(weight_shards[1], ("grp", "seq"), axis=0, tiled=True),
        lax.all_gather(weight_shards[2], ("grp", "seq"), axis=0, tiled=True),
        lax.all_gather(weight_shards[3], ("grp", "seq"), axis=0, tiled=True),
        lax.all_gather(weight_shards[4], ("grp", "seq"), axis=0, tiled=True),
        lax.all_gather(weight_shards[5], ("grp", "seq"), axis=0, tiled=True),
    )
    weight_matrices, adapter_sections = unpack_sections(gathered_rows, adapter_index)
    frozen_query_key_value, frozen_attention_out, frozen_feedforward_in, frozen_feedforward_out = (
        weight_matrices
    )
    (
        down_query_key_value,
        down_attention_out,
        down_feedforward_in,
        down_feedforward_out,
        up_query_key_value,
        up_attention_out,
        up_feedforward_in,
        up_feedforward_out,
    ) = adapter_sections
    shift_one = biases[:MODEL_WIDTH]
    shift_two = biases[MODEL_WIDTH : 2 * MODEL_WIDTH]
    query_key_value_bias = jnp.concatenate(
        [
            biases[2 * MODEL_WIDTH : 3 * MODEL_WIDTH],
            jnp.zeros((MODEL_WIDTH,), jnp.float32),
            biases[3 * MODEL_WIDTH : 4 * MODEL_WIDTH],
        ]
    )
    bias_out = biases[4 * MODEL_WIDTH : 5 * MODEL_WIDTH]
    bias_proj = biases[5 * MODEL_WIDTH : 6 * MODEL_WIDTH]
    bias_fc = biases[6 * MODEL_WIDTH :]
    inputs = tokens.astype(jnp.float32)
    normed_one = layer_norm(inputs, layer_norm_gains[0], shift_one).astype(jnp.bfloat16)
    inner_one = product(normed_one[prompt_rows:], down_query_key_value).astype(jnp.bfloat16)
    mixed_query_key_value = product(normed_one, frozen_query_key_value) + query_key_value_bias
    mixed_query_key_value = mixed_query_key_value.at[prompt_rows:].add(
        product(inner_one, up_query_key_value)
    )
    qkv_rows = mixed_query_key_value.astype(jnp.bfloat16)
    prompt_keys, prompt_values = (
        lax.all_gather(
            qkv_rows[:prompt_rows, MODEL_WIDTH : 2 * MODEL_WIDTH], "seq", axis=0, tiled=True
        ),
        lax.all_gather(qkv_rows[:prompt_rows, 2 * MODEL_WIDTH :], "seq", axis=0, tiled=True),
    )
    all_keys = jnp.concatenate(
        [prompt_keys, qkv_rows[prompt_rows:, MODEL_WIDTH : 2 * MODEL_WIDTH]], 0
    )
    all_values = jnp.concatenate([prompt_values, qkv_rows[prompt_rows:, 2 * MODEL_WIDTH :]], 0)
    allowed = visible(row_count, prompt_rows, prompt_total, key_count, seq_index)
    query_heads = split_heads(qkv_rows[:, :MODEL_WIDTH])
    key_heads = split_heads(all_keys)
    value_heads = split_heads(all_values)

    def forward_head(operands):
        query_head, key_head, value_head = operands
        scores = jnp.where(allowed, product_nt(query_head, key_head) * 0.125, NEGATIVE)
        row_max = jnp.max(scores, axis=1, keepdims=True)
        exp_scores = jnp.exp(scores - row_max)
        exp_total = jnp.sum(exp_scores, axis=1, keepdims=True)
        weights = (exp_scores / exp_total).astype(jnp.bfloat16)
        return (product(weights, value_head), (row_max + jnp.log(exp_total))[:, 0])

    head_contexts, log_total = lax.map(forward_head, (query_heads, key_heads, value_heads))
    attention_context = merge_heads(head_contexts).astype(jnp.bfloat16)
    inner_two = product(attention_context[prompt_rows:], down_attention_out).astype(jnp.bfloat16)
    attention_output = product(attention_context, frozen_attention_out) + bias_out
    attention_output = attention_output.at[prompt_rows:].add(product(inner_two, up_attention_out))
    hidden = inputs + attention_output
    normed_two = layer_norm(hidden, layer_norm_gains[1], shift_two).astype(jnp.bfloat16)
    inner_three = product(normed_two[prompt_rows:], down_feedforward_in).astype(jnp.bfloat16)
    before_activation = product(normed_two, frozen_feedforward_in) + bias_fc
    before_activation = before_activation.at[prompt_rows:].add(
        product(inner_three, up_feedforward_in)
    )
    activated_hidden = jax.nn.gelu(before_activation, approximate=True).astype(jnp.bfloat16)
    inner_four = product(activated_hidden[prompt_rows:], down_feedforward_out).astype(jnp.bfloat16)
    adapter_branch = product(activated_hidden, frozen_feedforward_out) + bias_proj
    adapter_branch = adapter_branch.at[prompt_rows:].add(product(inner_four, up_feedforward_out))
    outputs = (hidden + adapter_branch).astype(jnp.bfloat16)
    weight_matrices, adapter_sections = unpack_sections(
        (
            lax.all_gather(weight_shards[0], ("grp", "seq"), axis=0, tiled=True),
            lax.all_gather(weight_shards[1], ("grp", "seq"), axis=0, tiled=True),
            lax.all_gather(weight_shards[2], ("grp", "seq"), axis=0, tiled=True),
            lax.all_gather(weight_shards[3], ("grp", "seq"), axis=0, tiled=True),
            lax.all_gather(weight_shards[4], ("grp", "seq"), axis=0, tiled=True),
            lax.all_gather(weight_shards[5], ("grp", "seq"), axis=0, tiled=True),
        ),
        adapter_index,
    )
    frozen_query_key_value, frozen_attention_out, frozen_feedforward_in, frozen_feedforward_out = (
        weight_matrices
    )
    (
        down_query_key_value,
        down_attention_out,
        down_feedforward_in,
        down_feedforward_out,
        up_query_key_value,
        up_attention_out,
        up_feedforward_in,
        up_feedforward_out,
    ) = adapter_sections
    grad_inner_four = product_nt(cotangent[prompt_rows:], up_feedforward_out).astype(jnp.bfloat16)
    grad_act = product_nt(cotangent, frozen_feedforward_out)
    grad_act = grad_act.at[prompt_rows:].add(product_nt(grad_inner_four, down_feedforward_out))
    gelu_pull = jax.vjp(lambda field: jax.nn.gelu(field, approximate=True), before_activation)[1]
    grad_pre = gelu_pull(grad_act)[0].astype(jnp.bfloat16)
    grad_inner_three = product_nt(grad_pre[prompt_rows:], up_feedforward_in).astype(jnp.bfloat16)
    grad_normed_two = product_nt(grad_pre, frozen_feedforward_in)
    grad_normed_two = grad_normed_two.at[prompt_rows:].add(
        product_nt(grad_inner_three, down_feedforward_in)
    )
    second_pull = jax.vjp(lambda field: layer_norm(field, layer_norm_gains[1], shift_two), hidden)[
        1
    ]
    grad_hidden = cotangent.astype(jnp.float32) + second_pull(grad_normed_two)[0]
    grad_attn = grad_hidden.astype(jnp.bfloat16)
    grad_inner_two = product_nt(grad_attn[prompt_rows:], up_attention_out).astype(jnp.bfloat16)
    grad_context = product_nt(grad_attn, frozen_attention_out)
    grad_context = (
        grad_context.at[prompt_rows:]
        .add(product_nt(grad_inner_two, down_attention_out))
        .astype(jnp.bfloat16)
    )

    def backward_head(operands):
        query_head, key_head, value_head, grad_head, total_head = operands
        scores = jnp.where(allowed, product_nt(query_head, key_head) * 0.125, NEGATIVE)
        prob_full = jnp.exp(scores - total_head[:, None])
        weights = prob_full.astype(jnp.bfloat16)
        grad_weights = product_nt(grad_head, value_head)
        row_delta = jnp.sum(prob_full * grad_weights, axis=1, keepdims=True)
        grad_scores = (prob_full * (grad_weights - row_delta)).astype(jnp.bfloat16)
        return (
            product(grad_scores, key_head) * 0.125,
            product_tn(grad_scores, query_head) * 0.125,
            product_tn(weights, grad_head),
        )

    grad_q, grad_k, grad_v = lax.map(
        backward_head, (query_heads, key_heads, value_heads, split_heads(grad_context), log_total)
    )
    grad_query = merge_heads(grad_q)
    grad_keys = merge_heads(grad_k)
    grad_values = merge_heads(grad_v)
    own_keys, own_values = (
        lax.psum_scatter(
            grad_keys[:prompt_total].astype(jnp.bfloat16), "seq", scatter_dimension=0, tiled=True
        ).astype(jnp.float32),
        lax.psum_scatter(
            grad_values[:prompt_total].astype(jnp.bfloat16), "seq", scatter_dimension=0, tiled=True
        ).astype(jnp.float32),
    )
    grad_qkv = jnp.concatenate(
        [
            grad_query,
            jnp.concatenate([own_keys, grad_keys[prompt_total:]], 0),
            jnp.concatenate([own_values, grad_values[prompt_total:]], 0),
        ],
        1,
    ).astype(jnp.bfloat16)
    grad_inner_one = product_nt(grad_qkv[prompt_rows:], up_query_key_value).astype(jnp.bfloat16)
    grad_normed_one = product_nt(grad_qkv, frozen_query_key_value)
    grad_normed_one = grad_normed_one.at[prompt_rows:].add(
        product_nt(grad_inner_one, down_query_key_value)
    )
    first_pull = jax.vjp(lambda field: layer_norm(field, layer_norm_gains[0], shift_one), inputs)[1]
    input_grad = grad_hidden + first_pull(grad_normed_one)[0]
    down_term = jnp.concatenate(
        [
            product_tn(normed_one[prompt_rows:], grad_inner_one),
            product_tn(attention_context[prompt_rows:], grad_inner_two),
            product_tn(normed_two[prompt_rows:], grad_inner_three),
            product_tn(activated_hidden[prompt_rows:], grad_inner_four),
        ],
        0,
    )
    up_term = jnp.concatenate(
        [
            product_tn(inner_one, grad_qkv[prompt_rows:]),
            product_tn(inner_two, grad_attn[prompt_rows:]),
            product_tn(inner_three, grad_pre[prompt_rows:]),
            product_tn(inner_four, cotangent[prompt_rows:]),
        ],
        1,
    )
    select = (jnp.arange(ADAPTER_COUNT, dtype=jnp.int32) == adapter_index).astype(jnp.float32)
    down_grad, up_grad = (
        lax.psum_scatter(
            (select[:, None, None] * down_term[None]).reshape(-1),
            ("grp", "seq"),
            scatter_dimension=0,
            tiled=True,
        ),
        lax.psum_scatter(
            (select[:, None, None] * up_term[None]).reshape(-1),
            ("grp", "seq"),
            scatter_dimension=0,
            tiled=True,
        ),
    )
    return (outputs, input_grad, down_grad, up_grad)


def fast(
    tokens,
    cotangent,
    query_key_value_weight,
    attention_out_weight,
    feedforward_in_weight,
    feedforward_out_weight,
    layer_norm_gains,
    biases,
    adapter_down_matrices,
    adapter_up_matrices,
    adapter_of_continuation,
):
    groups = (lax.axis_size("grp"), lax.axis_size("seq"))
    prompt_rows = tokens.shape[0] - CONT_LEN
    prompt_total = prompt_rows * groups[1]
    up_cols = 5 * MODEL_WIDTH + HIDDEN_UNITS
    adapter_index = adapter_of_continuation[0, 0]
    shift_one = biases[:MODEL_WIDTH]
    shift_two = biases[MODEL_WIDTH : 2 * MODEL_WIDTH]
    bias_proj = biases[5 * MODEL_WIDTH : 6 * MODEL_WIDTH]
    ups_shard = adapter_up_matrices.reshape(4, up_cols)
    up_parts, first = [], 0
    for size in UP_SECTIONS:
        up_parts.append(ups_shard[:, first : first + size].reshape(16, size // 4))
        first += size
    (
        queries,
        keys_values,
        context,
        log_total,
        hidden,
        normed_two,
        before_activation,
        activated,
        inners,
        _,
        downs,
        ups,
        w_qkv,
        w_out,
        w_fc,
        w_proj,
    ) = forward_and_gather(
        groups,
        adapter_of_continuation,
        tokens,
        layer_norm_gains,
        biases.reshape(1, -1),
        [
            adapter_down_matrices.reshape(-1, ADAPTER_RANK).T,
            jnp.concatenate(up_parts, 1),
            query_key_value_weight.reshape(-1, 3 * MODEL_WIDTH),
            attention_out_weight.reshape(-1, MODEL_WIDTH),
            feedforward_in_weight.reshape(-1, HIDDEN_UNITS),
            feedforward_out_weight.reshape(-1, MODEL_WIDTH),
        ],
        1,
    )
    down_all = lax.dynamic_index_in_dim(
        downs.reshape(ADAPTER_COUNT, 4, ADAPTER_RANK, QUARTER), adapter_index, 0, keepdims=False
    )
    down_all = jnp.concatenate([down_all[i] for i in range(4)], 1)
    up_all = lax.dynamic_index_in_dim(
        ups.reshape(ADAPTER_COUNT, ADAPTER_RANK, 4, UP_QUARTER), adapter_index, 0, keepdims=False
    )
    down_qkv = down_all[:, :MODEL_WIDTH]
    down_out = down_all[:, MODEL_WIDTH : 2 * MODEL_WIDTH]
    down_fc = down_all[:, 2 * MODEL_WIDTH : 3 * MODEL_WIDTH]
    down_proj = down_all[:, 3 * MODEL_WIDTH :]
    up_qkv, up_out, up_fc, up_proj = (
        up_all[:, :, start : start + size // 4].reshape(ADAPTER_RANK, size)
        for start, size in zip(UP_STARTS, UP_SECTIONS)
    )
    inner_one, inner_two, inner_three = inners[0], inners[1], inners[2]
    inputs = tokens.astype(jnp.float32)
    normed_later = layer_norm(inputs[prompt_rows:], layer_norm_gains[0], shift_one).astype(
        jnp.bfloat16
    )
    inner_four = product_nt(activated[prompt_rows:], down_proj).astype(jnp.bfloat16)
    branch = product(activated, w_proj) + bias_proj
    branch = branch.at[prompt_rows:].add(product(inner_four, up_proj))
    outputs = (hidden + branch).astype(jnp.bfloat16)

    later_cotangent = cotangent[prompt_rows:]
    grad_inner_four = product_nt(later_cotangent, up_proj).astype(jnp.bfloat16)
    grad_act = product_nt(cotangent, w_proj)
    grad_act = grad_act.at[prompt_rows:].add(product(grad_inner_four, down_proj))
    gelu_pull = jax.vjp(lambda field: jax.nn.gelu(field, approximate=True), before_activation)[1]
    grad_pre = gelu_pull(grad_act)[0].astype(jnp.bfloat16)
    grad_inner_three = product_nt(grad_pre[prompt_rows:], up_fc).astype(jnp.bfloat16)
    grad_normed_two = product_nt(grad_pre, w_fc)
    grad_normed_two = grad_normed_two.at[prompt_rows:].add(product(grad_inner_three, down_fc))
    second_pull = jax.vjp(lambda field: layer_norm(field, layer_norm_gains[1], shift_two), hidden)[
        1
    ]
    grad_hidden = cotangent.astype(jnp.float32) + second_pull(grad_normed_two)[0]
    grad_attn = grad_hidden.astype(jnp.bfloat16)
    grad_inner_two = product_nt(grad_attn[prompt_rows:], up_out).astype(jnp.bfloat16)
    grad_context = product_nt(grad_attn, w_out)
    grad_context = (
        grad_context.at[prompt_rows:]
        .add(product(grad_inner_two, down_out))
        .astype(jnp.bfloat16)
    )

    down_early = jnp.concatenate(
        [
            jnp.zeros((ADAPTER_RANK, MODEL_WIDTH), jnp.float32),
            product_tn(grad_inner_two, context[prompt_rows:]),
            product_tn(grad_inner_three, normed_two[prompt_rows:]),
            product_tn(grad_inner_four, activated[prompt_rows:]),
        ],
        1,
    )
    up_early = [
        product_tn(inner_two, grad_attn[prompt_rows:]),
        product_tn(inner_three, grad_pre[prompt_rows:]),
        product_tn(inner_four, later_cotangent),
    ]
    up_early = jnp.concatenate([x.reshape(4, 16, -1) for x in up_early], 2)
    down_early = jnp.stack([down_early[:, i * QUARTER : (i + 1) * QUARTER] for i in range(4)])
    early_term = jnp.concatenate([down_early, up_early], 2).astype(jnp.bfloat16)
    ident = jnp.full((16, 128), adapter_index, jnp.int32).astype(jnp.bfloat16)

    grad_q, grad_k, grad_v, early = attend_back_and_reduce(
        queries, keys_values, grad_context, context, log_total, early_term, ident, 3
    )

    w_q, w_k, w_v = (
        w_qkv[:, :MODEL_WIDTH],
        w_qkv[:, MODEL_WIDTH : 2 * MODEL_WIDTH],
        w_qkv[:, 2 * MODEL_WIDTH :],
    )
    rows_term = (
        product_nt(grad_k[:prompt_total], w_k) + product_nt(grad_v[:prompt_total], w_v)
    ).astype(jnp.bfloat16)
    grad_later = jnp.concatenate(
        [grad_q[prompt_rows:], grad_k[prompt_total:], grad_v[prompt_total:]], 1
    )
    grad_inner_one = product_nt(grad_later, up_qkv).astype(jnp.bfloat16)
    down_late = product_tn(grad_inner_one, normed_later)
    down_late = jnp.stack([down_late] + [jnp.zeros_like(down_late)] * 3)
    up_late = product_tn(inner_one, grad_later).reshape(4, 16, -1)
    late_term = jnp.concatenate([down_late, up_late], 2).astype(jnp.bfloat16)
    prompt_sum, late = last_exchange(
        rows_term.reshape(groups[1] // 2, 2, prompt_rows, MODEL_WIDTH), late_term, ident, 4
    )
    later_normed_grad = product_nt(grad_later, w_qkv) + product(grad_inner_one, down_qkv)
    prompt_normed_grad = product_nt(grad_q[:prompt_rows], w_q) + prompt_sum
    grad_normed_one = jnp.concatenate([prompt_normed_grad, later_normed_grad], 0)
    first_pull = jax.vjp(lambda field: layer_norm(field, layer_norm_gains[0], shift_one), inputs)[1]
    input_grad = grad_hidden + first_pull(grad_normed_one)[0]

    down_grad = early[:, :QUARTER].at[:, :MODEL_WIDTH].add(late[:, :MODEL_WIDTH])
    down_grad = down_grad.T.reshape(-1)
    up_pieces = [late[:, MODEL_WIDTH:]]
    for start, size in zip(UP_STARTS[1:], UP_SECTIONS[1:]):
        start += QUARTER - UP_STARTS[1]
        up_pieces.append(early[:, start : start + size // 4])
    up_grad = jnp.concatenate([x.reshape(4, -1) for x in up_pieces], 1).reshape(-1)
    return (outputs, input_grad, down_grad, up_grad)


def solution(mesh):
    placed = (
        P(("grp", "seq"), None),
        P(("grp", "seq"), None),
        P(("grp", "seq")),
        P(("grp", "seq")),
        P(("grp", "seq")),
        P(("grp", "seq")),
        P(),
        P(),
        P(("grp", "seq")),
        P(("grp", "seq")),
        P(("grp", "seq"), None),
    )
    fits = mesh.shape["grp"] == 4 and mesh.shape["seq"] == 8
    return jax.shard_map(
        fast if fits else local_general,
        mesh=mesh,
        in_specs=placed,
        out_specs=(
            P(("grp", "seq"), None),
            P(("grp", "seq"), None),
            P(("grp", "seq")),
            P(("grp", "seq")),
        ),
        check_vma=False,
    )
```

```python
import functools

import jax
import jax.numpy as jnp
from jax import lax
from jax.experimental import pallas as pl
from jax.experimental.pallas import tpu as pltpu
from jax.sharding import PartitionSpec as P

MODEL_WIDTH = 1024
HEADS = 16
HEAD_DIM = 64
HIDDEN_UNITS = 4096
ADAPTER_RANK = 16
ADAPTER_COUNT = 8
CONT_LEN = 512


EPSILON = 1e-05
NEGATIVE = -1e30


def product(left_side, right_side):
    return jnp.dot(left_side, right_side, preferred_element_type=jnp.float32)


def product_tn(left_side, right_side):
    return lax.dot_general(
        left_side, right_side, (((0,), (0,)), ((), ())), preferred_element_type=jnp.float32
    )


def product_nt(left_side, right_side):
    return lax.dot_general(
        left_side, right_side, (((1,), (1,)), ((), ())), preferred_element_type=jnp.float32
    )


def layer_norm(values, gain_vec, shift_vec):
    row_mean = jnp.mean(values, axis=-1, keepdims=True)
    centred = values - row_mean
    row_var = jnp.mean(centred * centred, axis=-1, keepdims=True)
    return centred * lax.rsqrt(row_var + EPSILON) * gain_vec + shift_vec


def unpack_sections(pieces, adapter_index):
    qkv_flat, out_flat, fc_flat, proj_flat, down_flat, up_flat = pieces
    every_down_matrix = down_flat.reshape(
        ADAPTER_COUNT, 3 * MODEL_WIDTH + HIDDEN_UNITS, ADAPTER_RANK
    )
    every_up_matrix = up_flat.reshape(ADAPTER_COUNT, ADAPTER_RANK, 5 * MODEL_WIDTH + HIDDEN_UNITS)
    down_rows = lax.dynamic_index_in_dim(every_down_matrix, adapter_index, 0, keepdims=False)
    up_cols = lax.dynamic_index_in_dim(every_up_matrix, adapter_index, 0, keepdims=False)
    weight_matrices = (
        qkv_flat.reshape(MODEL_WIDTH, 3 * MODEL_WIDTH),
        out_flat.reshape(MODEL_WIDTH, MODEL_WIDTH),
        fc_flat.reshape(MODEL_WIDTH, HIDDEN_UNITS),
        proj_flat.reshape(HIDDEN_UNITS, MODEL_WIDTH),
    )
    adapter_sections = (
        down_rows[:MODEL_WIDTH],
        down_rows[MODEL_WIDTH : 2 * MODEL_WIDTH],
        down_rows[2 * MODEL_WIDTH : 3 * MODEL_WIDTH],
        down_rows[3 * MODEL_WIDTH :],
        up_cols[:, : 3 * MODEL_WIDTH],
        up_cols[:, 3 * MODEL_WIDTH : 4 * MODEL_WIDTH],
        up_cols[:, 4 * MODEL_WIDTH : 4 * MODEL_WIDTH + HIDDEN_UNITS],
        up_cols[:, 4 * MODEL_WIDTH + HIDDEN_UNITS :],
    )
    return (weight_matrices, adapter_sections)


def visible(row_count, prompt_rows, prompt_total, key_count, seq_index):
    row_ids = jnp.arange(row_count, dtype=jnp.int32)[:, None]
    col_ids = jnp.arange(key_count, dtype=jnp.int32)[None, :]
    in_prompt = col_ids < prompt_total
    prompt_seen = in_prompt & (col_ids <= seq_index * prompt_rows + row_ids)
    later_seen = in_prompt | (col_ids - prompt_total <= row_ids - prompt_rows)
    return jnp.where(row_ids < prompt_rows, prompt_seen, later_seen)


def split_heads(values):
    return values.reshape(values.shape[0], HEADS, HEAD_DIM).transpose(1, 0, 2)


def merge_heads(values):
    return values.transpose(1, 0, 2).reshape(values.shape[1], HEADS * HEAD_DIM)


MESH = pl.DeviceIdType.MESH
SCALE2 = 0.125 * 1.4426950408889634
VMEM_LIMIT = 63 << 20


def gather_stages(groups, sizes, chunks, ins, outs, sems):
    grp_n, seq_n = groups
    z_n, y_n = seq_n // 2, grp_n // 2
    z_sem, x_sem, y_sem, d_sem, p_sem, s_sem, l_sem = sems
    g, s = lax.axis_index("grp"), lax.axis_index("seq")
    core, z = lax.rem(s, 2), s // 2
    gx, gy = lax.rem(g, 2), g // 2
    partner = (g, z * 2 + 1 - core)
    other_x = gy * 2 + 1 - gx
    x_next = (other_x, s)
    far_z = [lax.rem(z + d, z_n) for d in range(1, z_n)]
    far_y = [lax.rem(gy + d, y_n) for d in range(1, y_n)]
    y_next = [(y * 2 + gx, s) for y in far_y]

    def enter():
        peers = [partner, x_next] + y_next + [(g, far * 2 + core) for far in far_z]
        barrier = pltpu.get_barrier_semaphore()
        for peer in peers:
            pl.semaphore_signal(barrier, inc=1, device_id=peer, device_id_type=MESH)
        pl.semaphore_wait(barrier, len(peers))

    def place(ch, gg, ss):
        arr, row, rows, full = chunks[ch]
        block = gg * seq_n + ss if full else ss
        return outs[arr].at[pl.ds(pl.multiple_of(block * sizes[arr] + row, 16), rows)]

    def send(ch, src, gg, ss, sem, device):
        pltpu.make_async_remote_copy(
            src_ref=src,
            dst_ref=place(ch, gg, ss),
            send_sem=s_sem.at[ch],
            recv_sem=sem,
            device_id=device,
            device_id_type=MESH,
        ).start()

    def drain(ch, sem, count=1):
        arr, _, rows, _ = chunks[ch]
        block = outs[arr].at[pl.ds(0, count * rows)]
        pltpu.make_async_copy(block, block, sem).wait()

    def own(ch):
        arr, row, rows, full = chunks[ch]
        src = ins[arr].at[pl.ds(row, rows)]
        for far in far_z:
            send(ch, src, g, s, z_sem.at[ch, z], (g, far * 2 + core))
        if full:
            send(ch, src, g, s, x_sem.at[ch, z], x_next)
            for peer in y_next:
                send(ch, src, g, s, y_sem.at[ch, gy, z], peer)
        send(ch, src, g, s, p_sem.at[ch, 0], partner)
        pltpu.make_async_copy(src, place(ch, g, s), l_sem.at[ch]).start()

    def line(ch):
        for far in far_z:
            drain(ch, z_sem.at[ch, far])
            from_s = far * 2 + core
            src = place(ch, g, from_s)
            if chunks[ch][3]:
                send(ch, src, g, from_s, x_sem.at[ch, far], x_next)
                for peer in y_next:
                    send(ch, src, g, from_s, y_sem.at[ch, gy, far], peer)
            send(ch, src, g, from_s, p_sem.at[ch, 0], partner)

    def side(ch):
        if not chunks[ch][3]:
            return
        for far in range(z_n):
            from_s = far * 2 + core
            drain(ch, x_sem.at[ch, far])
            src = place(ch, other_x, from_s)
            if far % 2 == 0:
                for peer in y_next:
                    send(ch, src, other_x, from_s, d_sem.at[ch, gy, far], peer)
            send(ch, src, other_x, from_s, p_sem.at[ch, 1], partner)
            for y in far_y:
                drain(ch, y_sem.at[ch, y, far])
                from_g = y * 2 + gx
                src = place(ch, from_g, from_s)
                if far % 2 == 1:
                    send(ch, src, from_g, from_s, d_sem.at[ch, y, far], x_next)
                send(ch, src, from_g, from_s, p_sem.at[ch, 2], partner)

    def corner(ch):
        if not chunks[ch][3]:
            return
        for far in range(z_n):
            from_s = far * 2 + core
            for y in far_y:
                drain(ch, d_sem.at[ch, y, far])
                from_g = y * 2 + 1 - gx
                src = place(ch, from_g, from_s)
                send(ch, src, from_g, from_s, p_sem.at[ch, 3], partner)

    def ready(ch, kinds=range(4)):
        for kind in kinds if chunks[ch][3] else (0,):
            drain(ch, p_sem.at[ch, kind], z_n * (y_n - 1 if kind >= 2 else 1))
            if kind == 0:
                drain(ch, l_sem.at[ch])

    def finish(ch):
        sends = 2 * z_n - 1
        if chunks[ch][3]:
            sends += z_n * y_n
            sends += z_n * (y_n - 1)
            sends += z_n * (2 * y_n - 1)
        drain(ch, s_sem.at[ch], sends)

    steps = (own, line, side, corner)

    def tick(t):
        for lag, step in enumerate(steps):
            if 0 <= t - lag < len(chunks):
                step(t - lag)

    return enter, tick, ready, finish


def gather_plan(groups, shards, splits):
    grp_n, seq_n = groups
    chunks, shapes = [], []
    for i, (rows, cols, full) in enumerate(shards):
        part = rows // splits[i]
        chunks += [(i, j * part, part, full) for j in range(splits[i])]
        total = (grp_n if full else 1) * seq_n * rows
        shapes.append(jax.ShapeDtypeStruct((total, cols), jnp.bfloat16))
    dma, count = pltpu.SemaphoreType.DMA, len(chunks)
    sems = [
        dma((count, seq_n // 2)),
        dma((count, seq_n // 2)),
        dma((count, grp_n // 2, seq_n // 2)),
        dma((count, grp_n // 2, seq_n // 2)),
        dma((count, 4)),
        dma((count,)),
        dma((count,)),
    ]
    return [rows for rows, _, _ in shards], chunks, shapes, sems


def dot_nt(left, right):
    return lax.dot_general(
        left, right, (((1,), (1,)), ((), ())), preferred_element_type=jnp.float32
    )


def dot_nn(left, right):
    return lax.dot_general(
        left, right, (((1,), (0,)), ((), ())), preferred_element_type=jnp.float32
    )


def stacked_heads(pair):
    first = lax.broadcasted_iota(jnp.int32, pair.shape, 1) < HEAD_DIM
    zero = jnp.zeros_like(pair)
    return jnp.concatenate([jnp.where(first, pair, zero), jnp.where(first, zero, pair)], 0)


def row_groups(prompt_rows, prompt_total, later_rows):
    block = min(256, later_rows)
    return [(prompt_rows + i, block, prompt_total + i) for i in range(0, later_rows, block)]


def attention_forward(sizes, q_ref, k_ref, v_ref, ctx_ref, lse_ref, wide_ref):
    prompt_rows, prompt_total, later_rows = sizes
    seq = lax.axis_index("seq")
    wide_ref[:, :128] = v_ref[...]
    wide_ref[:, 128:] = jnp.ones((prompt_total + later_rows, 128), jnp.bfloat16)

    def finish(start, rows, row_max, summed):
        total = summed[:, 128:]
        mixed = summed[:, :128] / total
        log_total = row_max * SCALE2 + jnp.log2(total)
        first = lax.broadcasted_iota(jnp.int32, (rows, 128), 1) < HEAD_DIM
        ctx_ref[start : start + rows] = jnp.where(first, mixed[:rows], mixed[rows:]).astype(
            jnp.bfloat16
        )
        lse_ref[start : start + rows] = jnp.where(first, log_total[:rows], log_total[rows:])

    for start, rows, free in row_groups(prompt_rows, prompt_total, later_rows):
        queries = stacked_heads(q_ref[start : start + rows])
        open_scores = dot_nt(queries, k_ref[:free])
        edge_scores = dot_nt(queries, k_ref[free : free + rows])
        row = lax.broadcasted_iota(jnp.int32, (rows, rows), 0)
        key = lax.broadcasted_iota(jnp.int32, (rows, rows), 1)
        seen = key <= row
        edge_scores = jnp.where(jnp.concatenate([seen, seen], 0), edge_scores, NEGATIVE)
        row_max = jnp.maximum(
            jnp.max(open_scores, 1, keepdims=True), jnp.max(edge_scores, 1, keepdims=True)
        )
        scaled = row_max * SCALE2
        open_p = jnp.exp2(open_scores * SCALE2 - scaled).astype(jnp.bfloat16)
        edge_p = jnp.exp2(edge_scores * SCALE2 - scaled).astype(jnp.bfloat16)
        summed = dot_nn(open_p, wide_ref[:free]) + dot_nn(edge_p, wide_ref[free : free + rows])
        finish(start, rows, row_max, summed)
    scores = dot_nt(stacked_heads(q_ref[:prompt_rows]), k_ref[:prompt_total])
    row = lax.broadcasted_iota(jnp.int32, (prompt_rows, prompt_total), 0)
    key = lax.broadcasted_iota(jnp.int32, (prompt_rows, prompt_total), 1)
    seen = key <= row + seq * prompt_rows
    scores = jnp.where(jnp.concatenate([seen, seen], 0), scores, NEGATIVE)
    row_max = jnp.max(scores, 1, keepdims=True)
    p = jnp.exp2(scores * SCALE2 - row_max * SCALE2).astype(jnp.bfloat16)
    finish(0, prompt_rows, row_max, dot_nn(p, wide_ref[:prompt_total]))


def attention_backward(
    sizes, q_ref, k_ref, v_ref, d_ref, ctx_ref, lse_ref, dq_ref, dk_ref, dv_ref, k_sum, v_sum
):
    prompt_rows, prompt_total, later_rows = sizes
    seq = lax.axis_index("seq")
    keys_t = k_ref[...].astype(jnp.float32).T.astype(jnp.bfloat16)
    lse_t = lse_ref[...].T
    weighed_t = (d_ref[...].astype(jnp.float32) * ctx_ref[...].astype(jnp.float32)).T
    deltas = [
        jnp.sum(weighed_t[:HEAD_DIM], 0, keepdims=True),
        jnp.sum(weighed_t[HEAD_DIM:], 0, keepdims=True),
    ]
    totals = [lse_t[0:1], lse_t[HEAD_DIM : HEAD_DIM + 1]]

    def group(start, rows, count, mask):
        queries = stacked_heads(q_ref[start : start + rows])
        grads = stacked_heads(d_ref[start : start + rows])
        total = jnp.concatenate([t[:, start : start + rows] for t in totals], 1)
        delta = jnp.concatenate([t[:, start : start + rows] for t in deltas], 1)
        p = mask(jnp.exp2(dot_nt(k_ref[:count], queries) * SCALE2 - total))
        d_scores = (p * (dot_nt(v_ref[:count], grads) - delta)).astype(jnp.bfloat16)
        dq_t = dot_nn(keys_t[:, :count], d_scores)
        first = lax.broadcasted_iota(jnp.int32, (128, rows), 0) < HEAD_DIM
        dq = jnp.where(first, dq_t[:, :rows], dq_t[:, rows:]).T * 0.125
        dq_ref[start : start + rows] = dq.astype(jnp.bfloat16)
        return dot_nn(d_scores, queries), dot_nn(p.astype(jnp.bfloat16), grads)

    def causal(free, rows):
        def mask(p):
            key = lax.broadcasted_iota(jnp.int32, (rows, rows), 0)
            row = lax.broadcasted_iota(jnp.int32, (rows, rows), 1)
            seen = key <= row
            edge = jnp.where(jnp.concatenate([seen, seen], 1), p[free:], 0.0)
            return jnp.concatenate([p[:free], edge], 0)

        return mask

    def prompt_mask(p):
        key = lax.broadcasted_iota(jnp.int32, (prompt_total, prompt_rows), 0)
        row = lax.broadcasted_iota(jnp.int32, (prompt_total, prompt_rows), 1)
        seen = key <= row + seq * prompt_rows
        return jnp.where(jnp.concatenate([seen, seen], 1), p, 0.0)

    groups = row_groups(prompt_rows, prompt_total, later_rows)
    start, rows, free = groups[-1]
    k_sum[...], v_sum[...] = group(start, rows, free + rows, causal(free, rows))
    for start, rows, free in groups[:-1]:
        d_keys, d_values = group(start, rows, free + rows, causal(free, rows))
        k_sum[: free + rows] += d_keys
        v_sum[: free + rows] += d_values
    d_keys, d_values = group(0, prompt_rows, prompt_total, prompt_mask)
    k_sum[:prompt_total] += d_keys
    v_sum[:prompt_total] += d_values
    dk_ref[...] = (k_sum[...] * 0.125).astype(jnp.bfloat16)
    dv_ref[...] = v_sum[...].astype(jnp.bfloat16)


UP_SECTIONS = (3 * MODEL_WIDTH, MODEL_WIDTH, HIDDEN_UNITS, MODEL_WIDTH)
UP_STARTS = (0, 768, 1024, 2048)
UP_FIRST = (0, 3 * MODEL_WIDTH, 4 * MODEL_WIDTH, 4 * MODEL_WIDTH + HIDDEN_UNITS)
QUARTER = (3 * MODEL_WIDTH + HIDDEN_UNITS) // 4
UP_QUARTER = sum(UP_SECTIONS) // 4
EARLY_COLS = QUARTER + UP_QUARTER - UP_STARTS[1]
TILE = 256


def for_blocks(count, body):
    def step(i, carry):
        body(pl.multiple_of(i * 128, 128))
        return carry

    lax.fori_loop(0, count // 128, step, 0)


def centre(values):
    centred = values - jnp.mean(values, axis=1, keepdims=True)
    var = jnp.mean(centred * centred, axis=1, keepdims=True)
    return centred, lax.rsqrt(var + EPSILON)


def normalize_rows(read, write, count, gain, shift):
    def body(start):
        centred, scale = centre(read(start))
        write(start, (centred * scale * gain + shift).astype(jnp.bfloat16))

    for_blocks(count, body)


def norm_pull(values, grads, gain):
    centred, scale = centre(values)
    unit = centred * scale
    grads = grads * gain
    along = jnp.mean(grads * unit, axis=1, keepdims=True)
    return scale * (grads - jnp.mean(grads, axis=1, keepdims=True) - unit * along)


def gelu_both(field):
    square = field * field
    bent = jnp.tanh(0.7978845608028654 * (field + 0.044715 * square * field))
    half = 0.5 * (1.0 + bent)
    slope = 0.7978845608028654 * (1.0 + 3.0 * 0.044715 * square)
    return field * half, half + 0.5 * field * (1.0 - bent * bent) * slope


def quarter_rows(rows, offset, part, across):
    rank = lax.broadcasted_iota(jnp.int32, (ADAPTER_RANK, rows), 0)
    row = lax.broadcasted_iota(jnp.int32, (ADAPTER_RANK, rows), 1)
    if across:
        rank = lax.broadcasted_iota(jnp.int32, (rows, ADAPTER_RANK), 1)
        row = lax.broadcasted_iota(jnp.int32, (rows, ADAPTER_RANK), 0)
    return (row == offset + (rank // 4) * 16 + (rank % 4) * 4 + part).astype(jnp.bfloat16)


def forward_and_gather(groups, ident, tokens, cotangent, gains, biases, shards, collective_id):
    rows = tokens.shape[0]
    prompt_rows = rows - CONT_LEN
    prompt_total = prompt_rows * groups[1]
    keys = prompt_total + CONT_LEN
    sizes = (prompt_rows, prompt_total, CONT_LEN)
    width, hidden_units = MODEL_WIDTH, HIDDEN_UNITS
    pairs = width // 128
    plan = [(prompt_rows, width, False)] + [(a.shape[0], a.shape[1], True) for a in shards]
    splits = [1, 1, 1, 2, 1, 2, 2]
    lengths, chunks, gathered, sems = gather_plan(groups, plan, splits)
    count = len(plan)
    dma = pltpu.SemaphoreType.DMA
    bf, f32 = jnp.bfloat16, jnp.float32

    def kernel(id_ref, tokens_ref, cot_ref, gains_ref, bias_ref, *refs):
        ins = (tokens_ref,) + refs[: count - 1]
        refs = refs[count - 1 :]
        q_out, kv_out, ctx_out, lse_out, act_out, dh_out, dc_out = refs[:7]
        early_out, inner_out, down_out, up_out = refs[7:11]
        outs, refs = refs[11 : 11 + count], refs[11 + count :]
        (
            prompt_v,
            norm_v,
            weight_v,
            w_out_v,
            q_v,
            kv_v,
            wide_v,
            ctx_v,
            lse_v,
            h_v,
            n_v,
            gl_v,
            gp_v,
            dn_v,
            downs_v,
            ups_v,
            down_v,
            up_v,
            low_v,
            turned_v,
            d_low,
            d_turned,
            acc_low,
            acc_turned,
            down_e,
            up_e,
            in_sem,
            out_sem,
        ) = refs[:28]
        enter, tick, ready, finish = gather_stages(groups, lengths, chunks, ins, outs, refs[28:])
        adapter = id_ref[0, 0]
        seq = lax.axis_index("seq")
        grp = lax.axis_index("grp")

        def load(src, dst, sem):
            copy = pltpu.make_async_copy(src, dst, in_sem.at[sem])
            copy.start()
            return copy

        stores, store_sem = [], iter(range(8))

        def store(src, dst):
            copy = pltpu.make_async_copy(src, dst, out_sem.at[next(store_sem)])
            copy.start()
            stores.append(copy)
            return copy

        def settle(copy):
            copy.wait()
            stores[:] = [other for other in stores if other is not copy]

        def bias(start, size):
            return bias_ref[:, pl.ds(pl.multiple_of(start, 128), size)]

        def tile(i, size=TILE, first=0):
            return pl.ds(pl.multiple_of(i * size + first, 128), size)

        def read_tokens(start):
            at = pl.multiple_of(start + prompt_rows, 128)
            return tokens_ref[pl.ds(at, 128)].astype(f32)

        def write_later(start, values):
            norm_v[pl.ds(pl.multiple_of(start + prompt_total, 128), 128)] = values

        def read_prompt(start):
            return prompt_v[pl.ds(start, 128)].astype(f32)

        def write_prompt(start, values):
            norm_v[pl.ds(start, 128)] = values

        def read_hidden(start):
            return h_v[pl.ds(start, 128)]

        def write_hidden(start, values):
            n_v[pl.ds(start, 128)] = values

        def inner(which, values, down):
            low_v[which] = dot_nt(values, down).astype(bf)
            turned_v[which] = dot_nt(down, values).astype(bf)

        def d_inner(which, values, up):
            d_low[which] = dot_nt(values, up).astype(bf)
            d_turned[which] = dot_nt(up, values).astype(bf)

        enter()
        tick(0)
        shift_one = bias_ref[:, :width]
        normalize_rows(read_tokens, write_later, CONT_LEN, gains_ref[0:1], shift_one)
        tick(1)
        ready(0)
        load(outs[0], prompt_v, 0).wait()
        normalize_rows(read_prompt, write_prompt, prompt_total, gains_ref[0:1], shift_one)
        tick(2)
        tick(3)
        tick(4)
        ready(1)
        copy_down = load(outs[1], downs_v, 1)
        tick(5)
        ready(2)
        copy_up = load(outs[2], ups_v, 2)
        copy_down.wait()
        copy_up.wait()
        at = lax.broadcasted_iota(jnp.int32, (ADAPTER_RANK, downs_v.shape[0]), 1)
        rank = lax.broadcasted_iota(jnp.int32, (ADAPTER_RANK, downs_v.shape[0]), 0)
        for part in range(4):
            chosen = (at == rank + (adapter * 64 + part * 16)).astype(bf)
            down_v[:, part * QUARTER : (part + 1) * QUARTER] = dot_nn(chosen, downs_v[...]).astype(
                bf
            )
            chosen = quarter_rows(ups_v.shape[0], adapter * 64, part, False)
            for first, start, size in zip(UP_FIRST, UP_STARTS, UP_SECTIONS):
                size //= 4
                up_v[:, first + part * size : first + (part + 1) * size] = dot_nn(
                    chosen, ups_v[:, start : start + size]
                ).astype(bf)
        down_out[...] = down_v[:, :width]
        up_out[...] = up_v[:, : 3 * width]
        inner(0, norm_v[prompt_total:], down_v[:, :width])
        inner_out[...] = turned_v[0]
        d_inner(3, cot_ref[prompt_rows:], up_v[:, UP_FIRST[3] :])
        tick(6)
        tick(7)
        ready(3)
        ready(4)
        load(outs[3], weight_v.at[:, : 3 * width], 3).wait()

        def later_tile(i):
            weight = weight_v[:, tile(i)]
            later = dot_nn(norm_v[prompt_total:], weight) + dot_nn(low_v[0], up_v[:, tile(i)])
            return weight, later

        def key_tile(i, carry):
            weight, later = later_tile(i)
            shift = jnp.where(i >= 8, bias(i * TILE + width, TILE), 0.0)
            to = tile(i - 4)
            kv_v[prompt_total:, to] = (later + shift).astype(bf)
            early = dot_nn(norm_v[:prompt_total], weight)
            kv_v[:prompt_total, to] = (early + shift).astype(bf)
            return carry

        def query_tile(i, carry):
            weight, later = later_tile(i)
            shift = bias(i * TILE + 2 * width, TILE)
            q_v[prompt_rows:, tile(i)] = (later + shift).astype(bf)
            mine = norm_v[pl.ds(pl.multiple_of(seq * prompt_rows, 128), prompt_rows)]
            q_v[:prompt_rows, tile(i)] = (dot_nn(mine, weight) + shift).astype(bf)
            return carry

        lax.fori_loop(4, 12, key_tile, 0)
        kv_store = store(kv_v, kv_out)
        tick(8)
        ready(5)
        load_out = load(outs[4], w_out_v, 4)
        lax.fori_loop(0, 4, query_tile, 0)
        q_store = store(q_v, q_out)

        def attend(i, carry):
            cols = pl.ds(pl.multiple_of(i * 128, 128), 128)
            values = pl.ds(pl.multiple_of(i * 128 + width, 128), 128)

            @pl.when(i == pairs // 2)
            def _():
                tick(9)

            attention_forward(
                sizes,
                q_v.at[:, cols],
                kv_v.at[:, cols],
                kv_v.at[:, values],
                ctx_v.at[:, cols],
                lse_v.at[:, cols],
                wide_v,
            )
            return carry

        lax.fori_loop(0, pairs, attend, 0)
        store(ctx_v, ctx_out)
        lse_store = store(lse_v, lse_out)
        tick(10)
        ready(6)
        ready(7)
        load_fc = load(outs[5], weight_v, 5)
        load_out.wait()
        inner(1, ctx_v[prompt_rows:], down_v[:, width : 2 * width])

        def out_tile(j, carry):
            cols = tile(j)
            mixed = dot_nn(ctx_v[...], w_out_v[:, cols]) + bias(j * TILE + 4 * width, TILE)
            mixed = tokens_ref[:, cols].astype(f32) + mixed
            extra = dot_nn(low_v[1], up_v[:, tile(j, first=UP_FIRST[1])])
            h_v[:prompt_rows, cols] = mixed[:prompt_rows]
            h_v[prompt_rows:, cols] = mixed[prompt_rows:] + extra
            return carry

        lax.fori_loop(0, 4, out_tile, 0)
        normalize_rows(
            read_hidden, write_hidden, rows, gains_ref[1:2], bias_ref[:, width : 2 * width]
        )
        inner(2, n_v[prompt_rows:], down_v[:, 2 * width : 3 * width])
        settle(lse_store)
        sum_v = lse_v

        def start_sums(start):
            at = pl.ds(start, 128)
            sum_v[at] = h_v[at] + bias_ref[:, 5 * width : 6 * width]
            dn_v[at] = jnp.zeros((128, width), f32)

        for_blocks(rows, start_sums)
        load_fc.wait()

        tiles = hidden_units // TILE

        def hidden_tile(i, carry):
            cols = tile(i)

            @pl.when(i == tiles // 2)
            def _():
                tick(11)

            wide = dot_nn(n_v[...], weight_v[:, cols]) + bias(i * TILE + 6 * width, TILE)
            extra = dot_nn(low_v[2], up_v[:, tile(i, first=UP_FIRST[2])])
            for at, field in (
                (slice(0, prompt_rows), wide[:prompt_rows]),
                (slice(prompt_rows, rows), wide[prompt_rows:] + extra),
            ):
                value, slope = gelu_both(field)
                gl_v[at, cols] = value.astype(bf)
                gp_v[at, cols] = slope.astype(bf)
            return carry

        lax.fori_loop(0, tiles, hidden_tile, 0)
        settle(kv_store)
        tick(12)

        df_v = norm_v.at[:rows]
        part_rows = hidden_units // 4
        for which in range(2):
            acc_low[which] = jnp.zeros((CONT_LEN, ADAPTER_RANK), f32)
            acc_turned[which] = jnp.zeros((ADAPTER_RANK, CONT_LEN), f32)
        gx, gy = lax.rem(grp, 2), grp // 2
        order = [grp, gy * 2 + 1 - gx, (1 - gy) * 2 + gx, (1 - gy) * 2 + 1 - gx]
        for kind, unit in enumerate(order):
            ready(8, (kind,))
            ready(9, (kind,))
            base = pl.multiple_of(unit * part_rows, part_rows)
            part = pl.ds(base, part_rows)
            down_part = pl.ds(pl.multiple_of(base + 3 * width, width), part_rows)
            up_part = pl.ds(pl.multiple_of(base + UP_FIRST[2], width), part_rows)
            slot = kv_v.at[:part_rows, (kind % 2) * width : (kind % 2 + 1) * width]
            load(outs[6].at[part], slot, 6 + kind % 2).wait()

            def d_hidden(j, carry, base=base, slot=slot):
                cols = tile(j, first=base)
                wide = dot_nt(cot_ref[...], slot[tile(j)])
                extra = dot_nn(d_low[3], down_v[:, tile(j, first=base + 3 * width)])
                slope = gp_v[:, cols].astype(f32)
                to = tile(j)
                df_v[:prompt_rows, to] = (wide[:prompt_rows] * slope[:prompt_rows]).astype(bf)
                later = (wide[prompt_rows:] + extra) * slope[prompt_rows:]
                df_v[prompt_rows:, to] = later.astype(bf)
                return carry

            lax.fori_loop(0, part_rows // TILE, d_hidden, 0)
            df_later = df_v[prompt_rows:]
            gl_later = gl_v[prompt_rows:, part]
            acc_low[0] += dot_nt(df_later, up_v[:, up_part])
            acc_turned[0] += dot_nt(up_v[:, up_part], df_later)
            acc_low[1] += dot_nt(gl_later, down_v[:, down_part])
            acc_turned[1] += dot_nt(down_v[:, down_part], gl_later)
            down_e[:, down_part] = dot_nn(d_turned[3], gl_later).astype(bf)
            up_e[:, up_part] = dot_nn(turned_v[2], df_later).astype(bf)

            def sums(j, carry, part=part, slot=slot):
                cols = tile(j)
                sum_v[:, cols] += dot_nn(gl_v[:, part], slot[:, cols])
                dn_v[:, cols] += dot_nt(df_v[...], weight_v[cols, part])
                return carry

            lax.fori_loop(0, width // TILE, sums, 0)

        d_low[2] = acc_low[0].astype(bf)
        d_turned[2] = acc_turned[0].astype(bf)
        low_v[3] = acc_low[1].astype(bf)
        turned_v[3] = acc_turned[1].astype(bf)
        act_v, attn_v, dc_v = prompt_v.at[:rows], q_v, norm_v.at[:rows]

        def last_tile(j, carry):
            cols = tile(j)
            dn_v[prompt_rows:, cols] += dot_nn(d_low[2], down_v[:, tile(j, first=2 * width)])
            act_v[:prompt_rows, cols] = sum_v[:prompt_rows, cols].astype(bf)
            extra = dot_nn(low_v[3], up_v[:, tile(j, first=UP_FIRST[3])])
            act_v[prompt_rows:, cols] = (sum_v[prompt_rows:, cols] + extra).astype(bf)
            return carry

        lax.fori_loop(0, width // TILE, last_tile, 0)
        store(act_v, act_out)
        settle(q_store)

        def pull_rows(start):
            at = pl.ds(start, 128)
            grads = cot_ref[at].astype(f32) + norm_pull(h_v[at], dn_v[at], gains_ref[1:2])
            dn_v[at] = grads
            attn_v[at] = grads.astype(bf)

        for_blocks(rows, pull_rows)
        store(dn_v, dh_out)
        d_inner(1, attn_v[prompt_rows:], up_v[:, UP_FIRST[1] : UP_FIRST[2]])

        def context_tile(j, carry):
            cols = tile(j)
            wide = dot_nt(attn_v[...], w_out_v[cols])
            extra = dot_nn(d_low[1], down_v[:, tile(j, first=width)])
            dc_v[:prompt_rows, cols] = wide[:prompt_rows].astype(bf)
            dc_v[prompt_rows:, cols] = (wide[prompt_rows:] + extra).astype(bf)
            return carry

        lax.fori_loop(0, width // TILE, context_tile, 0)
        store(dc_v, dc_out)
        down_e[:, :width] = jnp.zeros((ADAPTER_RANK, width), bf)
        down_e[:, width : 2 * width] = dot_nn(d_turned[1], ctx_v[prompt_rows:]).astype(bf)
        down_e[:, 2 * width : 3 * width] = dot_nn(d_turned[2], n_v[prompt_rows:]).astype(bf)
        up_e[:, UP_FIRST[1] : UP_FIRST[2]] = dot_nn(turned_v[1], attn_v[prompt_rows:]).astype(bf)
        up_e[:, UP_FIRST[3] :] = dot_nn(turned_v[3], cot_ref[prompt_rows:]).astype(bf)
        for quarter in range(4):
            early_out[quarter, :, :QUARTER] = down_e[:, quarter * QUARTER : (quarter + 1) * QUARTER]
        for section in range(1, 4):
            size = UP_SECTIONS[section] // 4
            moved = jnp.zeros((64, size), f32)
            for part in range(4):
                first = UP_FIRST[section] + part * size
                moved += dot_nn(quarter_rows(64, 0, part, True), up_e[:, first : first + size])
            first = QUARTER + UP_STARTS[section] - UP_STARTS[1]
            for quarter in range(4):
                early_out[quarter, :, first : first + size] = moved[
                    16 * quarter : 16 * quarter + 16
                ].astype(bf)
        for ch in range(len(chunks)):
            finish(ch)
        for copy in stores:
            copy.wait()

    vmem = pl.BlockSpec(memory_space=pltpu.VMEM)
    hbm = pl.BlockSpec(memory_space=pl.ANY)
    return pl.pallas_call(
        kernel,
        in_specs=[pl.BlockSpec(memory_space=pltpu.SMEM)] + [vmem] * (3 + count),
        out_specs=[hbm] * 7 + [vmem] * 4 + [hbm] * count,
        out_shape=[
            jax.ShapeDtypeStruct((rows, width), bf),
            jax.ShapeDtypeStruct((keys, 2 * width), bf),
            jax.ShapeDtypeStruct((rows, width), bf),
            jax.ShapeDtypeStruct((rows, width), f32),
            jax.ShapeDtypeStruct((rows, width), bf),
            jax.ShapeDtypeStruct((rows, width), f32),
            jax.ShapeDtypeStruct((rows, width), bf),
            jax.ShapeDtypeStruct((4, 16, EARLY_COLS), bf),
            jax.ShapeDtypeStruct((ADAPTER_RANK, CONT_LEN), bf),
            jax.ShapeDtypeStruct((ADAPTER_RANK, width), bf),
            jax.ShapeDtypeStruct((ADAPTER_RANK, 3 * width), bf),
        ]
        + gathered,
        scratch_shapes=[
            pltpu.VMEM((prompt_total, width), bf),
            pltpu.VMEM((keys, width), bf),
            pltpu.VMEM((width, hidden_units), bf),
            pltpu.VMEM((width, width), bf),
            pltpu.VMEM((rows, width), bf),
            pltpu.VMEM((keys, 2 * width), bf),
            pltpu.VMEM((keys, 256), bf),
            pltpu.VMEM((rows, width), bf),
            pltpu.VMEM((rows, width), f32),
            pltpu.VMEM((rows, width), f32),
            pltpu.VMEM((rows, width), bf),
            pltpu.VMEM((rows, hidden_units), bf),
            pltpu.VMEM((rows, hidden_units), bf),
            pltpu.VMEM((rows, width), f32),
            pltpu.VMEM(gathered[1].shape, bf),
            pltpu.VMEM(gathered[2].shape, bf),
            pltpu.VMEM((ADAPTER_RANK, 4 * QUARTER), bf),
            pltpu.VMEM((ADAPTER_RANK, 4 * UP_QUARTER), bf),
            pltpu.VMEM((4, CONT_LEN, ADAPTER_RANK), bf),
            pltpu.VMEM((4, ADAPTER_RANK, CONT_LEN), bf),
            pltpu.VMEM((4, CONT_LEN, ADAPTER_RANK), bf),
            pltpu.VMEM((4, ADAPTER_RANK, CONT_LEN), bf),
            pltpu.VMEM((2, CONT_LEN, ADAPTER_RANK), f32),
            pltpu.VMEM((2, ADAPTER_RANK, CONT_LEN), f32),
            pltpu.VMEM((ADAPTER_RANK, 4 * QUARTER), bf),
            pltpu.VMEM((ADAPTER_RANK, 4 * UP_QUARTER), bf),
            dma((8,)),
            dma((8,)),
        ]
        + sems,
        compiler_params=pltpu.CompilerParams(
            collective_id=collective_id, has_side_effects=True, vmem_limit_bytes=VMEM_LIMIT
        ),
    )(ident, tokens, cotangent, gains, biases, *shards)


def adapter_scratch(cols):
    dma = pltpu.SemaphoreType.DMA
    return [
        pltpu.VMEM((2, 16, cols), jnp.bfloat16),
        pltpu.VMEM((16, 128), jnp.bfloat16),
        pltpu.VMEM((3, 4, 16, cols), jnp.bfloat16),
        pltpu.VMEM((3, 4, 16, cols), jnp.bfloat16),
        pltpu.VMEM((4, 16, cols), jnp.float32),
        pltpu.VMEM((3, 16, cols), jnp.bfloat16),
        pltpu.VMEM((3, 16, cols), jnp.bfloat16),
        dma((3,)),
        dma((3,)),
        dma((3,)),
        dma((3,)),
        dma((3,)),
        dma((3,)),
    ]


def adapter_stages(term_ref, id_ref, out_ref, scratch):
    from_core, other_id, to_grp, from_grp, total, to_z, from_z = scratch[:7]
    a_send, a_recv, g_send, g_recv, z_send, z_recv = scratch[7:]
    g, s = lax.axis_index("grp"), lax.axis_index("seq")
    core, z = lax.rem(s, 2), s // 2
    other = 1 - core
    partner = (g, z * 2 + other)
    grps = [lax.rem(g + d, 4) for d in range(1, 4)]
    lines = [lax.rem(z + d, 4) for d in range(1, 4)]

    def enter():
        peers = [partner] + [(far, s) for far in grps] + [(g, far * 2 + core) for far in lines]
        barrier = pltpu.get_barrier_semaphore()
        for peer in peers:
            pl.semaphore_signal(barrier, inc=1, device_id=peer, device_id_type=MESH)
        pl.semaphore_wait(barrier, len(peers))

    def remote(src, dst, send_sem, recv_sem, device):
        return pltpu.make_async_remote_copy(
            src_ref=src,
            dst_ref=dst,
            send_sem=send_sem,
            recv_sem=recv_sem,
            device_id=device,
            device_id_type=MESH,
        )

    copies_a = [
        remote(term_ref.at[i * 2 + other], from_core.at[i], a_send.at[i], a_recv.at[i], partner)
        for i in range(2)
    ] + [remote(id_ref, other_id, a_send.at[2], a_recv.at[2], partner)]
    copies_g = [
        remote(to_grp.at[d], from_grp.at[d], g_send.at[d], g_recv.at[d], (grps[d], s))
        for d in range(3)
    ]
    copies_z = [
        remote(to_z.at[d], from_z.at[d], z_send.at[d], z_recv.at[d], (g, lines[d] * 2 + core))
        for d in range(3)
    ]

    def start(copies):
        for copy in copies:
            copy.start()

    def wait(copies):
        for copy in copies:
            copy.wait()

    def select():
        wait(copies_a)
        mine = id_ref[0:1, 0:1].astype(jnp.float32)
        theirs = other_id[0:1, 0:1].astype(jnp.float32)
        for d, grp in enumerate(grps + [g]):
            for slot in range(4):
                adapter = (grp * 2 + slot // 2).astype(jnp.float32)
                own_term = term_ref[(slot % 2) * 2 + core].astype(jnp.float32)
                other_term = from_core[slot % 2].astype(jnp.float32)
                picked = jnp.where(mine == adapter, own_term, 0.0) + jnp.where(
                    theirs == adapter, other_term, 0.0
                )
                if d < 3:
                    to_grp[d, slot] = picked.astype(jnp.bfloat16)
                else:
                    total[slot] = picked

    def add_grps():
        wait(copies_g)
        for slot in range(4):
            total[slot] += sum(from_grp[d, slot].astype(jnp.float32) for d in range(3))
        for d in range(3):
            to_z[d] = total[lines[d]].astype(jnp.bfloat16)

    def add_lines():
        wait(copies_z)
        out_ref[...] = total[z] + sum(from_z[d].astype(jnp.float32) for d in range(3))

    return (
        enter,
        lambda: start(copies_a),
        select,
        lambda: start(copies_g),
        add_grps,
        lambda: start(copies_z),
        add_lines,
    )


def attend_back_and_reduce(q, kv, d_ctx, ctx, lse, term, ident, collective_id):
    rows, keys, pairs = q.shape[0], kv.shape[0], q.shape[1] // 128
    sizes = (rows - CONT_LEN, keys - CONT_LEN, CONT_LEN)
    term_cols = term.shape[2]

    def kernel(q_ref, k_ref, v_ref, d_ref, ctx_ref, lse_ref, term_ref, id_ref, *refs):
        dq_ref, dk_ref, dv_ref, out_ref, k_sum, v_sum = refs[:6]
        enter, send_core, select, send_grp, add_grps, send_z, add_lines = adapter_stages(
            term_ref, id_ref, out_ref, refs[6:]
        )
        step = pl.program_id(0)

        @pl.when(step == 0)
        def _():
            enter()
            send_core()

        attention_backward(
            sizes,
            q_ref,
            k_ref,
            v_ref,
            d_ref,
            ctx_ref,
            lse_ref,
            dq_ref,
            dk_ref,
            dv_ref,
            k_sum,
            v_sum,
        )

        @pl.when(step == 0)
        def _():
            select()
            send_grp()

        @pl.when(step == pairs - 4)
        def _():
            add_grps()
            send_z()

        @pl.when(step == pairs - 1)
        def _():
            add_lines()

    def pair(i):
        return (0, i)

    row_spec = pl.BlockSpec((rows, 128), pair)
    key_spec = pl.BlockSpec((keys, 128), pair)
    whole = pl.BlockSpec(memory_space=pltpu.VMEM)
    return pl.pallas_call(
        kernel,
        grid=(pairs,),
        in_specs=[
            row_spec,
            key_spec,
            pl.BlockSpec((keys, 128), lambda i: (0, pairs + i)),
            row_spec,
            row_spec,
            row_spec,
            whole,
            whole,
        ],
        out_specs=[row_spec, key_spec, key_spec, whole],
        out_shape=[
            jax.ShapeDtypeStruct(q.shape, jnp.bfloat16),
            jax.ShapeDtypeStruct((keys, q.shape[1]), jnp.bfloat16),
            jax.ShapeDtypeStruct((keys, q.shape[1]), jnp.bfloat16),
            jax.ShapeDtypeStruct((16, term_cols), jnp.float32),
        ],
        scratch_shapes=[pltpu.VMEM((keys, 128), jnp.float32)] * 2 + adapter_scratch(term_cols),
        compiler_params=pltpu.CompilerParams(
            collective_id=collective_id, has_side_effects=True, vmem_limit_bytes=VMEM_LIMIT
        ),
    )(q, kv, kv, d_ctx, ctx, lse, term, ident)


def last_exchange(rows_term, term, ident, collective_id):
    blocks, cols = rows_term.shape[0], rows_term.shape[3]
    rows = rows_term.shape[2]
    term_cols = term.shape[2]
    dma = pltpu.SemaphoreType.DMA

    def kernel(x_ref, term_ref, id_ref, sum_ref, out_ref, pair_in, to_line, from_line, *refs):
        p_send, p_recv, l_send, l_recv = refs[:4]
        enter, send_core, select, send_grp, add_grps, send_z, add_lines = adapter_stages(
            term_ref, id_ref, out_ref, refs[4:]
        )
        g, s = lax.axis_index("grp"), lax.axis_index("seq")
        core, z = lax.rem(s, 2), s // 2
        far_z = [lax.rem(z + d, blocks) for d in range(1, blocks)]
        across = pltpu.make_async_remote_copy(
            src_ref=x_ref.at[:, 1 - core],
            dst_ref=pair_in,
            send_sem=p_send,
            recv_sem=p_recv,
            device_id=(g, z * 2 + 1 - core),
            device_id_type=MESH,
        )
        along = [
            pltpu.make_async_remote_copy(
                src_ref=to_line.at[d],
                dst_ref=from_line.at[d],
                send_sem=l_send.at[d],
                recv_sem=l_recv.at[d],
                device_id=(g, far * 2 + core),
                device_id_type=MESH,
            )
            for d, far in enumerate(far_z)
        ]
        enter()
        send_core()
        across.start()
        select()
        send_grp()
        across.wait()
        for d, far in enumerate(far_z):
            both = x_ref[far, core].astype(jnp.float32) + pair_in[far].astype(jnp.float32)
            to_line[d] = both.astype(jnp.bfloat16)
            along[d].start()
        add_grps()
        send_z()
        total = x_ref[z, core].astype(jnp.float32) + pair_in[z].astype(jnp.float32)
        for d, copy in enumerate(along):
            copy.wait()
            total = total + from_line[d].astype(jnp.float32)
        sum_ref[...] = total
        add_lines()

    whole = pl.BlockSpec(memory_space=pltpu.VMEM)
    return pl.pallas_call(
        kernel,
        in_specs=[whole] * 3,
        out_specs=[whole] * 2,
        out_shape=[
            jax.ShapeDtypeStruct((rows, cols), jnp.float32),
            jax.ShapeDtypeStruct((16, term_cols), jnp.float32),
        ],
        scratch_shapes=[
            pltpu.VMEM((blocks, rows, cols), jnp.bfloat16),
            pltpu.VMEM((blocks - 1, rows, cols), jnp.bfloat16),
            pltpu.VMEM((blocks - 1, rows, cols), jnp.bfloat16),
            dma,
            dma,
            dma((blocks - 1,)),
            dma((blocks - 1,)),
        ]
        + adapter_scratch(term_cols),
        compiler_params=pltpu.CompilerParams(
            collective_id=collective_id, has_side_effects=True, vmem_limit_bytes=VMEM_LIMIT
        ),
    )(rows_term, term, ident)


def local_general(
    tokens,
    cotangent,
    query_key_value_weight,
    attention_out_weight,
    feedforward_in_weight,
    feedforward_out_weight,
    layer_norm_gains,
    biases,
    adapter_down_matrices,
    adapter_up_matrices,
    adapter_of_continuation,
):
    row_count = tokens.shape[0]
    prompt_rows = row_count - CONT_LEN
    prompt_total = prompt_rows * lax.axis_size("seq")
    key_count = prompt_total + CONT_LEN
    seq_index = lax.axis_index("seq")
    adapter_index = adapter_of_continuation[0, 0]
    weight_shards = (
        query_key_value_weight,
        attention_out_weight,
        feedforward_in_weight,
        feedforward_out_weight,
        adapter_down_matrices,
        adapter_up_matrices,
    )
    gathered_rows = (
        lax.all_gather(weight_shards[0], ("grp", "seq"), axis=0, tiled=True),
        lax.all_gather(weight_shards[1], ("grp", "seq"), axis=0, tiled=True),
        lax.all_gather(weight_shards[2], ("grp", "seq"), axis=0, tiled=True),
        lax.all_gather(weight_shards[3], ("grp", "seq"), axis=0, tiled=True),
        lax.all_gather(weight_shards[4], ("grp", "seq"), axis=0, tiled=True),
        lax.all_gather(weight_shards[5], ("grp", "seq"), axis=0, tiled=True),
    )
    weight_matrices, adapter_sections = unpack_sections(gathered_rows, adapter_index)
    frozen_query_key_value, frozen_attention_out, frozen_feedforward_in, frozen_feedforward_out = (
        weight_matrices
    )
    (
        down_query_key_value,
        down_attention_out,
        down_feedforward_in,
        down_feedforward_out,
        up_query_key_value,
        up_attention_out,
        up_feedforward_in,
        up_feedforward_out,
    ) = adapter_sections
    shift_one = biases[:MODEL_WIDTH]
    shift_two = biases[MODEL_WIDTH : 2 * MODEL_WIDTH]
    query_key_value_bias = jnp.concatenate(
        [
            biases[2 * MODEL_WIDTH : 3 * MODEL_WIDTH],
            jnp.zeros((MODEL_WIDTH,), jnp.float32),
            biases[3 * MODEL_WIDTH : 4 * MODEL_WIDTH],
        ]
    )
    bias_out = biases[4 * MODEL_WIDTH : 5 * MODEL_WIDTH]
    bias_proj = biases[5 * MODEL_WIDTH : 6 * MODEL_WIDTH]
    bias_fc = biases[6 * MODEL_WIDTH :]
    inputs = tokens.astype(jnp.float32)
    normed_one = layer_norm(inputs, layer_norm_gains[0], shift_one).astype(jnp.bfloat16)
    inner_one = product(normed_one[prompt_rows:], down_query_key_value).astype(jnp.bfloat16)
    mixed_query_key_value = product(normed_one, frozen_query_key_value) + query_key_value_bias
    mixed_query_key_value = mixed_query_key_value.at[prompt_rows:].add(
        product(inner_one, up_query_key_value)
    )
    qkv_rows = mixed_query_key_value.astype(jnp.bfloat16)
    prompt_keys, prompt_values = (
        lax.all_gather(
            qkv_rows[:prompt_rows, MODEL_WIDTH : 2 * MODEL_WIDTH], "seq", axis=0, tiled=True
        ),
        lax.all_gather(qkv_rows[:prompt_rows, 2 * MODEL_WIDTH :], "seq", axis=0, tiled=True),
    )
    all_keys = jnp.concatenate(
        [prompt_keys, qkv_rows[prompt_rows:, MODEL_WIDTH : 2 * MODEL_WIDTH]], 0
    )
    all_values = jnp.concatenate([prompt_values, qkv_rows[prompt_rows:, 2 * MODEL_WIDTH :]], 0)
    allowed = visible(row_count, prompt_rows, prompt_total, key_count, seq_index)
    query_heads = split_heads(qkv_rows[:, :MODEL_WIDTH])
    key_heads = split_heads(all_keys)
    value_heads = split_heads(all_values)

    def forward_head(operands):
        query_head, key_head, value_head = operands
        scores = jnp.where(allowed, product_nt(query_head, key_head) * 0.125, NEGATIVE)
        row_max = jnp.max(scores, axis=1, keepdims=True)
        exp_scores = jnp.exp(scores - row_max)
        exp_total = jnp.sum(exp_scores, axis=1, keepdims=True)
        weights = (exp_scores / exp_total).astype(jnp.bfloat16)
        return (product(weights, value_head), (row_max + jnp.log(exp_total))[:, 0])

    head_contexts, log_total = lax.map(forward_head, (query_heads, key_heads, value_heads))
    attention_context = merge_heads(head_contexts).astype(jnp.bfloat16)
    inner_two = product(attention_context[prompt_rows:], down_attention_out).astype(jnp.bfloat16)
    attention_output = product(attention_context, frozen_attention_out) + bias_out
    attention_output = attention_output.at[prompt_rows:].add(product(inner_two, up_attention_out))
    hidden = inputs + attention_output
    normed_two = layer_norm(hidden, layer_norm_gains[1], shift_two).astype(jnp.bfloat16)
    inner_three = product(normed_two[prompt_rows:], down_feedforward_in).astype(jnp.bfloat16)
    before_activation = product(normed_two, frozen_feedforward_in) + bias_fc
    before_activation = before_activation.at[prompt_rows:].add(
        product(inner_three, up_feedforward_in)
    )
    activated_hidden = jax.nn.gelu(before_activation, approximate=True).astype(jnp.bfloat16)
    inner_four = product(activated_hidden[prompt_rows:], down_feedforward_out).astype(jnp.bfloat16)
    adapter_branch = product(activated_hidden, frozen_feedforward_out) + bias_proj
    adapter_branch = adapter_branch.at[prompt_rows:].add(product(inner_four, up_feedforward_out))
    outputs = (hidden + adapter_branch).astype(jnp.bfloat16)
    weight_matrices, adapter_sections = unpack_sections(
        (
            lax.all_gather(weight_shards[0], ("grp", "seq"), axis=0, tiled=True),
            lax.all_gather(weight_shards[1], ("grp", "seq"), axis=0, tiled=True),
            lax.all_gather(weight_shards[2], ("grp", "seq"), axis=0, tiled=True),
            lax.all_gather(weight_shards[3], ("grp", "seq"), axis=0, tiled=True),
            lax.all_gather(weight_shards[4], ("grp", "seq"), axis=0, tiled=True),
            lax.all_gather(weight_shards[5], ("grp", "seq"), axis=0, tiled=True),
        ),
        adapter_index,
    )
    frozen_query_key_value, frozen_attention_out, frozen_feedforward_in, frozen_feedforward_out = (
        weight_matrices
    )
    (
        down_query_key_value,
        down_attention_out,
        down_feedforward_in,
        down_feedforward_out,
        up_query_key_value,
        up_attention_out,
        up_feedforward_in,
        up_feedforward_out,
    ) = adapter_sections
    grad_inner_four = product_nt(cotangent[prompt_rows:], up_feedforward_out).astype(jnp.bfloat16)
    grad_act = product_nt(cotangent, frozen_feedforward_out)
    grad_act = grad_act.at[prompt_rows:].add(product_nt(grad_inner_four, down_feedforward_out))
    gelu_pull = jax.vjp(lambda field: jax.nn.gelu(field, approximate=True), before_activation)[1]
    grad_pre = gelu_pull(grad_act)[0].astype(jnp.bfloat16)
    grad_inner_three = product_nt(grad_pre[prompt_rows:], up_feedforward_in).astype(jnp.bfloat16)
    grad_normed_two = product_nt(grad_pre, frozen_feedforward_in)
    grad_normed_two = grad_normed_two.at[prompt_rows:].add(
        product_nt(grad_inner_three, down_feedforward_in)
    )
    second_pull = jax.vjp(lambda field: layer_norm(field, layer_norm_gains[1], shift_two), hidden)[
        1
    ]
    grad_hidden = cotangent.astype(jnp.float32) + second_pull(grad_normed_two)[0]
    grad_attn = grad_hidden.astype(jnp.bfloat16)
    grad_inner_two = product_nt(grad_attn[prompt_rows:], up_attention_out).astype(jnp.bfloat16)
    grad_context = product_nt(grad_attn, frozen_attention_out)
    grad_context = (
        grad_context.at[prompt_rows:]
        .add(product_nt(grad_inner_two, down_attention_out))
        .astype(jnp.bfloat16)
    )

    def backward_head(operands):
        query_head, key_head, value_head, grad_head, total_head = operands
        scores = jnp.where(allowed, product_nt(query_head, key_head) * 0.125, NEGATIVE)
        prob_full = jnp.exp(scores - total_head[:, None])
        weights = prob_full.astype(jnp.bfloat16)
        grad_weights = product_nt(grad_head, value_head)
        row_delta = jnp.sum(prob_full * grad_weights, axis=1, keepdims=True)
        grad_scores = (prob_full * (grad_weights - row_delta)).astype(jnp.bfloat16)
        return (
            product(grad_scores, key_head) * 0.125,
            product_tn(grad_scores, query_head) * 0.125,
            product_tn(weights, grad_head),
        )

    grad_q, grad_k, grad_v = lax.map(
        backward_head, (query_heads, key_heads, value_heads, split_heads(grad_context), log_total)
    )
    grad_query = merge_heads(grad_q)
    grad_keys = merge_heads(grad_k)
    grad_values = merge_heads(grad_v)
    own_keys, own_values = (
        lax.psum_scatter(
            grad_keys[:prompt_total].astype(jnp.bfloat16), "seq", scatter_dimension=0, tiled=True
        ).astype(jnp.float32),
        lax.psum_scatter(
            grad_values[:prompt_total].astype(jnp.bfloat16), "seq", scatter_dimension=0, tiled=True
        ).astype(jnp.float32),
    )
    grad_qkv = jnp.concatenate(
        [
            grad_query,
            jnp.concatenate([own_keys, grad_keys[prompt_total:]], 0),
            jnp.concatenate([own_values, grad_values[prompt_total:]], 0),
        ],
        1,
    ).astype(jnp.bfloat16)
    grad_inner_one = product_nt(grad_qkv[prompt_rows:], up_query_key_value).astype(jnp.bfloat16)
    grad_normed_one = product_nt(grad_qkv, frozen_query_key_value)
    grad_normed_one = grad_normed_one.at[prompt_rows:].add(
        product_nt(grad_inner_one, down_query_key_value)
    )
    first_pull = jax.vjp(lambda field: layer_norm(field, layer_norm_gains[0], shift_one), inputs)[1]
    input_grad = grad_hidden + first_pull(grad_normed_one)[0]
    down_term = jnp.concatenate(
        [
            product_tn(normed_one[prompt_rows:], grad_inner_one),
            product_tn(attention_context[prompt_rows:], grad_inner_two),
            product_tn(normed_two[prompt_rows:], grad_inner_three),
            product_tn(activated_hidden[prompt_rows:], grad_inner_four),
        ],
        0,
    )
    up_term = jnp.concatenate(
        [
            product_tn(inner_one, grad_qkv[prompt_rows:]),
            product_tn(inner_two, grad_attn[prompt_rows:]),
            product_tn(inner_three, grad_pre[prompt_rows:]),
            product_tn(inner_four, cotangent[prompt_rows:]),
        ],
        1,
    )
    select = (jnp.arange(ADAPTER_COUNT, dtype=jnp.int32) == adapter_index).astype(jnp.float32)
    down_grad, up_grad = (
        lax.psum_scatter(
            (select[:, None, None] * down_term[None]).reshape(-1),
            ("grp", "seq"),
            scatter_dimension=0,
            tiled=True,
        ),
        lax.psum_scatter(
            (select[:, None, None] * up_term[None]).reshape(-1),
            ("grp", "seq"),
            scatter_dimension=0,
            tiled=True,
        ),
    )
    return (outputs, input_grad, down_grad, up_grad)


def fast(
    tokens,
    cotangent,
    query_key_value_weight,
    attention_out_weight,
    feedforward_in_weight,
    feedforward_out_weight,
    layer_norm_gains,
    biases,
    adapter_down_matrices,
    adapter_up_matrices,
    adapter_of_continuation,
):
    groups = (lax.axis_size("grp"), lax.axis_size("seq"))
    prompt_rows = tokens.shape[0] - CONT_LEN
    prompt_total = prompt_rows * groups[1]
    up_cols = 5 * MODEL_WIDTH + HIDDEN_UNITS
    adapter_index = adapter_of_continuation[0, 0]
    shift_one = biases[:MODEL_WIDTH]
    ups_shard = adapter_up_matrices.reshape(4, up_cols)
    up_parts, first = [], 0
    for size in UP_SECTIONS:
        up_parts.append(ups_shard[:, first : first + size].reshape(16, size // 4))
        first += size
    (
        queries,
        keys_values,
        context,
        log_total,
        outputs,
        grad_hidden,
        grad_context,
        early_term,
        inner_one,
        down_qkv,
        up_qkv,
        _,
        _,
        _,
        w_qkv,
        _,
        _,
        _,
    ) = forward_and_gather(
        groups,
        adapter_of_continuation,
        tokens,
        cotangent,
        layer_norm_gains,
        biases.reshape(1, -1),
        [
            adapter_down_matrices.reshape(-1, ADAPTER_RANK).T,
            jnp.concatenate(up_parts, 1),
            query_key_value_weight.reshape(-1, 3 * MODEL_WIDTH),
            attention_out_weight.reshape(-1, MODEL_WIDTH),
            feedforward_in_weight.reshape(-1, HIDDEN_UNITS),
            feedforward_out_weight.reshape(-1, MODEL_WIDTH),
        ],
        1,
    )
    inputs = tokens.astype(jnp.float32)
    normed_later = layer_norm(inputs[prompt_rows:], layer_norm_gains[0], shift_one).astype(
        jnp.bfloat16
    )
    ident = jnp.full((16, 128), adapter_index, jnp.int32).astype(jnp.bfloat16)

    grad_q, grad_k, grad_v, early = attend_back_and_reduce(
        queries, keys_values, grad_context, context, log_total, early_term, ident, 3
    )

    w_q, w_k, w_v = (
        w_qkv[:, :MODEL_WIDTH],
        w_qkv[:, MODEL_WIDTH : 2 * MODEL_WIDTH],
        w_qkv[:, 2 * MODEL_WIDTH :],
    )
    rows_term = (
        product_nt(grad_k[:prompt_total], w_k) + product_nt(grad_v[:prompt_total], w_v)
    ).astype(jnp.bfloat16)
    grad_later = jnp.concatenate(
        [grad_q[prompt_rows:], grad_k[prompt_total:], grad_v[prompt_total:]], 1
    )
    grad_inner_one = product_nt(grad_later, up_qkv).astype(jnp.bfloat16)
    down_late = product_tn(grad_inner_one, normed_later)
    down_late = jnp.stack([down_late] + [jnp.zeros_like(down_late)] * 3)
    up_late = product(inner_one, grad_later).reshape(4, 16, -1)
    late_term = jnp.concatenate([down_late, up_late], 2).astype(jnp.bfloat16)
    prompt_sum, late = last_exchange(
        rows_term.reshape(groups[1] // 2, 2, prompt_rows, MODEL_WIDTH), late_term, ident, 4
    )
    later_normed_grad = product_nt(grad_later, w_qkv) + product(grad_inner_one, down_qkv)
    prompt_normed_grad = product_nt(grad_q[:prompt_rows], w_q) + prompt_sum
    grad_normed_one = jnp.concatenate([prompt_normed_grad, later_normed_grad], 0)
    first_pull = jax.vjp(lambda field: layer_norm(field, layer_norm_gains[0], shift_one), inputs)[1]
    input_grad = grad_hidden + first_pull(grad_normed_one)[0]

    down_grad = early[:, :QUARTER].at[:, :MODEL_WIDTH].add(late[:, :MODEL_WIDTH])
    down_grad = down_grad.T.reshape(-1)
    up_pieces = [late[:, MODEL_WIDTH:]]
    for start, size in zip(UP_STARTS[1:], UP_SECTIONS[1:]):
        start += QUARTER - UP_STARTS[1]
        up_pieces.append(early[:, start : start + size // 4])
    up_grad = jnp.concatenate([x.reshape(4, -1) for x in up_pieces], 1).reshape(-1)
    return (outputs, input_grad, down_grad, up_grad)


def solution(mesh):
    placed = (
        P(("grp", "seq"), None),
        P(("grp", "seq"), None),
        P(("grp", "seq")),
        P(("grp", "seq")),
        P(("grp", "seq")),
        P(("grp", "seq")),
        P(),
        P(),
        P(("grp", "seq")),
        P(("grp", "seq")),
        P(("grp", "seq"), None),
    )
    fits = mesh.shape["grp"] == 4 and mesh.shape["seq"] == 8
    return jax.shard_map(
        fast if fits else local_general,
        mesh=mesh,
        in_specs=placed,
        out_specs=(
            P(("grp", "seq"), None),
            P(("grp", "seq"), None),
            P(("grp", "seq")),
            P(("grp", "seq")),
        ),
        check_vma=False,
    )
```

```python
import functools

import jax
import jax.numpy as jnp
from jax import lax
from jax.experimental import pallas as pl
from jax.experimental.pallas import tpu as pltpu
from jax.sharding import PartitionSpec as P

MODEL_WIDTH = 1024
HEADS = 16
HEAD_DIM = 64
HIDDEN_UNITS = 4096
ADAPTER_RANK = 16
ADAPTER_COUNT = 8
CONT_LEN = 512


EPSILON = 1e-05
NEGATIVE = -1e30


def product(left_side, right_side):
    return jnp.dot(left_side, right_side, preferred_element_type=jnp.float32)


def product_tn(left_side, right_side):
    return lax.dot_general(
        left_side, right_side, (((0,), (0,)), ((), ())), preferred_element_type=jnp.float32
    )


def product_nt(left_side, right_side):
    return lax.dot_general(
        left_side, right_side, (((1,), (1,)), ((), ())), preferred_element_type=jnp.float32
    )


def layer_norm(values, gain_vec, shift_vec):
    row_mean = jnp.mean(values, axis=-1, keepdims=True)
    centred = values - row_mean
    row_var = jnp.mean(centred * centred, axis=-1, keepdims=True)
    return centred * lax.rsqrt(row_var + EPSILON) * gain_vec + shift_vec


def unpack_sections(pieces, adapter_index):
    qkv_flat, out_flat, fc_flat, proj_flat, down_flat, up_flat = pieces
    every_down_matrix = down_flat.reshape(
        ADAPTER_COUNT, 3 * MODEL_WIDTH + HIDDEN_UNITS, ADAPTER_RANK
    )
    every_up_matrix = up_flat.reshape(ADAPTER_COUNT, ADAPTER_RANK, 5 * MODEL_WIDTH + HIDDEN_UNITS)
    down_rows = lax.dynamic_index_in_dim(every_down_matrix, adapter_index, 0, keepdims=False)
    up_cols = lax.dynamic_index_in_dim(every_up_matrix, adapter_index, 0, keepdims=False)
    weight_matrices = (
        qkv_flat.reshape(MODEL_WIDTH, 3 * MODEL_WIDTH),
        out_flat.reshape(MODEL_WIDTH, MODEL_WIDTH),
        fc_flat.reshape(MODEL_WIDTH, HIDDEN_UNITS),
        proj_flat.reshape(HIDDEN_UNITS, MODEL_WIDTH),
    )
    adapter_sections = (
        down_rows[:MODEL_WIDTH],
        down_rows[MODEL_WIDTH : 2 * MODEL_WIDTH],
        down_rows[2 * MODEL_WIDTH : 3 * MODEL_WIDTH],
        down_rows[3 * MODEL_WIDTH :],
        up_cols[:, : 3 * MODEL_WIDTH],
        up_cols[:, 3 * MODEL_WIDTH : 4 * MODEL_WIDTH],
        up_cols[:, 4 * MODEL_WIDTH : 4 * MODEL_WIDTH + HIDDEN_UNITS],
        up_cols[:, 4 * MODEL_WIDTH + HIDDEN_UNITS :],
    )
    return (weight_matrices, adapter_sections)


def visible(row_count, prompt_rows, prompt_total, key_count, seq_index):
    row_ids = jnp.arange(row_count, dtype=jnp.int32)[:, None]
    col_ids = jnp.arange(key_count, dtype=jnp.int32)[None, :]
    in_prompt = col_ids < prompt_total
    prompt_seen = in_prompt & (col_ids <= seq_index * prompt_rows + row_ids)
    later_seen = in_prompt | (col_ids - prompt_total <= row_ids - prompt_rows)
    return jnp.where(row_ids < prompt_rows, prompt_seen, later_seen)


def split_heads(values):
    return values.reshape(values.shape[0], HEADS, HEAD_DIM).transpose(1, 0, 2)


def merge_heads(values):
    return values.transpose(1, 0, 2).reshape(values.shape[1], HEADS * HEAD_DIM)


MESH = pl.DeviceIdType.MESH
SCALE2 = 0.125 * 1.4426950408889634
VMEM_LIMIT = 63 << 20


def gather_stages(groups, sizes, chunks, ins, outs, sems):
    grp_n, seq_n = groups
    z_n, y_n = seq_n // 2, grp_n // 2
    z_sem, x_sem, y_sem, d_sem, p_sem, s_sem, l_sem = sems
    g, s = lax.axis_index("grp"), lax.axis_index("seq")
    core, z = lax.rem(s, 2), s // 2
    gx, gy = lax.rem(g, 2), g // 2
    partner = (g, z * 2 + 1 - core)
    other_x = gy * 2 + 1 - gx
    x_next = (other_x, s)
    far_z = [lax.rem(z + d, z_n) for d in range(1, z_n)]
    far_y = [lax.rem(gy + d, y_n) for d in range(1, y_n)]
    y_next = [(y * 2 + gx, s) for y in far_y]

    def enter():
        peers = [partner, x_next] + y_next + [(g, far * 2 + core) for far in far_z]
        barrier = pltpu.get_barrier_semaphore()
        for peer in peers:
            pl.semaphore_signal(barrier, inc=1, device_id=peer, device_id_type=MESH)
        pl.semaphore_wait(barrier, len(peers))

    def place(ch, gg, ss):
        arr, row, rows, full = chunks[ch]
        block = gg * seq_n + ss if full else ss
        return outs[arr].at[pl.ds(pl.multiple_of(block * sizes[arr] + row, 16), rows)]

    def send(ch, src, gg, ss, sem, device):
        pltpu.make_async_remote_copy(
            src_ref=src,
            dst_ref=place(ch, gg, ss),
            send_sem=s_sem.at[ch],
            recv_sem=sem,
            device_id=device,
            device_id_type=MESH,
        ).start()

    def drain(ch, sem, count=1):
        arr, _, rows, _ = chunks[ch]
        block = outs[arr].at[pl.ds(0, count * rows)]
        pltpu.make_async_copy(block, block, sem).wait()

    def own(ch):
        arr, row, rows, full = chunks[ch]
        src = ins[arr].at[pl.ds(row, rows)]
        for far in far_z:
            send(ch, src, g, s, z_sem.at[ch, z], (g, far * 2 + core))
        if full:
            send(ch, src, g, s, x_sem.at[ch, z], x_next)
            for peer in y_next:
                send(ch, src, g, s, y_sem.at[ch, gy, z], peer)
        send(ch, src, g, s, p_sem.at[ch, 0], partner)
        pltpu.make_async_copy(src, place(ch, g, s), l_sem.at[ch]).start()

    def line(ch):
        for far in far_z:
            drain(ch, z_sem.at[ch, far])
            from_s = far * 2 + core
            src = place(ch, g, from_s)
            if chunks[ch][3]:
                send(ch, src, g, from_s, x_sem.at[ch, far], x_next)
                for peer in y_next:
                    send(ch, src, g, from_s, y_sem.at[ch, gy, far], peer)
            send(ch, src, g, from_s, p_sem.at[ch, 0], partner)

    def side(ch):
        if not chunks[ch][3]:
            return
        for far in range(z_n):
            from_s = far * 2 + core
            drain(ch, x_sem.at[ch, far])
            src = place(ch, other_x, from_s)
            if far % 2 == 0:
                for peer in y_next:
                    send(ch, src, other_x, from_s, d_sem.at[ch, gy, far], peer)
            send(ch, src, other_x, from_s, p_sem.at[ch, 1], partner)
            for y in far_y:
                drain(ch, y_sem.at[ch, y, far])
                from_g = y * 2 + gx
                src = place(ch, from_g, from_s)
                if far % 2 == 1:
                    send(ch, src, from_g, from_s, d_sem.at[ch, y, far], x_next)
                send(ch, src, from_g, from_s, p_sem.at[ch, 2], partner)

    def corner(ch):
        if not chunks[ch][3]:
            return
        for far in range(z_n):
            from_s = far * 2 + core
            for y in far_y:
                drain(ch, d_sem.at[ch, y, far])
                from_g = y * 2 + 1 - gx
                src = place(ch, from_g, from_s)
                send(ch, src, from_g, from_s, p_sem.at[ch, 3], partner)

    def ready(ch, kinds=range(4)):
        for kind in kinds if chunks[ch][3] else (0,):
            drain(ch, p_sem.at[ch, kind], z_n * (y_n - 1 if kind >= 2 else 1))
            if kind == 0:
                drain(ch, l_sem.at[ch])

    def finish(ch):
        sends = 2 * z_n - 1
        if chunks[ch][3]:
            sends += z_n * y_n
            sends += z_n * (y_n - 1)
            sends += z_n * (2 * y_n - 1)
        drain(ch, s_sem.at[ch], sends)

    steps = (own, line, side, corner)

    def tick(t):
        for lag, step in enumerate(steps):
            if 0 <= t - lag < len(chunks):
                step(t - lag)

    return enter, tick, ready, finish


def gather_plan(groups, shards, splits):
    grp_n, seq_n = groups
    chunks, shapes = [], []
    for i, (rows, cols, full) in enumerate(shards):
        part = rows // splits[i]
        chunks += [(i, j * part, part, full) for j in range(splits[i])]
        total = (grp_n if full else 1) * seq_n * rows
        shapes.append(jax.ShapeDtypeStruct((total, cols), jnp.bfloat16))
    dma, count = pltpu.SemaphoreType.DMA, len(chunks)
    sems = [
        dma((count, seq_n // 2)),
        dma((count, seq_n // 2)),
        dma((count, grp_n // 2, seq_n // 2)),
        dma((count, grp_n // 2, seq_n // 2)),
        dma((count, 4)),
        dma((count,)),
        dma((count,)),
    ]
    return [rows for rows, _, _ in shards], chunks, shapes, sems


def dot_nt(left, right):
    return lax.dot_general(
        left, right, (((1,), (1,)), ((), ())), preferred_element_type=jnp.float32
    )


def dot_nn(left, right):
    return lax.dot_general(
        left, right, (((1,), (0,)), ((), ())), preferred_element_type=jnp.float32
    )


def stacked_heads(pair):
    first = lax.broadcasted_iota(jnp.int32, pair.shape, 1) < HEAD_DIM
    zero = jnp.zeros_like(pair)
    return jnp.concatenate([jnp.where(first, pair, zero), jnp.where(first, zero, pair)], 0)


def row_groups(prompt_rows, prompt_total, later_rows):
    block = min(256, later_rows)
    return [(prompt_rows + i, block, prompt_total + i) for i in range(0, later_rows, block)]


def attention_forward(sizes, q_ref, k_ref, v_ref, ctx_ref, lse_ref, wide_ref):
    prompt_rows, prompt_total, later_rows = sizes
    seq = lax.axis_index("seq")
    wide_ref[:, :128] = v_ref[...]
    wide_ref[:, 128:] = jnp.ones((prompt_total + later_rows, 128), jnp.bfloat16)

    def finish(start, rows, row_max, summed):
        total = summed[:, 128:]
        mixed = summed[:, :128] / total
        log_total = row_max * SCALE2 + jnp.log2(total)
        first = lax.broadcasted_iota(jnp.int32, (rows, 128), 1) < HEAD_DIM
        ctx_ref[start : start + rows] = jnp.where(first, mixed[:rows], mixed[rows:]).astype(
            jnp.bfloat16
        )
        lse_ref[start : start + rows] = jnp.where(first, log_total[:rows], log_total[rows:])

    for start, rows, free in row_groups(prompt_rows, prompt_total, later_rows):
        queries = stacked_heads(q_ref[start : start + rows])
        open_scores = dot_nt(queries, k_ref[:free])
        edge_scores = dot_nt(queries, k_ref[free : free + rows])
        row = lax.broadcasted_iota(jnp.int32, (rows, rows), 0)
        key = lax.broadcasted_iota(jnp.int32, (rows, rows), 1)
        seen = key <= row
        edge_scores = jnp.where(jnp.concatenate([seen, seen], 0), edge_scores, NEGATIVE)
        row_max = jnp.maximum(
            jnp.max(open_scores, 1, keepdims=True), jnp.max(edge_scores, 1, keepdims=True)
        )
        scaled = row_max * SCALE2
        open_p = jnp.exp2(open_scores * SCALE2 - scaled).astype(jnp.bfloat16)
        edge_p = jnp.exp2(edge_scores * SCALE2 - scaled).astype(jnp.bfloat16)
        summed = dot_nn(open_p, wide_ref[:free]) + dot_nn(edge_p, wide_ref[free : free + rows])
        finish(start, rows, row_max, summed)
    scores = dot_nt(stacked_heads(q_ref[:prompt_rows]), k_ref[:prompt_total])
    row = lax.broadcasted_iota(jnp.int32, (prompt_rows, prompt_total), 0)
    key = lax.broadcasted_iota(jnp.int32, (prompt_rows, prompt_total), 1)
    seen = key <= row + seq * prompt_rows
    scores = jnp.where(jnp.concatenate([seen, seen], 0), scores, NEGATIVE)
    row_max = jnp.max(scores, 1, keepdims=True)
    p = jnp.exp2(scores * SCALE2 - row_max * SCALE2).astype(jnp.bfloat16)
    finish(0, prompt_rows, row_max, dot_nn(p, wide_ref[:prompt_total]))


def attention_backward(
    sizes, q_ref, k_ref, v_ref, d_ref, ctx_ref, lse_ref, dq_ref, k_sum, v_sum
):
    prompt_rows, prompt_total, later_rows = sizes
    seq = lax.axis_index("seq")
    keys_t = k_ref[...].astype(jnp.float32).T.astype(jnp.bfloat16)
    lse_t = lse_ref[...].T
    weighed_t = (d_ref[...].astype(jnp.float32) * ctx_ref[...].astype(jnp.float32)).T
    deltas = [
        jnp.sum(weighed_t[:HEAD_DIM], 0, keepdims=True),
        jnp.sum(weighed_t[HEAD_DIM:], 0, keepdims=True),
    ]
    totals = [lse_t[0:1], lse_t[HEAD_DIM : HEAD_DIM + 1]]

    def group(start, rows, count, mask):
        queries = stacked_heads(q_ref[start : start + rows])
        grads = stacked_heads(d_ref[start : start + rows])
        total = jnp.concatenate([t[:, start : start + rows] for t in totals], 1)
        delta = jnp.concatenate([t[:, start : start + rows] for t in deltas], 1)
        p = mask(jnp.exp2(dot_nt(k_ref[:count], queries) * SCALE2 - total))
        d_scores = (p * (dot_nt(v_ref[:count], grads) - delta)).astype(jnp.bfloat16)
        dq_t = dot_nn(keys_t[:, :count], d_scores)
        first = lax.broadcasted_iota(jnp.int32, (128, rows), 0) < HEAD_DIM
        dq = jnp.where(first, dq_t[:, :rows], dq_t[:, rows:]).T * 0.125
        dq_ref[start : start + rows] = dq.astype(jnp.bfloat16)
        return dot_nn(d_scores, queries), dot_nn(p.astype(jnp.bfloat16), grads)

    def causal(free, rows):
        def mask(p):
            key = lax.broadcasted_iota(jnp.int32, (rows, rows), 0)
            row = lax.broadcasted_iota(jnp.int32, (rows, rows), 1)
            seen = key <= row
            edge = jnp.where(jnp.concatenate([seen, seen], 1), p[free:], 0.0)
            return jnp.concatenate([p[:free], edge], 0)

        return mask

    def prompt_mask(p):
        key = lax.broadcasted_iota(jnp.int32, (prompt_total, prompt_rows), 0)
        row = lax.broadcasted_iota(jnp.int32, (prompt_total, prompt_rows), 1)
        seen = key <= row + seq * prompt_rows
        return jnp.where(jnp.concatenate([seen, seen], 1), p, 0.0)

    groups = row_groups(prompt_rows, prompt_total, later_rows)
    start, rows, free = groups[-1]
    k_sum[...], v_sum[...] = group(start, rows, free + rows, causal(free, rows))
    for start, rows, free in groups[:-1]:
        d_keys, d_values = group(start, rows, free + rows, causal(free, rows))
        k_sum[: free + rows] += d_keys
        v_sum[: free + rows] += d_values
    d_keys, d_values = group(0, prompt_rows, prompt_total, prompt_mask)
    k_sum[:prompt_total] += d_keys
    v_sum[:prompt_total] += d_values


UP_SECTIONS = (3 * MODEL_WIDTH, MODEL_WIDTH, HIDDEN_UNITS, MODEL_WIDTH)
UP_STARTS = (0, 768, 1024, 2048)
UP_FIRST = (0, 3 * MODEL_WIDTH, 4 * MODEL_WIDTH, 4 * MODEL_WIDTH + HIDDEN_UNITS)
QUARTER = (3 * MODEL_WIDTH + HIDDEN_UNITS) // 4
UP_QUARTER = sum(UP_SECTIONS) // 4
EARLY_COLS = QUARTER + UP_QUARTER - UP_STARTS[1]
TILE = 256


def for_blocks(count, body):
    def step(i, carry):
        body(pl.multiple_of(i * 128, 128))
        return carry

    lax.fori_loop(0, count // 128, step, 0)


def centre(values):
    centred = values - jnp.mean(values, axis=1, keepdims=True)
    var = jnp.mean(centred * centred, axis=1, keepdims=True)
    return centred, lax.rsqrt(var + EPSILON)


def normalize_rows(read, write, count, gain, shift):
    def body(start):
        centred, scale = centre(read(start))
        write(start, (centred * scale * gain + shift).astype(jnp.bfloat16))

    for_blocks(count, body)


def norm_pull(values, grads, gain):
    centred, scale = centre(values)
    unit = centred * scale
    grads = grads * gain
    along = jnp.mean(grads * unit, axis=1, keepdims=True)
    return scale * (grads - jnp.mean(grads, axis=1, keepdims=True) - unit * along)


def gelu_both(field):
    square = field * field
    bent = jnp.tanh(0.7978845608028654 * (field + 0.044715 * square * field))
    half = 0.5 * (1.0 + bent)
    slope = 0.7978845608028654 * (1.0 + 3.0 * 0.044715 * square)
    return field * half, half + 0.5 * field * (1.0 - bent * bent) * slope


def quarter_rows(rows, offset, part, across):
    rank = lax.broadcasted_iota(jnp.int32, (ADAPTER_RANK, rows), 0)
    row = lax.broadcasted_iota(jnp.int32, (ADAPTER_RANK, rows), 1)
    if across:
        rank = lax.broadcasted_iota(jnp.int32, (rows, ADAPTER_RANK), 1)
        row = lax.broadcasted_iota(jnp.int32, (rows, ADAPTER_RANK), 0)
    return (row == offset + (rank // 4) * 16 + (rank % 4) * 4 + part).astype(jnp.bfloat16)


def forward_and_gather(groups, ident, tokens, cotangent, gains, biases, shards, collective_id):
    rows = tokens.shape[0]
    prompt_rows = rows - CONT_LEN
    prompt_total = prompt_rows * groups[1]
    keys = prompt_total + CONT_LEN
    sizes = (prompt_rows, prompt_total, CONT_LEN)
    width, hidden_units = MODEL_WIDTH, HIDDEN_UNITS
    pairs = width // 128
    plan = [(prompt_rows, width, False)] + [(a.shape[0], a.shape[1], True) for a in shards]
    splits = [1, 1, 1, 2, 1, 2, 2]
    lengths, chunks, gathered, sems = gather_plan(groups, plan, splits)
    count = len(plan)
    dma = pltpu.SemaphoreType.DMA
    bf, f32 = jnp.bfloat16, jnp.float32

    def kernel(id_ref, tokens_ref, cot_ref, gains_ref, bias_ref, *refs):
        ins = (tokens_ref,) + refs[: count - 1]
        refs = refs[count - 1 :]
        q_out, kv_out, ctx_out, lse_out, act_out, dh_out, dc_out = refs[:7]
        early_out, inner_out, down_out, up_out = refs[7:11]
        outs, refs = refs[11 : 11 + count], refs[11 + count :]
        (
            prompt_v,
            norm_v,
            weight_v,
            w_out_v,
            q_v,
            kv_v,
            wide_v,
            ctx_v,
            lse_v,
            h_v,
            n_v,
            gl_v,
            gp_v,
            dn_v,
            downs_v,
            ups_v,
            down_v,
            up_v,
            low_v,
            turned_v,
            d_low,
            d_turned,
            acc_low,
            acc_turned,
            down_e,
            up_e,
            in_sem,
            out_sem,
        ) = refs[:28]
        enter, tick, ready, finish = gather_stages(groups, lengths, chunks, ins, outs, refs[28:])
        adapter = id_ref[0, 0]
        seq = lax.axis_index("seq")
        grp = lax.axis_index("grp")

        def load(src, dst, sem):
            copy = pltpu.make_async_copy(src, dst, in_sem.at[sem])
            copy.start()
            return copy

        stores, store_sem = [], iter(range(8))

        def store(src, dst):
            copy = pltpu.make_async_copy(src, dst, out_sem.at[next(store_sem)])
            copy.start()
            stores.append(copy)
            return copy

        def settle(copy):
            copy.wait()
            stores[:] = [other for other in stores if other is not copy]

        def bias(start, size):
            return bias_ref[:, pl.ds(pl.multiple_of(start, 128), size)]

        def tile(i, size=TILE, first=0):
            return pl.ds(pl.multiple_of(i * size + first, 128), size)

        def read_tokens(start):
            at = pl.multiple_of(start + prompt_rows, 128)
            return tokens_ref[pl.ds(at, 128)].astype(f32)

        def write_later(start, values):
            norm_v[pl.ds(pl.multiple_of(start + prompt_total, 128), 128)] = values

        def read_prompt(start):
            return prompt_v[pl.ds(start, 128)].astype(f32)

        def write_prompt(start, values):
            norm_v[pl.ds(start, 128)] = values

        def read_hidden(start):
            return h_v[pl.ds(start, 128)]

        def write_hidden(start, values):
            n_v[pl.ds(start, 128)] = values

        def inner(which, values, down):
            low_v[which] = dot_nt(values, down).astype(bf)
            turned_v[which] = dot_nt(down, values).astype(bf)

        def d_inner(which, values, up):
            d_low[which] = dot_nt(values, up).astype(bf)
            d_turned[which] = dot_nt(up, values).astype(bf)

        enter()
        tick(0)
        shift_one = bias_ref[:, :width]
        normalize_rows(read_tokens, write_later, CONT_LEN, gains_ref[0:1], shift_one)
        tick(1)
        ready(0)
        load(outs[0], prompt_v, 0).wait()
        normalize_rows(read_prompt, write_prompt, prompt_total, gains_ref[0:1], shift_one)
        tick(2)
        tick(3)
        tick(4)
        ready(1)
        copy_down = load(outs[1], downs_v, 1)
        tick(5)
        ready(2)
        copy_up = load(outs[2], ups_v, 2)
        copy_down.wait()
        copy_up.wait()
        at = lax.broadcasted_iota(jnp.int32, (ADAPTER_RANK, downs_v.shape[0]), 1)
        rank = lax.broadcasted_iota(jnp.int32, (ADAPTER_RANK, downs_v.shape[0]), 0)
        for part in range(4):
            chosen = (at == rank + (adapter * 64 + part * 16)).astype(bf)
            down_v[:, part * QUARTER : (part + 1) * QUARTER] = dot_nn(chosen, downs_v[...]).astype(
                bf
            )
            chosen = quarter_rows(ups_v.shape[0], adapter * 64, part, False)
            for first, start, size in zip(UP_FIRST, UP_STARTS, UP_SECTIONS):
                size //= 4
                up_v[:, first + part * size : first + (part + 1) * size] = dot_nn(
                    chosen, ups_v[:, start : start + size]
                ).astype(bf)
        down_out[...] = down_v[:, :width]
        up_out[...] = up_v[:, : 3 * width]
        inner(0, norm_v[prompt_total:], down_v[:, :width])
        inner_out[...] = turned_v[0]
        d_inner(3, cot_ref[prompt_rows:], up_v[:, UP_FIRST[3] :])
        tick(6)
        tick(7)
        ready(3)
        ready(4)
        load(outs[3], weight_v.at[:, : 3 * width], 3).wait()

        def later_tile(i):
            weight = weight_v[:, tile(i)]
            later = dot_nn(norm_v[prompt_total:], weight) + dot_nn(low_v[0], up_v[:, tile(i)])
            return weight, later

        def key_tile(i, carry):
            weight, later = later_tile(i)
            shift = jnp.where(i >= 8, bias(i * TILE + width, TILE), 0.0)
            to = tile(i - 4)
            kv_v[prompt_total:, to] = (later + shift).astype(bf)
            early = dot_nn(norm_v[:prompt_total], weight)
            kv_v[:prompt_total, to] = (early + shift).astype(bf)
            return carry

        def query_tile(i, carry):
            weight, later = later_tile(i)
            shift = bias(i * TILE + 2 * width, TILE)
            q_v[prompt_rows:, tile(i)] = (later + shift).astype(bf)
            mine = norm_v[pl.ds(pl.multiple_of(seq * prompt_rows, 128), prompt_rows)]
            q_v[:prompt_rows, tile(i)] = (dot_nn(mine, weight) + shift).astype(bf)
            return carry

        lax.fori_loop(4, 12, key_tile, 0)
        kv_store = store(kv_v, kv_out)
        tick(8)
        ready(5)
        load_out = load(outs[4], w_out_v, 4)
        lax.fori_loop(0, 4, query_tile, 0)
        q_store = store(q_v, q_out)

        def attend(i, carry):
            cols = pl.ds(pl.multiple_of(i * 128, 128), 128)
            values = pl.ds(pl.multiple_of(i * 128 + width, 128), 128)

            @pl.when(i == pairs // 2)
            def _():
                tick(9)

            attention_forward(
                sizes,
                q_v.at[:, cols],
                kv_v.at[:, cols],
                kv_v.at[:, values],
                ctx_v.at[:, cols],
                lse_v.at[:, cols],
                wide_v,
            )
            return carry

        lax.fori_loop(0, pairs, attend, 0)
        store(ctx_v, ctx_out)
        lse_store = store(lse_v, lse_out)
        tick(10)
        ready(6)
        ready(7)
        load_fc = load(outs[5], weight_v, 5)
        load_out.wait()
        inner(1, ctx_v[prompt_rows:], down_v[:, width : 2 * width])

        def out_tile(j, carry):
            cols = tile(j)
            mixed = dot_nn(ctx_v[...], w_out_v[:, cols]) + bias(j * TILE + 4 * width, TILE)
            mixed = tokens_ref[:, cols].astype(f32) + mixed
            extra = dot_nn(low_v[1], up_v[:, tile(j, first=UP_FIRST[1])])
            h_v[:prompt_rows, cols] = mixed[:prompt_rows]
            h_v[prompt_rows:, cols] = mixed[prompt_rows:] + extra
            return carry

        lax.fori_loop(0, 4, out_tile, 0)
        normalize_rows(
            read_hidden, write_hidden, rows, gains_ref[1:2], bias_ref[:, width : 2 * width]
        )
        inner(2, n_v[prompt_rows:], down_v[:, 2 * width : 3 * width])
        settle(lse_store)
        sum_v = lse_v

        def start_sums(start):
            at = pl.ds(start, 128)
            sum_v[at] = h_v[at] + bias_ref[:, 5 * width : 6 * width]
            dn_v[at] = jnp.zeros((128, width), f32)

        for_blocks(rows, start_sums)
        load_fc.wait()

        tiles = hidden_units // TILE

        def hidden_tile(i, carry):
            cols = tile(i)

            @pl.when(i == tiles // 2)
            def _():
                tick(11)

            wide = dot_nn(n_v[...], weight_v[:, cols]) + bias(i * TILE + 6 * width, TILE)
            extra = dot_nn(low_v[2], up_v[:, tile(i, first=UP_FIRST[2])])
            for at, field in (
                (slice(0, prompt_rows), wide[:prompt_rows]),
                (slice(prompt_rows, rows), wide[prompt_rows:] + extra),
            ):
                value, slope = gelu_both(field)
                gl_v[at, cols] = value.astype(bf)
                gp_v[at, cols] = slope.astype(bf)
            return carry

        lax.fori_loop(0, tiles, hidden_tile, 0)
        settle(kv_store)
        tick(12)

        df_v = norm_v.at[:rows]
        part_rows = hidden_units // 4
        for which in range(2):
            acc_low[which] = jnp.zeros((CONT_LEN, ADAPTER_RANK), f32)
            acc_turned[which] = jnp.zeros((ADAPTER_RANK, CONT_LEN), f32)
        gx, gy = lax.rem(grp, 2), grp // 2
        order = [grp, gy * 2 + 1 - gx, (1 - gy) * 2 + gx, (1 - gy) * 2 + 1 - gx]
        for kind, unit in enumerate(order):
            ready(8, (kind,))
            ready(9, (kind,))
            base = pl.multiple_of(unit * part_rows, part_rows)
            part = pl.ds(base, part_rows)
            down_part = pl.ds(pl.multiple_of(base + 3 * width, width), part_rows)
            up_part = pl.ds(pl.multiple_of(base + UP_FIRST[2], width), part_rows)
            slot = kv_v.at[:part_rows, (kind % 2) * width : (kind % 2 + 1) * width]
            load(outs[6].at[part], slot, 6 + kind % 2).wait()

            def d_hidden(j, carry, base=base, slot=slot):
                cols = tile(j, first=base)
                wide = dot_nt(cot_ref[...], slot[tile(j)])
                extra = dot_nn(d_low[3], down_v[:, tile(j, first=base + 3 * width)])
                slope = gp_v[:, cols].astype(f32)
                to = tile(j)
                df_v[:prompt_rows, to] = (wide[:prompt_rows] * slope[:prompt_rows]).astype(bf)
                later = (wide[prompt_rows:] + extra) * slope[prompt_rows:]
                df_v[prompt_rows:, to] = later.astype(bf)
                return carry

            lax.fori_loop(0, part_rows // TILE, d_hidden, 0)
            df_later = df_v[prompt_rows:]
            gl_later = gl_v[prompt_rows:, part]
            acc_low[0] += dot_nt(df_later, up_v[:, up_part])
            acc_turned[0] += dot_nt(up_v[:, up_part], df_later)
            acc_low[1] += dot_nt(gl_later, down_v[:, down_part])
            acc_turned[1] += dot_nt(down_v[:, down_part], gl_later)
            down_e[:, down_part] = dot_nn(d_turned[3], gl_later).astype(bf)
            up_e[:, up_part] = dot_nn(turned_v[2], df_later).astype(bf)

            def sums(j, carry, part=part, slot=slot):
                cols = tile(j)
                sum_v[:, cols] += dot_nn(gl_v[:, part], slot[:, cols])
                dn_v[:, cols] += dot_nt(df_v[...], weight_v[cols, part])
                return carry

            lax.fori_loop(0, width // TILE, sums, 0)

        d_low[2] = acc_low[0].astype(bf)
        d_turned[2] = acc_turned[0].astype(bf)
        low_v[3] = acc_low[1].astype(bf)
        turned_v[3] = acc_turned[1].astype(bf)
        act_v, attn_v, dc_v = prompt_v.at[:rows], q_v, norm_v.at[:rows]

        def last_tile(j, carry):
            cols = tile(j)
            dn_v[prompt_rows:, cols] += dot_nn(d_low[2], down_v[:, tile(j, first=2 * width)])
            act_v[:prompt_rows, cols] = sum_v[:prompt_rows, cols].astype(bf)
            extra = dot_nn(low_v[3], up_v[:, tile(j, first=UP_FIRST[3])])
            act_v[prompt_rows:, cols] = (sum_v[prompt_rows:, cols] + extra).astype(bf)
            return carry

        lax.fori_loop(0, width // TILE, last_tile, 0)
        store(act_v, act_out)
        settle(q_store)

        def pull_rows(start):
            at = pl.ds(start, 128)
            grads = cot_ref[at].astype(f32) + norm_pull(h_v[at], dn_v[at], gains_ref[1:2])
            dn_v[at] = grads
            attn_v[at] = grads.astype(bf)

        for_blocks(rows, pull_rows)
        store(dn_v, dh_out)
        d_inner(1, attn_v[prompt_rows:], up_v[:, UP_FIRST[1] : UP_FIRST[2]])

        def context_tile(j, carry):
            cols = tile(j)
            wide = dot_nt(attn_v[...], w_out_v[cols])
            extra = dot_nn(d_low[1], down_v[:, tile(j, first=width)])
            dc_v[:prompt_rows, cols] = wide[:prompt_rows].astype(bf)
            dc_v[prompt_rows:, cols] = (wide[prompt_rows:] + extra).astype(bf)
            return carry

        lax.fori_loop(0, width // TILE, context_tile, 0)
        store(dc_v, dc_out)
        down_e[:, :width] = jnp.zeros((ADAPTER_RANK, width), bf)
        down_e[:, width : 2 * width] = dot_nn(d_turned[1], ctx_v[prompt_rows:]).astype(bf)
        down_e[:, 2 * width : 3 * width] = dot_nn(d_turned[2], n_v[prompt_rows:]).astype(bf)
        up_e[:, UP_FIRST[1] : UP_FIRST[2]] = dot_nn(turned_v[1], attn_v[prompt_rows:]).astype(bf)
        up_e[:, UP_FIRST[3] :] = dot_nn(turned_v[3], cot_ref[prompt_rows:]).astype(bf)
        for quarter in range(4):
            early_out[quarter, :, :QUARTER] = down_e[:, quarter * QUARTER : (quarter + 1) * QUARTER]
        for section in range(1, 4):
            size = UP_SECTIONS[section] // 4
            moved = jnp.zeros((64, size), f32)
            for part in range(4):
                first = UP_FIRST[section] + part * size
                moved += dot_nn(quarter_rows(64, 0, part, True), up_e[:, first : first + size])
            first = QUARTER + UP_STARTS[section] - UP_STARTS[1]
            for quarter in range(4):
                early_out[quarter, :, first : first + size] = moved[
                    16 * quarter : 16 * quarter + 16
                ].astype(bf)
        for ch in range(len(chunks)):
            finish(ch)
        for copy in stores:
            copy.wait()

    vmem = pl.BlockSpec(memory_space=pltpu.VMEM)
    hbm = pl.BlockSpec(memory_space=pl.ANY)
    return pl.pallas_call(
        kernel,
        in_specs=[pl.BlockSpec(memory_space=pltpu.SMEM)] + [vmem] * (3 + count),
        out_specs=[hbm] * 7 + [vmem] * 4 + [hbm] * count,
        out_shape=[
            jax.ShapeDtypeStruct((rows, width), bf),
            jax.ShapeDtypeStruct((keys, 2 * width), bf),
            jax.ShapeDtypeStruct((rows, width), bf),
            jax.ShapeDtypeStruct((rows, width), f32),
            jax.ShapeDtypeStruct((rows, width), bf),
            jax.ShapeDtypeStruct((rows, width), f32),
            jax.ShapeDtypeStruct((rows, width), bf),
            jax.ShapeDtypeStruct((4, 16, EARLY_COLS), bf),
            jax.ShapeDtypeStruct((ADAPTER_RANK, CONT_LEN), bf),
            jax.ShapeDtypeStruct((ADAPTER_RANK, width), bf),
            jax.ShapeDtypeStruct((ADAPTER_RANK, 3 * width), bf),
        ]
        + gathered,
        scratch_shapes=[
            pltpu.VMEM((prompt_total, width), bf),
            pltpu.VMEM((keys, width), bf),
            pltpu.VMEM((width, hidden_units), bf),
            pltpu.VMEM((width, width), bf),
            pltpu.VMEM((rows, width), bf),
            pltpu.VMEM((keys, 2 * width), bf),
            pltpu.VMEM((keys, 256), bf),
            pltpu.VMEM((rows, width), bf),
            pltpu.VMEM((rows, width), f32),
            pltpu.VMEM((rows, width), f32),
            pltpu.VMEM((rows, width), bf),
            pltpu.VMEM((rows, hidden_units), bf),
            pltpu.VMEM((rows, hidden_units), bf),
            pltpu.VMEM((rows, width), f32),
            pltpu.VMEM(gathered[1].shape, bf),
            pltpu.VMEM(gathered[2].shape, bf),
            pltpu.VMEM((ADAPTER_RANK, 4 * QUARTER), bf),
            pltpu.VMEM((ADAPTER_RANK, 4 * UP_QUARTER), bf),
            pltpu.VMEM((4, CONT_LEN, ADAPTER_RANK), bf),
            pltpu.VMEM((4, ADAPTER_RANK, CONT_LEN), bf),
            pltpu.VMEM((4, CONT_LEN, ADAPTER_RANK), bf),
            pltpu.VMEM((4, ADAPTER_RANK, CONT_LEN), bf),
            pltpu.VMEM((2, CONT_LEN, ADAPTER_RANK), f32),
            pltpu.VMEM((2, ADAPTER_RANK, CONT_LEN), f32),
            pltpu.VMEM((ADAPTER_RANK, 4 * QUARTER), bf),
            pltpu.VMEM((ADAPTER_RANK, 4 * UP_QUARTER), bf),
            dma((8,)),
            dma((8,)),
        ]
        + sems,
        compiler_params=pltpu.CompilerParams(
            collective_id=collective_id, has_side_effects=True, vmem_limit_bytes=VMEM_LIMIT
        ),
    )(ident, tokens, cotangent, gains, biases, *shards)


def adapter_scratch(cols):
    dma = pltpu.SemaphoreType.DMA
    return [
        pltpu.VMEM((2, 16, cols), jnp.bfloat16),
        pltpu.VMEM((16, 128), jnp.bfloat16),
        pltpu.VMEM((3, 4, 16, cols), jnp.bfloat16),
        pltpu.VMEM((3, 4, 16, cols), jnp.bfloat16),
        pltpu.VMEM((4, 16, cols), jnp.float32),
        pltpu.VMEM((3, 16, cols), jnp.bfloat16),
        pltpu.VMEM((3, 16, cols), jnp.bfloat16),
        dma((3,)),
        dma((3,)),
        dma((3,)),
        dma((3,)),
        dma((3,)),
        dma((3,)),
    ]


def adapter_stages(term_ref, id_ref, out_ref, scratch):
    from_core, other_id, to_grp, from_grp, total, to_z, from_z = scratch[:7]
    a_send, a_recv, g_send, g_recv, z_send, z_recv = scratch[7:]
    g, s = lax.axis_index("grp"), lax.axis_index("seq")
    core, z = lax.rem(s, 2), s // 2
    other = 1 - core
    partner = (g, z * 2 + other)
    grps = [lax.rem(g + d, 4) for d in range(1, 4)]
    lines = [lax.rem(z + d, 4) for d in range(1, 4)]

    def enter():
        peers = [partner] + [(far, s) for far in grps] + [(g, far * 2 + core) for far in lines]
        barrier = pltpu.get_barrier_semaphore()
        for peer in peers:
            pl.semaphore_signal(barrier, inc=1, device_id=peer, device_id_type=MESH)
        pl.semaphore_wait(barrier, len(peers))

    def remote(src, dst, send_sem, recv_sem, device):
        return pltpu.make_async_remote_copy(
            src_ref=src,
            dst_ref=dst,
            send_sem=send_sem,
            recv_sem=recv_sem,
            device_id=device,
            device_id_type=MESH,
        )

    copies_a = [
        remote(term_ref.at[i * 2 + other], from_core.at[i], a_send.at[i], a_recv.at[i], partner)
        for i in range(2)
    ] + [remote(id_ref, other_id, a_send.at[2], a_recv.at[2], partner)]
    copies_g = [
        remote(to_grp.at[d], from_grp.at[d], g_send.at[d], g_recv.at[d], (grps[d], s))
        for d in range(3)
    ]
    copies_z = [
        remote(to_z.at[d], from_z.at[d], z_send.at[d], z_recv.at[d], (g, lines[d] * 2 + core))
        for d in range(3)
    ]

    def start(copies):
        for copy in copies:
            copy.start()

    def wait(copies):
        for copy in copies:
            copy.wait()

    def select():
        wait(copies_a)
        mine = id_ref[0:1, 0:1].astype(jnp.float32)
        theirs = other_id[0:1, 0:1].astype(jnp.float32)
        for d, grp in enumerate(grps + [g]):
            for slot in range(4):
                adapter = (grp * 2 + slot // 2).astype(jnp.float32)
                own_term = term_ref[(slot % 2) * 2 + core].astype(jnp.float32)
                other_term = from_core[slot % 2].astype(jnp.float32)
                picked = jnp.where(mine == adapter, own_term, 0.0) + jnp.where(
                    theirs == adapter, other_term, 0.0
                )
                if d < 3:
                    to_grp[d, slot] = picked.astype(jnp.bfloat16)
                else:
                    total[slot] = picked

    def add_grps():
        wait(copies_g)
        for slot in range(4):
            total[slot] += sum(from_grp[d, slot].astype(jnp.float32) for d in range(3))
        for d in range(3):
            to_z[d] = total[lines[d]].astype(jnp.bfloat16)

    def add_lines():
        wait(copies_z)
        out_ref[...] = total[z] + sum(from_z[d].astype(jnp.float32) for d in range(3))

    return (
        enter,
        lambda: start(copies_a),
        select,
        lambda: start(copies_g),
        add_grps,
        lambda: start(copies_z),
        add_lines,
    )


LATE_COLS = MODEL_WIDTH + UP_STARTS[1]


def backward_tail(
    groups, q, kv, d_ctx, ctx, lse, early, ident, tokens, d_hidden, gains, biases, w_qkv, adapters,
    collective_id,
):
    rows, keys, pairs = q.shape[0], kv.shape[0], q.shape[1] // 128
    prompt_rows, prompt_total = rows - CONT_LEN, keys - CONT_LEN
    sizes = (prompt_rows, prompt_total, CONT_LEN)
    width, z_n = MODEL_WIDTH, groups[1] // 2
    bf, f32 = jnp.bfloat16, jnp.float32
    dma = pltpu.SemaphoreType.DMA
    adapter_shapes = len(adapter_scratch(128))

    def kernel(
        q_ref, k_ref, v_ref, d_ref, ctx_ref, lse_ref, early_ref, id_ref, tokens_ref, gains_ref,
        bias_ref, inner_ref, down_ref, up_ref, dh_hbm, w_hbm, *refs
    ):
        x_out, down_out, up_out = refs[:3]
        k_sum, v_sum, dqkv_v, term_v, pair_in, to_line, from_line = refs[3:10]
        w_v, dh_v, dn_v, n_v, late_v, early_sum, late_sum = refs[10:17]
        p_send, p_recv, l_send, l_recv, in_sem, out_sem = refs[17:23]
        scratch = refs[23:]
        e_enter, e_core, e_select, e_grp, e_add, e_z, e_lines = adapter_stages(
            early_ref, id_ref, early_sum, scratch[:adapter_shapes]
        )
        _, l_core, l_select, l_grp, l_add, l_z, l_lines = adapter_stages(
            late_v, id_ref, late_sum, scratch[adapter_shapes:]
        )
        g, s = lax.axis_index("grp"), lax.axis_index("seq")
        core, z = lax.rem(s, 2), s // 2
        far_z = [lax.rem(z + d, z_n) for d in range(1, z_n)]
        step = pl.program_id(0)

        def across(i):
            return pltpu.make_async_remote_copy(
                src_ref=term_v.at[i, 1 - core],
                dst_ref=pair_in.at[i],
                send_sem=p_send.at[i],
                recv_sem=p_recv.at[i],
                device_id=(g, z * 2 + 1 - core),
                device_id_type=MESH,
            )

        def along(i, d):
            return pltpu.make_async_remote_copy(
                src_ref=to_line.at[i, d],
                dst_ref=from_line.at[i, d],
                send_sem=l_send.at[i, d],
                recv_sem=l_recv.at[i, d],
                device_id=(g, far_z[d] * 2 + core),
                device_id_type=MESH,
            )

        def pass_on(i):
            across(i).wait()
            for d, far in enumerate(far_z):
                both = term_v[i, core, far].astype(f32) + pair_in[i, far].astype(f32)
                to_line[i, d] = both.astype(bf)
                along(i, d).start()

        load_w = pltpu.make_async_copy(w_hbm, w_v, in_sem.at[0])
        load_dh = pltpu.make_async_copy(dh_hbm, dh_v, in_sem.at[1])

        @pl.when(step == 0)
        def _():
            e_enter()
            e_core()
            load_w.start()
            load_dh.start()

        cols = pl.ds(pl.multiple_of(step * 128, 128), 128)
        attention_backward(
            sizes, q_ref, k_ref, v_ref, d_ref, ctx_ref, lse_ref, dqkv_v.at[:, cols], k_sum, v_sum
        )
        for block in range(2 * z_n):
            at = slice(block * prompt_rows, (block + 1) * prompt_rows)
            half = block % 2, block // 2
            term_v[step, half[0], half[1], :, :128] = (k_sum[at] * 0.125).astype(bf)
            term_v[step, half[0], half[1], :, 128:] = v_sum[at].astype(bf)
        across(step).start()
        for part, (total, scale) in enumerate(((k_sum, 0.125), (v_sum, 1.0))):
            to = pl.ds(pl.multiple_of(step * 128 + (part + 1) * width, 128), 128)
            dqkv_v[prompt_rows:, to] = (total[prompt_total:] * scale).astype(bf)

        @pl.when(step >= 1)
        def _():
            pass_on(step - 1)

        @pl.when(step == 1)
        def _():
            e_select()
            e_grp()

            def read(start):
                return tokens_ref[pl.ds(pl.multiple_of(start + prompt_rows, 128), 128)].astype(f32)

            def write(start, values):
                n_v[pl.ds(start, 128)] = values

            normalize_rows(read, write, CONT_LEN, gains_ref[0:1], bias_ref[:, :width])

        @pl.when(step == pairs // 2)
        def _():
            e_add()
            e_z()

        @pl.when(step == pairs - 1)
        def _():
            later = dqkv_v[prompt_rows:]
            d_low = dot_nt(later, up_ref[...]).astype(bf)
            d_turned = dot_nt(up_ref[...], later).astype(bf)
            late_v[...] = jnp.zeros(late_v.shape, bf)
            late_v[0, :, :width] = dot_nn(d_turned, n_v[...]).astype(bf)
            size = UP_SECTIONS[0] // 4
            moved = jnp.zeros((64, size), f32)
            for part in range(4):
                grads = dot_nn(inner_ref[...], dqkv_v[prompt_rows:, part * size : (part + 1) * size])
                moved += dot_nn(quarter_rows(64, 0, part, True), grads.astype(bf))
            for quarter in range(4):
                late_v[quarter, :, width:] = moved[16 * quarter : 16 * quarter + 16].astype(bf)
            l_core()
            pass_on(pairs - 1)
            load_w.wait()
            load_dh.wait()

            def pull(first, count):
                def body(start):
                    at = pl.ds(pl.multiple_of(start + first, 128), 128)
                    values = tokens_ref[at].astype(f32)
                    dn_v[at] = dh_v[at] + norm_pull(values, dn_v[at], gains_ref[0:1])

                for_blocks(count, body)
                copy = pltpu.make_async_copy(
                    dn_v.at[first : first + count], x_out.at[first : first + count],
                    out_sem.at[0 if first else 1],
                )
                copy.start()
                return copy

            def later_tile(j, carry):
                to = pl.ds(pl.multiple_of(j * TILE, TILE), TILE)
                wide = dot_nt(dqkv_v[prompt_rows:], w_v[to]) + dot_nn(d_low, down_ref[:, to])
                dn_v[prompt_rows:, to] = wide
                return carry

            lax.fori_loop(0, width // TILE, later_tile, 0)
            l_select()
            l_grp()
            later_store = pull(prompt_rows, CONT_LEN)
            e_lines()

            def arrived(i, carry):
                total = term_v[i, core, z].astype(f32) + pair_in[i, z].astype(f32)
                for d in range(z_n - 1):
                    along(i, d).wait()
                    total = total + from_line[i, d].astype(f32)
                for part in range(2):
                    to = pl.ds(pl.multiple_of(i * 128 + (part + 1) * width, 128), 128)
                    dqkv_v[:prompt_rows, to] = total[:, part * 128 : part * 128 + 128].astype(bf)
                return carry

            lax.fori_loop(0, pairs, arrived, 0)
            l_add()
            l_z()

            def prompt_tile(j, carry):
                to = pl.ds(pl.multiple_of(j * TILE, TILE), TILE)
                dn_v[:prompt_rows, to] = dot_nt(dqkv_v[:prompt_rows], w_v[to])
                return carry

            lax.fori_loop(0, width // TILE, prompt_tile, 0)
            prompt_store = pull(0, prompt_rows)
            l_lines()
            down_out[:, :width] = early_sum[:, :width] + late_sum[:, :width]
            down_out[:, width:] = early_sum[:, width:QUARTER]
            up_out[:, : UP_STARTS[1]] = late_sum[:, width:]
            up_out[:, UP_STARTS[1] :] = early_sum[:, QUARTER:]
            later_store.wait()
            prompt_store.wait()

    def pair(i):
        return (0, i)

    row_spec = pl.BlockSpec((rows, 128), pair)
    key_spec = pl.BlockSpec((keys, 128), pair)
    whole = pl.BlockSpec(memory_space=pltpu.VMEM)
    hbm = pl.BlockSpec(memory_space=pl.ANY)
    return pl.pallas_call(
        kernel,
        grid=(pairs,),
        in_specs=[
            row_spec,
            key_spec,
            pl.BlockSpec((keys, 128), lambda i: (0, pairs + i)),
            row_spec,
            row_spec,
            row_spec,
        ]
        + [whole] * 8
        + [hbm] * 2,
        out_specs=[hbm, whole, whole],
        out_shape=[
            jax.ShapeDtypeStruct((rows, width), f32),
            jax.ShapeDtypeStruct((16, QUARTER), f32),
            jax.ShapeDtypeStruct((16, UP_QUARTER), f32),
        ],
        scratch_shapes=[
            pltpu.VMEM((keys, 128), f32),
            pltpu.VMEM((keys, 128), f32),
            pltpu.VMEM((rows, 3 * width), bf),
            pltpu.VMEM((pairs, 2, z_n, prompt_rows, 256), bf),
            pltpu.VMEM((pairs, z_n, prompt_rows, 256), bf),
            pltpu.VMEM((pairs, z_n - 1, prompt_rows, 256), bf),
            pltpu.VMEM((pairs, z_n - 1, prompt_rows, 256), bf),
            pltpu.VMEM((width, 3 * width), bf),
            pltpu.VMEM((rows, width), f32),
            pltpu.VMEM((rows, width), f32),
            pltpu.VMEM((CONT_LEN, width), bf),
            pltpu.VMEM((4, 16, LATE_COLS), bf),
            pltpu.VMEM((16, EARLY_COLS), f32),
            pltpu.VMEM((16, LATE_COLS), f32),
            dma((pairs,)),
            dma((pairs,)),
            dma((pairs, z_n - 1)),
            dma((pairs, z_n - 1)),
            dma((2,)),
            dma((2,)),
        ]
        + adapter_scratch(EARLY_COLS)
        + adapter_scratch(LATE_COLS),
        compiler_params=pltpu.CompilerParams(
            collective_id=collective_id, has_side_effects=True, vmem_limit_bytes=VMEM_LIMIT
        ),
    )(
        q, kv, kv, d_ctx, ctx, lse, early, ident, tokens, gains, biases, *adapters, d_hidden, w_qkv
    )


def local_general(
    tokens,
    cotangent,
    query_key_value_weight,
    attention_out_weight,
    feedforward_in_weight,
    feedforward_out_weight,
    layer_norm_gains,
    biases,
    adapter_down_matrices,
    adapter_up_matrices,
    adapter_of_continuation,
):
    row_count = tokens.shape[0]
    prompt_rows = row_count - CONT_LEN
    prompt_total = prompt_rows * lax.axis_size("seq")
    key_count = prompt_total + CONT_LEN
    seq_index = lax.axis_index("seq")
    adapter_index = adapter_of_continuation[0, 0]
    weight_shards = (
        query_key_value_weight,
        attention_out_weight,
        feedforward_in_weight,
        feedforward_out_weight,
        adapter_down_matrices,
        adapter_up_matrices,
    )
    gathered_rows = (
        lax.all_gather(weight_shards[0], ("grp", "seq"), axis=0, tiled=True),
        lax.all_gather(weight_shards[1], ("grp", "seq"), axis=0, tiled=True),
        lax.all_gather(weight_shards[2], ("grp", "seq"), axis=0, tiled=True),
        lax.all_gather(weight_shards[3], ("grp", "seq"), axis=0, tiled=True),
        lax.all_gather(weight_shards[4], ("grp", "seq"), axis=0, tiled=True),
        lax.all_gather(weight_shards[5], ("grp", "seq"), axis=0, tiled=True),
    )
    weight_matrices, adapter_sections = unpack_sections(gathered_rows, adapter_index)
    frozen_query_key_value, frozen_attention_out, frozen_feedforward_in, frozen_feedforward_out = (
        weight_matrices
    )
    (
        down_query_key_value,
        down_attention_out,
        down_feedforward_in,
        down_feedforward_out,
        up_query_key_value,
        up_attention_out,
        up_feedforward_in,
        up_feedforward_out,
    ) = adapter_sections
    shift_one = biases[:MODEL_WIDTH]
    shift_two = biases[MODEL_WIDTH : 2 * MODEL_WIDTH]
    query_key_value_bias = jnp.concatenate(
        [
            biases[2 * MODEL_WIDTH : 3 * MODEL_WIDTH],
            jnp.zeros((MODEL_WIDTH,), jnp.float32),
            biases[3 * MODEL_WIDTH : 4 * MODEL_WIDTH],
        ]
    )
    bias_out = biases[4 * MODEL_WIDTH : 5 * MODEL_WIDTH]
    bias_proj = biases[5 * MODEL_WIDTH : 6 * MODEL_WIDTH]
    bias_fc = biases[6 * MODEL_WIDTH :]
    inputs = tokens.astype(jnp.float32)
    normed_one = layer_norm(inputs, layer_norm_gains[0], shift_one).astype(jnp.bfloat16)
    inner_one = product(normed_one[prompt_rows:], down_query_key_value).astype(jnp.bfloat16)
    mixed_query_key_value = product(normed_one, frozen_query_key_value) + query_key_value_bias
    mixed_query_key_value = mixed_query_key_value.at[prompt_rows:].add(
        product(inner_one, up_query_key_value)
    )
    qkv_rows = mixed_query_key_value.astype(jnp.bfloat16)
    prompt_keys, prompt_values = (
        lax.all_gather(
            qkv_rows[:prompt_rows, MODEL_WIDTH : 2 * MODEL_WIDTH], "seq", axis=0, tiled=True
        ),
        lax.all_gather(qkv_rows[:prompt_rows, 2 * MODEL_WIDTH :], "seq", axis=0, tiled=True),
    )
    all_keys = jnp.concatenate(
        [prompt_keys, qkv_rows[prompt_rows:, MODEL_WIDTH : 2 * MODEL_WIDTH]], 0
    )
    all_values = jnp.concatenate([prompt_values, qkv_rows[prompt_rows:, 2 * MODEL_WIDTH :]], 0)
    allowed = visible(row_count, prompt_rows, prompt_total, key_count, seq_index)
    query_heads = split_heads(qkv_rows[:, :MODEL_WIDTH])
    key_heads = split_heads(all_keys)
    value_heads = split_heads(all_values)

    def forward_head(operands):
        query_head, key_head, value_head = operands
        scores = jnp.where(allowed, product_nt(query_head, key_head) * 0.125, NEGATIVE)
        row_max = jnp.max(scores, axis=1, keepdims=True)
        exp_scores = jnp.exp(scores - row_max)
        exp_total = jnp.sum(exp_scores, axis=1, keepdims=True)
        weights = (exp_scores / exp_total).astype(jnp.bfloat16)
        return (product(weights, value_head), (row_max + jnp.log(exp_total))[:, 0])

    head_contexts, log_total = lax.map(forward_head, (query_heads, key_heads, value_heads))
    attention_context = merge_heads(head_contexts).astype(jnp.bfloat16)
    inner_two = product(attention_context[prompt_rows:], down_attention_out).astype(jnp.bfloat16)
    attention_output = product(attention_context, frozen_attention_out) + bias_out
    attention_output = attention_output.at[prompt_rows:].add(product(inner_two, up_attention_out))
    hidden = inputs + attention_output
    normed_two = layer_norm(hidden, layer_norm_gains[1], shift_two).astype(jnp.bfloat16)
    inner_three = product(normed_two[prompt_rows:], down_feedforward_in).astype(jnp.bfloat16)
    before_activation = product(normed_two, frozen_feedforward_in) + bias_fc
    before_activation = before_activation.at[prompt_rows:].add(
        product(inner_three, up_feedforward_in)
    )
    activated_hidden = jax.nn.gelu(before_activation, approximate=True).astype(jnp.bfloat16)
    inner_four = product(activated_hidden[prompt_rows:], down_feedforward_out).astype(jnp.bfloat16)
    adapter_branch = product(activated_hidden, frozen_feedforward_out) + bias_proj
    adapter_branch = adapter_branch.at[prompt_rows:].add(product(inner_four, up_feedforward_out))
    outputs = (hidden + adapter_branch).astype(jnp.bfloat16)
    weight_matrices, adapter_sections = unpack_sections(
        (
            lax.all_gather(weight_shards[0], ("grp", "seq"), axis=0, tiled=True),
            lax.all_gather(weight_shards[1], ("grp", "seq"), axis=0, tiled=True),
            lax.all_gather(weight_shards[2], ("grp", "seq"), axis=0, tiled=True),
            lax.all_gather(weight_shards[3], ("grp", "seq"), axis=0, tiled=True),
            lax.all_gather(weight_shards[4], ("grp", "seq"), axis=0, tiled=True),
            lax.all_gather(weight_shards[5], ("grp", "seq"), axis=0, tiled=True),
        ),
        adapter_index,
    )
    frozen_query_key_value, frozen_attention_out, frozen_feedforward_in, frozen_feedforward_out = (
        weight_matrices
    )
    (
        down_query_key_value,
        down_attention_out,
        down_feedforward_in,
        down_feedforward_out,
        up_query_key_value,
        up_attention_out,
        up_feedforward_in,
        up_feedforward_out,
    ) = adapter_sections
    grad_inner_four = product_nt(cotangent[prompt_rows:], up_feedforward_out).astype(jnp.bfloat16)
    grad_act = product_nt(cotangent, frozen_feedforward_out)
    grad_act = grad_act.at[prompt_rows:].add(product_nt(grad_inner_four, down_feedforward_out))
    gelu_pull = jax.vjp(lambda field: jax.nn.gelu(field, approximate=True), before_activation)[1]
    grad_pre = gelu_pull(grad_act)[0].astype(jnp.bfloat16)
    grad_inner_three = product_nt(grad_pre[prompt_rows:], up_feedforward_in).astype(jnp.bfloat16)
    grad_normed_two = product_nt(grad_pre, frozen_feedforward_in)
    grad_normed_two = grad_normed_two.at[prompt_rows:].add(
        product_nt(grad_inner_three, down_feedforward_in)
    )
    second_pull = jax.vjp(lambda field: layer_norm(field, layer_norm_gains[1], shift_two), hidden)[
        1
    ]
    grad_hidden = cotangent.astype(jnp.float32) + second_pull(grad_normed_two)[0]
    grad_attn = grad_hidden.astype(jnp.bfloat16)
    grad_inner_two = product_nt(grad_attn[prompt_rows:], up_attention_out).astype(jnp.bfloat16)
    grad_context = product_nt(grad_attn, frozen_attention_out)
    grad_context = (
        grad_context.at[prompt_rows:]
        .add(product_nt(grad_inner_two, down_attention_out))
        .astype(jnp.bfloat16)
    )

    def backward_head(operands):
        query_head, key_head, value_head, grad_head, total_head = operands
        scores = jnp.where(allowed, product_nt(query_head, key_head) * 0.125, NEGATIVE)
        prob_full = jnp.exp(scores - total_head[:, None])
        weights = prob_full.astype(jnp.bfloat16)
        grad_weights = product_nt(grad_head, value_head)
        row_delta = jnp.sum(prob_full * grad_weights, axis=1, keepdims=True)
        grad_scores = (prob_full * (grad_weights - row_delta)).astype(jnp.bfloat16)
        return (
            product(grad_scores, key_head) * 0.125,
            product_tn(grad_scores, query_head) * 0.125,
            product_tn(weights, grad_head),
        )

    grad_q, grad_k, grad_v = lax.map(
        backward_head, (query_heads, key_heads, value_heads, split_heads(grad_context), log_total)
    )
    grad_query = merge_heads(grad_q)
    grad_keys = merge_heads(grad_k)
    grad_values = merge_heads(grad_v)
    own_keys, own_values = (
        lax.psum_scatter(
            grad_keys[:prompt_total].astype(jnp.bfloat16), "seq", scatter_dimension=0, tiled=True
        ).astype(jnp.float32),
        lax.psum_scatter(
            grad_values[:prompt_total].astype(jnp.bfloat16), "seq", scatter_dimension=0, tiled=True
        ).astype(jnp.float32),
    )
    grad_qkv = jnp.concatenate(
        [
            grad_query,
            jnp.concatenate([own_keys, grad_keys[prompt_total:]], 0),
            jnp.concatenate([own_values, grad_values[prompt_total:]], 0),
        ],
        1,
    ).astype(jnp.bfloat16)
    grad_inner_one = product_nt(grad_qkv[prompt_rows:], up_query_key_value).astype(jnp.bfloat16)
    grad_normed_one = product_nt(grad_qkv, frozen_query_key_value)
    grad_normed_one = grad_normed_one.at[prompt_rows:].add(
        product_nt(grad_inner_one, down_query_key_value)
    )
    first_pull = jax.vjp(lambda field: layer_norm(field, layer_norm_gains[0], shift_one), inputs)[1]
    input_grad = grad_hidden + first_pull(grad_normed_one)[0]
    down_term = jnp.concatenate(
        [
            product_tn(normed_one[prompt_rows:], grad_inner_one),
            product_tn(attention_context[prompt_rows:], grad_inner_two),
            product_tn(normed_two[prompt_rows:], grad_inner_three),
            product_tn(activated_hidden[prompt_rows:], grad_inner_four),
        ],
        0,
    )
    up_term = jnp.concatenate(
        [
            product_tn(inner_one, grad_qkv[prompt_rows:]),
            product_tn(inner_two, grad_attn[prompt_rows:]),
            product_tn(inner_three, grad_pre[prompt_rows:]),
            product_tn(inner_four, cotangent[prompt_rows:]),
        ],
        1,
    )
    select = (jnp.arange(ADAPTER_COUNT, dtype=jnp.int32) == adapter_index).astype(jnp.float32)
    down_grad, up_grad = (
        lax.psum_scatter(
            (select[:, None, None] * down_term[None]).reshape(-1),
            ("grp", "seq"),
            scatter_dimension=0,
            tiled=True,
        ),
        lax.psum_scatter(
            (select[:, None, None] * up_term[None]).reshape(-1),
            ("grp", "seq"),
            scatter_dimension=0,
            tiled=True,
        ),
    )
    return (outputs, input_grad, down_grad, up_grad)


def fast(
    tokens,
    cotangent,
    query_key_value_weight,
    attention_out_weight,
    feedforward_in_weight,
    feedforward_out_weight,
    layer_norm_gains,
    biases,
    adapter_down_matrices,
    adapter_up_matrices,
    adapter_of_continuation,
):
    groups = (lax.axis_size("grp"), lax.axis_size("seq"))
    up_cols = 5 * MODEL_WIDTH + HIDDEN_UNITS
    ups_shard = adapter_up_matrices.reshape(4, up_cols)
    up_parts, first = [], 0
    for size in UP_SECTIONS:
        up_parts.append(ups_shard[:, first : first + size].reshape(16, size // 4))
        first += size
    (
        queries,
        keys_values,
        context,
        log_total,
        outputs,
        grad_hidden,
        grad_context,
        early_term,
        inner_one,
        down_qkv,
        up_qkv,
        _,
        _,
        _,
        w_qkv,
        _,
        _,
        _,
    ) = forward_and_gather(
        groups,
        adapter_of_continuation,
        tokens,
        cotangent,
        layer_norm_gains,
        biases.reshape(1, -1),
        [
            adapter_down_matrices.reshape(-1, ADAPTER_RANK).T,
            jnp.concatenate(up_parts, 1),
            query_key_value_weight.reshape(-1, 3 * MODEL_WIDTH),
            attention_out_weight.reshape(-1, MODEL_WIDTH),
            feedforward_in_weight.reshape(-1, HIDDEN_UNITS),
            feedforward_out_weight.reshape(-1, MODEL_WIDTH),
        ],
        1,
    )
    ident = jnp.full((16, 128), adapter_of_continuation[0, 0], jnp.int32).astype(jnp.bfloat16)
    input_grad, down_grad, up_grad = backward_tail(
        groups,
        queries,
        keys_values,
        grad_context,
        context,
        log_total,
        early_term,
        ident,
        tokens,
        grad_hidden,
        layer_norm_gains,
        biases.reshape(1, -1),
        w_qkv,
        (inner_one, down_qkv, up_qkv),
        3,
    )
    down_grad = down_grad.T.reshape(-1)
    up_pieces = []
    for start, size in zip(UP_STARTS, UP_SECTIONS):
        up_pieces.append(up_grad[:, start : start + size // 4].reshape(4, -1))
    up_grad = jnp.concatenate(up_pieces, 1).reshape(-1)
    return (outputs, input_grad, down_grad, up_grad)


def solution(mesh):
    placed = (
        P(("grp", "seq"), None),
        P(("grp", "seq"), None),
        P(("grp", "seq")),
        P(("grp", "seq")),
        P(("grp", "seq")),
        P(("grp", "seq")),
        P(),
        P(),
        P(("grp", "seq")),
        P(("grp", "seq")),
        P(("grp", "seq"), None),
    )
    fits = mesh.shape["grp"] == 4 and mesh.shape["seq"] == 8
    return jax.shard_map(
        fast if fits else local_general,
        mesh=mesh,
        in_specs=placed,
        out_specs=(
            P(("grp", "seq"), None),
            P(("grp", "seq"), None),
            P(("grp", "seq")),
            P(("grp", "seq")),
        ),
        check_vma=False,
    )
```

```python
import functools

import jax
import jax.numpy as jnp
from jax import lax
from jax.experimental import pallas as pl
from jax.experimental.pallas import tpu as pltpu
from jax.sharding import PartitionSpec as P

MODEL_WIDTH = 1024
HEADS = 16
HEAD_DIM = 64
HIDDEN_UNITS = 4096
ADAPTER_RANK = 16
ADAPTER_COUNT = 8
CONT_LEN = 512


EPSILON = 1e-05
NEGATIVE = -1e30


def product(left_side, right_side):
    return jnp.dot(left_side, right_side, preferred_element_type=jnp.float32)


def product_tn(left_side, right_side):
    return lax.dot_general(
        left_side, right_side, (((0,), (0,)), ((), ())), preferred_element_type=jnp.float32
    )


def product_nt(left_side, right_side):
    return lax.dot_general(
        left_side, right_side, (((1,), (1,)), ((), ())), preferred_element_type=jnp.float32
    )


def layer_norm(values, gain_vec, shift_vec):
    row_mean = jnp.mean(values, axis=-1, keepdims=True)
    centred = values - row_mean
    row_var = jnp.mean(centred * centred, axis=-1, keepdims=True)
    return centred * lax.rsqrt(row_var + EPSILON) * gain_vec + shift_vec


def unpack_sections(pieces, adapter_index):
    qkv_flat, out_flat, fc_flat, proj_flat, down_flat, up_flat = pieces
    every_down_matrix = down_flat.reshape(
        ADAPTER_COUNT, 3 * MODEL_WIDTH + HIDDEN_UNITS, ADAPTER_RANK
    )
    every_up_matrix = up_flat.reshape(ADAPTER_COUNT, ADAPTER_RANK, 5 * MODEL_WIDTH + HIDDEN_UNITS)
    down_rows = lax.dynamic_index_in_dim(every_down_matrix, adapter_index, 0, keepdims=False)
    up_cols = lax.dynamic_index_in_dim(every_up_matrix, adapter_index, 0, keepdims=False)
    weight_matrices = (
        qkv_flat.reshape(MODEL_WIDTH, 3 * MODEL_WIDTH),
        out_flat.reshape(MODEL_WIDTH, MODEL_WIDTH),
        fc_flat.reshape(MODEL_WIDTH, HIDDEN_UNITS),
        proj_flat.reshape(HIDDEN_UNITS, MODEL_WIDTH),
    )
    adapter_sections = (
        down_rows[:MODEL_WIDTH],
        down_rows[MODEL_WIDTH : 2 * MODEL_WIDTH],
        down_rows[2 * MODEL_WIDTH : 3 * MODEL_WIDTH],
        down_rows[3 * MODEL_WIDTH :],
        up_cols[:, : 3 * MODEL_WIDTH],
        up_cols[:, 3 * MODEL_WIDTH : 4 * MODEL_WIDTH],
        up_cols[:, 4 * MODEL_WIDTH : 4 * MODEL_WIDTH + HIDDEN_UNITS],
        up_cols[:, 4 * MODEL_WIDTH + HIDDEN_UNITS :],
    )
    return (weight_matrices, adapter_sections)


def visible(row_count, prompt_rows, prompt_total, key_count, seq_index):
    row_ids = jnp.arange(row_count, dtype=jnp.int32)[:, None]
    col_ids = jnp.arange(key_count, dtype=jnp.int32)[None, :]
    in_prompt = col_ids < prompt_total
    prompt_seen = in_prompt & (col_ids <= seq_index * prompt_rows + row_ids)
    later_seen = in_prompt | (col_ids - prompt_total <= row_ids - prompt_rows)
    return jnp.where(row_ids < prompt_rows, prompt_seen, later_seen)


def split_heads(values):
    return values.reshape(values.shape[0], HEADS, HEAD_DIM).transpose(1, 0, 2)


def merge_heads(values):
    return values.transpose(1, 0, 2).reshape(values.shape[1], HEADS * HEAD_DIM)


MESH = pl.DeviceIdType.MESH
SCALE2 = 0.125 * 1.4426950408889634
VMEM_LIMIT = 63 << 20


def gather_stages(groups, sizes, chunks, ins, outs, sems):
    grp_n, seq_n = groups
    z_n, y_n = seq_n // 2, grp_n // 2
    z_sem, x_sem, y_sem, d_sem, p_sem, s_sem, l_sem = sems
    g, s = lax.axis_index("grp"), lax.axis_index("seq")
    core, z = lax.rem(s, 2), s // 2
    gx, gy = lax.rem(g, 2), g // 2
    partner = (g, z * 2 + 1 - core)
    other_x = gy * 2 + 1 - gx
    x_next = (other_x, s)
    far_z = [lax.rem(z + d, z_n) for d in range(1, z_n)]
    far_y = [lax.rem(gy + d, y_n) for d in range(1, y_n)]
    y_next = [(y * 2 + gx, s) for y in far_y]

    def enter():
        peers = [partner, x_next] + y_next + [(g, far * 2 + core) for far in far_z]
        barrier = pltpu.get_barrier_semaphore()
        for peer in peers:
            pl.semaphore_signal(barrier, inc=1, device_id=peer, device_id_type=MESH)
        pl.semaphore_wait(barrier, len(peers))

    def place(ch, gg, ss):
        arr, row, rows, col, cols, full = chunks[ch]
        block = gg * seq_n + ss if full else ss
        at = pl.ds(pl.multiple_of(block * sizes[arr] + row, 16), rows)
        return outs[arr].at[at, pl.ds(col, cols)]

    def send(ch, src, gg, ss, sem, device):
        pltpu.make_async_remote_copy(
            src_ref=src,
            dst_ref=place(ch, gg, ss),
            send_sem=s_sem.at[ch],
            recv_sem=sem,
            device_id=device,
            device_id_type=MESH,
        ).start()

    def drain(ch, sem, count=1):
        arr, _, rows, col, cols, _ = chunks[ch]
        block = outs[arr].at[pl.ds(0, count * rows), pl.ds(col, cols)]
        pltpu.make_async_copy(block, block, sem).wait()

    def each(first, last, body):
        def step(i, carry):
            body(i)
            return carry

        lax.fori_loop(first, last, step, 0)

    def shard(ch):
        arr, row, rows, col, cols, _ = chunks[ch]
        return ins[arr].at[pl.ds(row, rows), pl.ds(col, cols)]

    def own(ch):
        src = shard(ch)

        def to_line(d):
            send(ch, src, g, s, z_sem.at[ch, z], (g, lax.rem(z + d, z_n) * 2 + core))

        each(1, z_n, to_line)
        send(ch, src, g, s, p_sem.at[ch, 0], partner)
        pltpu.make_async_copy(src, place(ch, g, s), l_sem.at[ch]).start()

    def near(ch):
        src = shard(ch)
        send(ch, src, g, s, x_sem.at[ch, z], x_next)
        for peer in y_next:
            send(ch, src, g, s, y_sem.at[ch, gy, z], peer)

    def line(ch):
        def relay(d):
            far = lax.rem(z + d, z_n)
            drain(ch, z_sem.at[ch, far])
            from_s = far * 2 + core
            src = place(ch, g, from_s)
            if chunks[ch][5]:
                send(ch, src, g, from_s, x_sem.at[ch, far], x_next)
                for peer in y_next:
                    send(ch, src, g, from_s, y_sem.at[ch, gy, far], peer)
            send(ch, src, g, from_s, p_sem.at[ch, 0], partner)

        each(1, z_n, relay)

    def side(ch):
        if not chunks[ch][5]:
            return

        def relay(half):
            for odd in range(2):
                far = half * 2 + odd
                from_s = far * 2 + core
                drain(ch, x_sem.at[ch, far])
                src = place(ch, other_x, from_s)
                if not odd:
                    for peer in y_next:
                        send(ch, src, other_x, from_s, d_sem.at[ch, gy, far], peer)
                send(ch, src, other_x, from_s, p_sem.at[ch, 1], partner)
                for y in far_y:
                    drain(ch, y_sem.at[ch, y, far])
                    from_g = y * 2 + gx
                    src = place(ch, from_g, from_s)
                    if odd:
                        send(ch, src, from_g, from_s, d_sem.at[ch, y, far], x_next)
                    send(ch, src, from_g, from_s, p_sem.at[ch, 2], partner)

        each(0, z_n // 2, relay)

    def corner(ch):
        if not chunks[ch][5]:
            return

        def relay(far):
            from_s = far * 2 + core
            for y in far_y:
                drain(ch, d_sem.at[ch, y, far])
                from_g = y * 2 + 1 - gx
                src = place(ch, from_g, from_s)
                send(ch, src, from_g, from_s, p_sem.at[ch, 3], partner)

        each(0, z_n, relay)

    def ready_kind(ch, kind):
        drain(ch, p_sem.at[ch, kind], z_n)
        pl.when(kind == 0)(lambda: drain(ch, l_sem.at[ch]))

    def ready(ch, kinds=range(4)):
        for kind in kinds if chunks[ch][5] else (0,):
            drain(ch, p_sem.at[ch, kind], z_n * (y_n - 1 if kind >= 2 else 1))
            if kind == 0:
                drain(ch, l_sem.at[ch])

    def finish(ch):
        sends = 2 * z_n - 1
        if chunks[ch][5]:
            sends += z_n * y_n
            sends += z_n * (y_n - 1)
            sends += z_n * (2 * y_n - 1)
        drain(ch, s_sem.at[ch], sends)

    steps = {"own": own, "near": near, "line": line, "side": side, "corner": corner}

    def tick(t):
        for step, which in GATHER_ORDER[t]:
            for ch in which:
                steps[step](ch)

    return enter, tick, ready, ready_kind, finish


def gather_plan(groups, shards, chunks):
    grp_n, seq_n = groups
    shapes = []
    for rows, cols, full in shards:
        total = (grp_n if full else 1) * seq_n * rows
        shapes.append(jax.ShapeDtypeStruct((total, cols), jnp.bfloat16))
    chunks = [chunk + (shards[chunk[0]][2],) for chunk in chunks]
    dma, count = pltpu.SemaphoreType.DMA, len(chunks)
    sems = [
        dma((count, seq_n // 2)),
        dma((count, seq_n // 2)),
        dma((count, grp_n // 2, seq_n // 2)),
        dma((count, grp_n // 2, seq_n // 2)),
        dma((count, 4)),
        dma((count,)),
        dma((count,)),
    ]
    return [rows for rows, _, _ in shards], chunks, shapes, sems


GATHER_ORDER = (
    (("own", (0, 1, 2, 3)), ("near", (1, 2, 3, 4, 5, 6, 7, 8))),
    (("own", (4, 5)), ("near", (9, 10, 11, 12, 13, 14)), ("line", (0,))),
    (("own", (6,)), ("line", (1,))),
    (("own", (7,)), ("line", (2,))),
    (("side", (1,)), ("line", (3,))),
    (("corner", (1,)), ("side", (2,)), ("line", (4,))),
    (("corner", (2,)), ("side", (3,)), ("line", (5,))),
    (("own", (8,)), ("corner", (3,)), ("side", (4,)), ("line", (6,))),
    (("own", (9,)), ("corner", (4,)), ("side", (5,)), ("line", (7,))),
    (("own", (10,)), ("corner", (5,)), ("side", (6,)), ("line", (8,))),
    (("own", (11,)), ("corner", (6,)), ("side", (7,))),
    (("line", (9,)),),
    (("own", (12,)), ("corner", (7,)), ("side", (8,))),
    (("line", (10,)),),
    (("own", (13,)), ("corner", (8,)), ("side", (9,))),
    (("line", (11,)),),
    (("own", (14,)), ("corner", (9,)), ("side", (10,))),
    (("line", (12,)),),
    (("corner", (10,)), ("side", (11,))),
    (("line", (13,)),),
    (("corner", (11,)), ("side", (12,))),
    (("line", (14,)),),
    (("corner", (12,)), ("side", (13,))),
    (("corner", (13,)), ("side", (14,))),
    (("corner", (14,)),),
)


def dot_nt(left, right):
    return lax.dot_general(
        left, right, (((1,), (1,)), ((), ())), preferred_element_type=jnp.float32
    )


def dot_nn(left, right):
    return lax.dot_general(
        left, right, (((1,), (0,)), ((), ())), preferred_element_type=jnp.float32
    )


def stacked_heads(pair):
    first = lax.broadcasted_iota(jnp.int32, pair.shape, 1) < HEAD_DIM
    zero = jnp.zeros_like(pair)
    return jnp.concatenate([jnp.where(first, pair, zero), jnp.where(first, zero, pair)], 0)


def row_groups(prompt_rows, prompt_total, later_rows):
    block = min(256, later_rows)
    return [(prompt_rows + i, block, prompt_total + i) for i in range(0, later_rows, block)]


def attention_forward(sizes, q_ref, k_ref, v_ref, ctx_ref, lse_ref, wide_ref):
    prompt_rows, prompt_total, later_rows = sizes
    seq = lax.axis_index("seq")
    wide_ref[:, :128] = v_ref[...]
    wide_ref[:, 128:] = jnp.ones((prompt_total + later_rows, 128), jnp.bfloat16)

    def finish(start, rows, row_max, summed):
        total = summed[:, 128:]
        mixed = summed[:, :128] / total
        log_total = row_max * SCALE2 + jnp.log2(total)
        first = lax.broadcasted_iota(jnp.int32, (rows, 128), 1) < HEAD_DIM
        ctx_ref[start : start + rows] = jnp.where(first, mixed[:rows], mixed[rows:]).astype(
            jnp.bfloat16
        )
        lse_ref[start : start + rows] = jnp.where(first, log_total[:rows], log_total[rows:])

    for start, rows, free in row_groups(prompt_rows, prompt_total, later_rows):
        queries = stacked_heads(q_ref[start : start + rows])
        open_scores = dot_nt(queries, k_ref[:free])
        edge_scores = dot_nt(queries, k_ref[free : free + rows])
        row = lax.broadcasted_iota(jnp.int32, (rows, rows), 0)
        key = lax.broadcasted_iota(jnp.int32, (rows, rows), 1)
        seen = key <= row
        edge_scores = jnp.where(jnp.concatenate([seen, seen], 0), edge_scores, NEGATIVE)
        row_max = jnp.maximum(
            jnp.max(open_scores, 1, keepdims=True), jnp.max(edge_scores, 1, keepdims=True)
        )
        scaled = row_max * SCALE2
        open_p = jnp.exp2(open_scores * SCALE2 - scaled).astype(jnp.bfloat16)
        edge_p = jnp.exp2(edge_scores * SCALE2 - scaled).astype(jnp.bfloat16)
        summed = dot_nn(open_p, wide_ref[:free]) + dot_nn(edge_p, wide_ref[free : free + rows])
        finish(start, rows, row_max, summed)
    scores = dot_nt(stacked_heads(q_ref[:prompt_rows]), k_ref[:prompt_total])
    row = lax.broadcasted_iota(jnp.int32, (prompt_rows, prompt_total), 0)
    key = lax.broadcasted_iota(jnp.int32, (prompt_rows, prompt_total), 1)
    seen = key <= row + seq * prompt_rows
    scores = jnp.where(jnp.concatenate([seen, seen], 0), scores, NEGATIVE)
    row_max = jnp.max(scores, 1, keepdims=True)
    p = jnp.exp2(scores * SCALE2 - row_max * SCALE2).astype(jnp.bfloat16)
    finish(0, prompt_rows, row_max, dot_nn(p, wide_ref[:prompt_total]))


def attention_backward(
    sizes, q_ref, k_ref, v_ref, d_ref, ctx_ref, lse_ref, dq_ref, k_sum, v_sum
):
    prompt_rows, prompt_total, later_rows = sizes
    seq = lax.axis_index("seq")
    keys_t = k_ref[...].astype(jnp.float32).T.astype(jnp.bfloat16)
    lse_t = lse_ref[...].T
    weighed_t = (d_ref[...].astype(jnp.float32) * ctx_ref[...].astype(jnp.float32)).T
    deltas = [
        jnp.sum(weighed_t[:HEAD_DIM], 0, keepdims=True),
        jnp.sum(weighed_t[HEAD_DIM:], 0, keepdims=True),
    ]
    totals = [lse_t[0:1], lse_t[HEAD_DIM : HEAD_DIM + 1]]

    def group(start, rows, count, mask):
        queries = stacked_heads(q_ref[start : start + rows])
        grads = stacked_heads(d_ref[start : start + rows])
        total = jnp.concatenate([t[:, start : start + rows] for t in totals], 1)
        delta = jnp.concatenate([t[:, start : start + rows] for t in deltas], 1)
        p = mask(jnp.exp2(dot_nt(k_ref[:count], queries) * SCALE2 - total))
        d_scores = (p * (dot_nt(v_ref[:count], grads) - delta)).astype(jnp.bfloat16)
        dq_t = dot_nn(keys_t[:, :count], d_scores)
        first = lax.broadcasted_iota(jnp.int32, (128, rows), 0) < HEAD_DIM
        dq = jnp.where(first, dq_t[:, :rows], dq_t[:, rows:]).T * 0.125
        dq_ref[start : start + rows] = dq.astype(jnp.bfloat16)
        return dot_nn(d_scores, queries), dot_nn(p.astype(jnp.bfloat16), grads)

    def causal(free, rows):
        def mask(p):
            key = lax.broadcasted_iota(jnp.int32, (rows, rows), 0)
            row = lax.broadcasted_iota(jnp.int32, (rows, rows), 1)
            seen = key <= row
            edge = jnp.where(jnp.concatenate([seen, seen], 1), p[free:], 0.0)
            return jnp.concatenate([p[:free], edge], 0)

        return mask

    def prompt_mask(p):
        key = lax.broadcasted_iota(jnp.int32, (prompt_total, prompt_rows), 0)
        row = lax.broadcasted_iota(jnp.int32, (prompt_total, prompt_rows), 1)
        seen = key <= row + seq * prompt_rows
        return jnp.where(jnp.concatenate([seen, seen], 1), p, 0.0)

    groups = row_groups(prompt_rows, prompt_total, later_rows)
    start, rows, free = groups[-1]
    k_sum[...], v_sum[...] = group(start, rows, free + rows, causal(free, rows))
    for start, rows, free in groups[:-1]:
        d_keys, d_values = group(start, rows, free + rows, causal(free, rows))
        k_sum[: free + rows] += d_keys
        v_sum[: free + rows] += d_values
    d_keys, d_values = group(0, prompt_rows, prompt_total, prompt_mask)
    k_sum[:prompt_total] += d_keys
    v_sum[:prompt_total] += d_values


UP_SECTIONS = (3 * MODEL_WIDTH, MODEL_WIDTH, HIDDEN_UNITS, MODEL_WIDTH)
UP_STARTS = (0, 768, 1024, 2048)
UP_FIRST = (0, 3 * MODEL_WIDTH, 4 * MODEL_WIDTH, 4 * MODEL_WIDTH + HIDDEN_UNITS)
QUARTER = (3 * MODEL_WIDTH + HIDDEN_UNITS) // 4
UP_QUARTER = sum(UP_SECTIONS) // 4
EARLY_COLS = QUARTER + UP_QUARTER - UP_STARTS[1]
TILE = 256
WIDE = 512


def for_blocks(count, body):
    def step(i, carry):
        body(pl.multiple_of(i * 128, 128))
        return carry

    lax.fori_loop(0, count // 128, step, 0)


def centre(values):
    centred = values - jnp.mean(values, axis=1, keepdims=True)
    var = jnp.mean(centred * centred, axis=1, keepdims=True)
    return centred, lax.rsqrt(var + EPSILON)


def normalize_rows(read, write, count, gain, shift):
    def body(start):
        centred, scale = centre(read(start))
        write(start, (centred * scale * gain + shift).astype(jnp.bfloat16))

    for_blocks(count, body)


def norm_pull(values, grads, gain):
    centred, scale = centre(values)
    unit = centred * scale
    grads = grads * gain
    along = jnp.mean(grads * unit, axis=1, keepdims=True)
    return scale * (grads - jnp.mean(grads, axis=1, keepdims=True) - unit * along)


def gelu_both(field):
    square = field * field
    bent = jnp.tanh(0.7978845608028654 * (field + 0.044715 * square * field))
    half = 0.5 * (1.0 + bent)
    slope = 0.7978845608028654 * (1.0 + 3.0 * 0.044715 * square)
    return field * half, half + 0.5 * field * (1.0 - bent * bent) * slope


def quarter_rows(rows, offset, part, across):
    rank = lax.broadcasted_iota(jnp.int32, (ADAPTER_RANK, rows), 0)
    row = lax.broadcasted_iota(jnp.int32, (ADAPTER_RANK, rows), 1)
    if across:
        rank = lax.broadcasted_iota(jnp.int32, (rows, ADAPTER_RANK), 1)
        row = lax.broadcasted_iota(jnp.int32, (rows, ADAPTER_RANK), 0)
    return (row == offset + (rank // 4) * 16 + (rank % 4) * 4 + part).astype(jnp.bfloat16)


def forward_and_gather(groups, ident, tokens, cotangent, gains, biases, shards, collective_id):
    rows = tokens.shape[0]
    prompt_rows = rows - CONT_LEN
    prompt_total = prompt_rows * groups[1]
    keys = prompt_total + CONT_LEN
    sizes = (prompt_rows, prompt_total, CONT_LEN)
    width, hidden_units = MODEL_WIDTH, HIDDEN_UNITS
    pairs = width // 128
    plan = [(prompt_rows, width, False)] + [(a.shape[0], a.shape[1], True) for a in shards]
    count = len(plan)
    whole = [(i, 0, plan[i][0], 0, plan[i][1]) for i in range(count)]
    part = plan[6][0] // 4
    cut = [whole[0], (3, 0, plan[3][0], width, width), (3, 0, plan[3][0], 2 * width, width)]
    cut += [whole[1], whole[2], (3, 0, plan[3][0], 0, width), whole[4]]
    cut += [(5, 0, plan[5][0], i * width, width) for i in range(4)]
    cut += [(6, i * part, part, 0, width) for i in range(4)]
    lengths, chunks, gathered, sems = gather_plan(groups, plan, cut)
    dma = pltpu.SemaphoreType.DMA
    bf, f32 = jnp.bfloat16, jnp.float32

    def kernel(id_ref, tokens_ref, cot_ref, gains_ref, bias_ref, *refs):
        ins = (tokens_ref,) + refs[: count - 1]
        refs = refs[count - 1 :]
        q_out, kv_out, ctx_out, lse_out, act_out, dh_out, dc_out = refs[:7]
        early_out, inner_out, down_out, up_out = refs[7:11]
        outs, refs = refs[11 : 11 + count], refs[11 + count :]
        (
            prompt_v,
            norm_v,
            weight_v,
            w_out_v,
            q_v,
            kv_v,
            wide_v,
            ctx_v,
            lse_v,
            h_v,
            n_v,
            gl_v,
            gp_v,
            dn_v,
            downs_v,
            ups_v,
            down_v,
            up_v,
            low_v,
            turned_v,
            d_low,
            d_turned,
            acc_low,
            acc_turned,
            down_e,
            up_e,
            in_sem,
            out_sem,
        ) = refs[:28]
        enter, tick, ready, ready_kind, finish = gather_stages(groups, lengths, chunks, ins, outs, refs[28:])
        adapter = id_ref[0, 0]
        seq = lax.axis_index("seq")
        grp = lax.axis_index("grp")

        def load(src, dst, sem):
            copy = pltpu.make_async_copy(src, dst, in_sem.at[sem])
            copy.start()
            return copy

        stores, store_sem = [], iter(range(8))

        def store(src, dst):
            copy = pltpu.make_async_copy(src, dst, out_sem.at[next(store_sem)])
            copy.start()
            stores.append(copy)
            return copy

        def settle(copy):
            copy.wait()
            stores[:] = [other for other in stores if other is not copy]

        def bias(start, size):
            return bias_ref[:, pl.ds(pl.multiple_of(start, 128), size)]

        def tile(i, size=TILE, first=0):
            return pl.ds(pl.multiple_of(i * size + first, 128), size)

        def read_tokens(start):
            at = pl.multiple_of(start + prompt_rows, 128)
            return tokens_ref[pl.ds(at, 128)].astype(f32)

        def write_later(start, values):
            norm_v[pl.ds(pl.multiple_of(start + prompt_total, 128), 128)] = values

        def read_prompt(start):
            return prompt_v[pl.ds(start, 128)].astype(f32)

        def write_prompt(start, values):
            norm_v[pl.ds(start, 128)] = values

        def read_hidden(start):
            return h_v[pl.ds(start, 128)]

        def write_hidden(start, values):
            n_v[pl.ds(start, 128)] = values

        def inner(which, values, down):
            low_v[which] = dot_nt(values, down).astype(bf)
            turned_v[which] = dot_nt(down, values).astype(bf)

        def d_inner(which, values, up):
            d_low[which] = dot_nt(values, up).astype(bf)
            d_turned[which] = dot_nt(up, values).astype(bf)

        enter()
        tick(0)
        shift_one = bias_ref[:, :width]
        normalize_rows(read_tokens, write_later, CONT_LEN, gains_ref[0:1], shift_one)
        tick(1)
        ready(0)
        load(outs[0], prompt_v, 0).wait()
        normalize_rows(read_prompt, write_prompt, prompt_total, gains_ref[0:1], shift_one)
        for t in range(2, 6):
            tick(t)

        def weight_part(i, sem):
            cols = slice(i * width, (i + 1) * width)
            return load(outs[3].at[:, cols], weight_v.at[:, cols], sem)

        def prompt_tile(i, carry):
            shift = jnp.where(i >= 8, bias(i * TILE + width, TILE), 0.0)
            early = dot_nn(norm_v[:prompt_total], weight_v[:, tile(i)])
            kv_v[:prompt_total, tile(i - 4)] = (early + shift).astype(bf)
            return carry

        ready(1)
        weight_part(1, 1).wait()
        lax.fori_loop(4, 8, prompt_tile, 0)
        tick(6)
        ready(2)
        weight_part(2, 2).wait()
        lax.fori_loop(8, 12, prompt_tile, 0)
        tick(7)
        ready(3)
        copy_down = load(outs[1], downs_v, 3)
        tick(8)
        ready(4)
        copy_up = load(outs[2], ups_v, 4)
        copy_down.wait()
        copy_up.wait()
        at = lax.broadcasted_iota(jnp.int32, (ADAPTER_RANK, downs_v.shape[0]), 1)
        rank = lax.broadcasted_iota(jnp.int32, (ADAPTER_RANK, downs_v.shape[0]), 0)
        for part in range(4):
            chosen = (at == rank + (adapter * 64 + part * 16)).astype(bf)
            down_v[:, part * QUARTER : (part + 1) * QUARTER] = dot_nn(chosen, downs_v[...]).astype(
                bf
            )
            chosen = quarter_rows(ups_v.shape[0], adapter * 64, part, False)
            for first, start, size in zip(UP_FIRST, UP_STARTS, UP_SECTIONS):
                size //= 4
                up_v[:, first + part * size : first + (part + 1) * size] = dot_nn(
                    chosen, ups_v[:, start : start + size]
                ).astype(bf)
        down_out[...] = down_v[:, :width]
        up_out[...] = up_v[:, : 3 * width]
        inner(0, norm_v[prompt_total:], down_v[:, :width])
        inner_out[...] = turned_v[0]
        d_inner(3, cot_ref[prompt_rows:], up_v[:, UP_FIRST[3] :])
        def later_tile(i):
            weight = weight_v[:, tile(i)]
            return dot_nn(norm_v[prompt_total:], weight) + dot_nn(low_v[0], up_v[:, tile(i)])

        def key_tile(i, carry):
            shift = jnp.where(i >= 8, bias(i * TILE + width, TILE), 0.0)
            kv_v[prompt_total:, tile(i - 4)] = (later_tile(i) + shift).astype(bf)
            return carry

        def query_tile(i, carry):
            shift = bias(i * TILE + 2 * width, TILE)
            q_v[prompt_rows:, tile(i)] = (later_tile(i) + shift).astype(bf)
            mine = norm_v[pl.ds(pl.multiple_of(seq * prompt_rows, 128), prompt_rows)]
            q_v[:prompt_rows, tile(i)] = (dot_nn(mine, weight_v[:, tile(i)]) + shift).astype(bf)
            return carry

        tick(9)
        lax.fori_loop(4, 12, key_tile, 0)
        kv_store = store(kv_v, kv_out)
        ready(5)
        weight_part(0, 5).wait()
        lax.fori_loop(0, 4, query_tile, 0)
        q_store = store(q_v, q_out)

        def attend(i, carry):
            cols = pl.ds(pl.multiple_of(i * 128, 128), 128)
            values = pl.ds(pl.multiple_of(i * 128 + width, 128), 128)

            for at in range(pairs):
                pl.when(i == at)(functools.partial(tick, 10 + at))

            attention_forward(
                sizes,
                q_v.at[:, cols],
                kv_v.at[:, cols],
                kv_v.at[:, values],
                ctx_v.at[:, cols],
                lse_v.at[:, cols],
                wide_v,
            )
            return carry

        lax.fori_loop(0, pairs, attend, 0)
        store(ctx_v, ctx_out)
        lse_store = store(lse_v, lse_out)
        tick(18)
        ready(6)
        load_out = load(outs[4], w_out_v, 6)
        ready(7)

        def hidden_part(i):
            cols = slice(i * width, (i + 1) * width)
            return load(outs[5].at[:, cols], weight_v.at[:, cols], 7 + i)

        hidden_loads = [hidden_part(0)]
        load_out.wait()
        inner(1, ctx_v[prompt_rows:], down_v[:, width : 2 * width])

        def out_tile(j, carry):
            cols = tile(j)
            mixed = dot_nn(ctx_v[...], w_out_v[:, cols]) + bias(j * TILE + 4 * width, TILE)
            mixed = tokens_ref[:, cols].astype(f32) + mixed
            extra = dot_nn(low_v[1], up_v[:, tile(j, first=UP_FIRST[1])])
            h_v[:prompt_rows, cols] = mixed[:prompt_rows]
            h_v[prompt_rows:, cols] = mixed[prompt_rows:] + extra
            return carry

        lax.fori_loop(0, 4, out_tile, 0)
        tick(19)
        normalize_rows(
            read_hidden, write_hidden, rows, gains_ref[1:2], bias_ref[:, width : 2 * width]
        )
        inner(2, n_v[prompt_rows:], down_v[:, 2 * width : 3 * width])
        settle(lse_store)
        sum_v = lse_v

        def start_sums(start):
            at = pl.ds(start, 128)
            sum_v[at] = h_v[at] + bias_ref[:, 5 * width : 6 * width]
            dn_v[at] = jnp.zeros((128, width), f32)

        for_blocks(rows, start_sums)
        tick(20)

        def hidden_tile(i, carry):
            cols = tile(i)

            wide = dot_nn(n_v[...], weight_v[:, cols]) + bias(i * TILE + 6 * width, TILE)
            extra = dot_nn(low_v[2], up_v[:, tile(i, first=UP_FIRST[2])])
            for at, field in (
                (slice(0, prompt_rows), wide[:prompt_rows]),
                (slice(prompt_rows, rows), wide[prompt_rows:] + extra),
            ):
                value, slope = gelu_both(field)
                gl_v[at, cols] = value.astype(bf)
                gp_v[at, cols] = slope.astype(bf)
            return carry

        for i in range(4):
            hidden_loads[i].wait()
            if i < 3:
                ready(8 + i)
                hidden_loads.append(hidden_part(i + 1))
            lax.fori_loop(i * 4, i * 4 + 4, hidden_tile, 0)
            if i < 2:
                tick(21 + i)
        settle(kv_store)
        tick(23)

        df_v = norm_v.at[:rows]
        part_rows = hidden_units // 4
        for which in range(2):
            acc_low[which] = jnp.zeros((CONT_LEN, ADAPTER_RANK), f32)
            acc_turned[which] = jnp.zeros((ADAPTER_RANK, CONT_LEN), f32)
        gx, gy = lax.rem(grp, 2), grp // 2

        def unit_part(kind, carry):
            pl.when(kind == 1)(functools.partial(tick, 24))
            for ch in range(11, 15):
                ready_kind(ch, kind)
            unit_x = lax.rem(gx + kind, 2)
            unit_y = lax.rem(gy + kind // 2, 2)
            base = pl.multiple_of((unit_y * 2 + unit_x) * part_rows, part_rows)
            part = pl.ds(base, part_rows)
            down_part = pl.ds(pl.multiple_of(base + 3 * width, width), part_rows)
            up_part = pl.ds(pl.multiple_of(base + UP_FIRST[2], width), part_rows)
            slot = kv_v.at[:part_rows, :width]
            load(outs[6].at[part], slot, 11).wait()

            def d_hidden(j, carry):
                cols = tile(j, WIDE, base)
                wide = dot_nt(cot_ref[...], slot[tile(j, WIDE)])
                extra = dot_nn(d_low[3], down_v[:, tile(j, WIDE, base + 3 * width)])
                slope = gp_v[:, cols].astype(f32)
                to = tile(j, WIDE)
                df_v[:prompt_rows, to] = (wide[:prompt_rows] * slope[:prompt_rows]).astype(bf)
                later = (wide[prompt_rows:] + extra) * slope[prompt_rows:]
                df_v[prompt_rows:, to] = later.astype(bf)
                return carry

            lax.fori_loop(0, part_rows // WIDE, d_hidden, 0)
            df_later = df_v[prompt_rows:]
            gl_later = gl_v[prompt_rows:, part]
            acc_low[0] += dot_nt(df_later, up_v[:, up_part])
            acc_turned[0] += dot_nt(up_v[:, up_part], df_later)
            acc_low[1] += dot_nt(gl_later, down_v[:, down_part])
            acc_turned[1] += dot_nt(down_v[:, down_part], gl_later)
            down_e[:, down_part] = dot_nn(d_turned[3], gl_later).astype(bf)
            up_e[:, up_part] = dot_nn(turned_v[2], df_later).astype(bf)

            def sums(j, carry):
                cols = tile(j, WIDE)
                sum_v[:, cols] += dot_nn(gl_v[:, part], slot[:, cols])
                dn_v[:, cols] += dot_nt(df_v[...], weight_v[cols, part])
                return carry

            lax.fori_loop(0, width // WIDE, sums, 0)
            return carry

        lax.fori_loop(0, 4, unit_part, 0)
        d_low[2] = acc_low[0].astype(bf)
        d_turned[2] = acc_turned[0].astype(bf)
        low_v[3] = acc_low[1].astype(bf)
        turned_v[3] = acc_turned[1].astype(bf)
        act_v, attn_v, dc_v = prompt_v.at[:rows], q_v, norm_v.at[:rows]

        def last_tile(j, carry):
            cols = tile(j)
            dn_v[prompt_rows:, cols] += dot_nn(d_low[2], down_v[:, tile(j, first=2 * width)])
            act_v[:prompt_rows, cols] = sum_v[:prompt_rows, cols].astype(bf)
            extra = dot_nn(low_v[3], up_v[:, tile(j, first=UP_FIRST[3])])
            act_v[prompt_rows:, cols] = (sum_v[prompt_rows:, cols] + extra).astype(bf)
            return carry

        lax.fori_loop(0, width // TILE, last_tile, 0)
        store(act_v, act_out)
        settle(q_store)

        def pull_rows(start):
            at = pl.ds(start, 128)
            grads = cot_ref[at].astype(f32) + norm_pull(h_v[at], dn_v[at], gains_ref[1:2])
            dn_v[at] = grads
            attn_v[at] = grads.astype(bf)

        for_blocks(rows, pull_rows)
        store(dn_v, dh_out)
        d_inner(1, attn_v[prompt_rows:], up_v[:, UP_FIRST[1] : UP_FIRST[2]])

        def context_tile(j, carry):
            cols = tile(j)
            wide = dot_nt(attn_v[...], w_out_v[cols])
            extra = dot_nn(d_low[1], down_v[:, tile(j, first=width)])
            dc_v[:prompt_rows, cols] = wide[:prompt_rows].astype(bf)
            dc_v[prompt_rows:, cols] = (wide[prompt_rows:] + extra).astype(bf)
            return carry

        lax.fori_loop(0, width // TILE, context_tile, 0)
        store(dc_v, dc_out)
        down_e[:, :width] = jnp.zeros((ADAPTER_RANK, width), bf)
        down_e[:, width : 2 * width] = dot_nn(d_turned[1], ctx_v[prompt_rows:]).astype(bf)
        down_e[:, 2 * width : 3 * width] = dot_nn(d_turned[2], n_v[prompt_rows:]).astype(bf)
        up_e[:, UP_FIRST[1] : UP_FIRST[2]] = dot_nn(turned_v[1], attn_v[prompt_rows:]).astype(bf)
        up_e[:, UP_FIRST[3] :] = dot_nn(turned_v[3], cot_ref[prompt_rows:]).astype(bf)
        for quarter in range(4):
            early_out[quarter, :, :QUARTER] = down_e[:, quarter * QUARTER : (quarter + 1) * QUARTER]
        for section in range(1, 4):
            size = UP_SECTIONS[section] // 4
            moved = jnp.zeros((64, size), f32)
            for part in range(4):
                first = UP_FIRST[section] + part * size
                moved += dot_nn(quarter_rows(64, 0, part, True), up_e[:, first : first + size])
            first = QUARTER + UP_STARTS[section] - UP_STARTS[1]
            for quarter in range(4):
                early_out[quarter, :, first : first + size] = moved[
                    16 * quarter : 16 * quarter + 16
                ].astype(bf)
        for ch in range(len(chunks)):
            finish(ch)
        for copy in stores:
            copy.wait()

    vmem = pl.BlockSpec(memory_space=pltpu.VMEM)
    hbm = pl.BlockSpec(memory_space=pl.ANY)
    return pl.pallas_call(
        kernel,
        in_specs=[pl.BlockSpec(memory_space=pltpu.SMEM)] + [vmem] * (3 + count),
        out_specs=[hbm] * 7 + [vmem] * 4 + [hbm] * count,
        out_shape=[
            jax.ShapeDtypeStruct((rows, width), bf),
            jax.ShapeDtypeStruct((keys, 2 * width), bf),
            jax.ShapeDtypeStruct((rows, width), bf),
            jax.ShapeDtypeStruct((rows, width), f32),
            jax.ShapeDtypeStruct((rows, width), bf),
            jax.ShapeDtypeStruct((rows, width), f32),
            jax.ShapeDtypeStruct((rows, width), bf),
            jax.ShapeDtypeStruct((4, 16, EARLY_COLS), bf),
            jax.ShapeDtypeStruct((ADAPTER_RANK, CONT_LEN), bf),
            jax.ShapeDtypeStruct((ADAPTER_RANK, width), bf),
            jax.ShapeDtypeStruct((ADAPTER_RANK, 3 * width), bf),
        ]
        + gathered,
        scratch_shapes=[
            pltpu.VMEM((prompt_total, width), bf),
            pltpu.VMEM((keys, width), bf),
            pltpu.VMEM((width, hidden_units), bf),
            pltpu.VMEM((width, width), bf),
            pltpu.VMEM((rows, width), bf),
            pltpu.VMEM((keys, 2 * width), bf),
            pltpu.VMEM((keys, 256), bf),
            pltpu.VMEM((rows, width), bf),
            pltpu.VMEM((rows, width), f32),
            pltpu.VMEM((rows, width), f32),
            pltpu.VMEM((rows, width), bf),
            pltpu.VMEM((rows, hidden_units), bf),
            pltpu.VMEM((rows, hidden_units), bf),
            pltpu.VMEM((rows, width), f32),
            pltpu.VMEM(gathered[1].shape, bf),
            pltpu.VMEM(gathered[2].shape, bf),
            pltpu.VMEM((ADAPTER_RANK, 4 * QUARTER), bf),
            pltpu.VMEM((ADAPTER_RANK, 4 * UP_QUARTER), bf),
            pltpu.VMEM((4, CONT_LEN, ADAPTER_RANK), bf),
            pltpu.VMEM((4, ADAPTER_RANK, CONT_LEN), bf),
            pltpu.VMEM((4, CONT_LEN, ADAPTER_RANK), bf),
            pltpu.VMEM((4, ADAPTER_RANK, CONT_LEN), bf),
            pltpu.VMEM((2, CONT_LEN, ADAPTER_RANK), f32),
            pltpu.VMEM((2, ADAPTER_RANK, CONT_LEN), f32),
            pltpu.VMEM((ADAPTER_RANK, 4 * QUARTER), bf),
            pltpu.VMEM((ADAPTER_RANK, 4 * UP_QUARTER), bf),
            dma((13,)),
            dma((8,)),
        ]
        + sems,
        compiler_params=pltpu.CompilerParams(
            collective_id=collective_id, has_side_effects=True, vmem_limit_bytes=VMEM_LIMIT
        ),
    )(ident, tokens, cotangent, gains, biases, *shards)


def adapter_scratch(cols):
    dma = pltpu.SemaphoreType.DMA
    return [
        pltpu.VMEM((2, 16, cols), jnp.bfloat16),
        pltpu.VMEM((16, 128), jnp.bfloat16),
        pltpu.VMEM((3, 4, 16, cols), jnp.bfloat16),
        pltpu.VMEM((3, 4, 16, cols), jnp.bfloat16),
        pltpu.VMEM((4, 16, cols), jnp.float32),
        pltpu.VMEM((3, 16, cols), jnp.bfloat16),
        pltpu.VMEM((3, 16, cols), jnp.bfloat16),
        dma((3,)),
        dma((3,)),
        dma((3,)),
        dma((3,)),
        dma((3,)),
        dma((3,)),
    ]


def adapter_stages(term_ref, id_ref, out_ref, scratch):
    from_core, other_id, to_grp, from_grp, total, to_z, from_z = scratch[:7]
    a_send, a_recv, g_send, g_recv, z_send, z_recv = scratch[7:]
    g, s = lax.axis_index("grp"), lax.axis_index("seq")
    core, z = lax.rem(s, 2), s // 2
    other = 1 - core
    partner = (g, z * 2 + other)
    grps = [lax.rem(g + d, 4) for d in range(1, 4)]
    lines = [lax.rem(z + d, 4) for d in range(1, 4)]

    def enter():
        peers = [partner] + [(far, s) for far in grps] + [(g, far * 2 + core) for far in lines]
        barrier = pltpu.get_barrier_semaphore()
        for peer in peers:
            pl.semaphore_signal(barrier, inc=1, device_id=peer, device_id_type=MESH)
        pl.semaphore_wait(barrier, len(peers))

    def remote(src, dst, send_sem, recv_sem, device):
        return pltpu.make_async_remote_copy(
            src_ref=src,
            dst_ref=dst,
            send_sem=send_sem,
            recv_sem=recv_sem,
            device_id=device,
            device_id_type=MESH,
        )

    copies_a = [
        remote(term_ref.at[i * 2 + other], from_core.at[i], a_send.at[i], a_recv.at[i], partner)
        for i in range(2)
    ] + [remote(id_ref, other_id, a_send.at[2], a_recv.at[2], partner)]
    copies_g = [
        remote(to_grp.at[d], from_grp.at[d], g_send.at[d], g_recv.at[d], (grps[d], s))
        for d in range(3)
    ]
    copies_z = [
        remote(to_z.at[d], from_z.at[d], z_send.at[d], z_recv.at[d], (g, lines[d] * 2 + core))
        for d in range(3)
    ]

    def start(copies):
        for copy in copies:
            copy.start()

    def wait(copies):
        for copy in copies:
            copy.wait()

    def select():
        wait(copies_a)
        mine = id_ref[0:1, 0:1].astype(jnp.float32)
        theirs = other_id[0:1, 0:1].astype(jnp.float32)
        for d, grp in enumerate(grps + [g]):
            for slot in range(4):
                adapter = (grp * 2 + slot // 2).astype(jnp.float32)
                own_term = term_ref[(slot % 2) * 2 + core].astype(jnp.float32)
                other_term = from_core[slot % 2].astype(jnp.float32)
                picked = jnp.where(mine == adapter, own_term, 0.0) + jnp.where(
                    theirs == adapter, other_term, 0.0
                )
                if d < 3:
                    to_grp[d, slot] = picked.astype(jnp.bfloat16)
                else:
                    total[slot] = picked

    def add_grps():
        wait(copies_g)
        for slot in range(4):
            total[slot] += sum(from_grp[d, slot].astype(jnp.float32) for d in range(3))
        for d in range(3):
            to_z[d] = total[lines[d]].astype(jnp.bfloat16)

    def add_lines():
        wait(copies_z)
        out_ref[...] = total[z] + sum(from_z[d].astype(jnp.float32) for d in range(3))

    return (
        enter,
        lambda: start(copies_a),
        select,
        lambda: start(copies_g),
        add_grps,
        lambda: start(copies_z),
        add_lines,
    )


LATE_COLS = MODEL_WIDTH + UP_STARTS[1]


def backward_tail(
    groups, q, kv, d_ctx, ctx, lse, early, ident, tokens, d_hidden, gains, biases, w_qkv, adapters,
    collective_id,
):
    rows, keys, pairs = q.shape[0], kv.shape[0], q.shape[1] // 128
    prompt_rows, prompt_total = rows - CONT_LEN, keys - CONT_LEN
    sizes = (prompt_rows, prompt_total, CONT_LEN)
    width, z_n = MODEL_WIDTH, groups[1] // 2
    bf, f32 = jnp.bfloat16, jnp.float32
    dma = pltpu.SemaphoreType.DMA
    adapter_shapes = len(adapter_scratch(128))

    def kernel(
        q_ref, k_ref, v_ref, d_ref, ctx_ref, lse_ref, early_ref, id_ref, tokens_ref, gains_ref,
        bias_ref, inner_ref, down_ref, up_ref, dh_hbm, w_hbm, *refs
    ):
        x_out, down_out, up_out = refs[:3]
        k_sum, v_sum, dqkv_v, term_v, pair_in, to_line, from_line = refs[3:10]
        w_v, dh_v, dn_v, n_v, late_v, early_sum, late_sum = refs[10:17]
        p_send, p_recv, l_send, l_recv, in_sem, out_sem = refs[17:23]
        scratch = refs[23:]
        e_enter, e_core, e_select, e_grp, e_add, e_z, e_lines = adapter_stages(
            early_ref, id_ref, early_sum, scratch[:adapter_shapes]
        )
        _, l_core, l_select, l_grp, l_add, l_z, l_lines = adapter_stages(
            late_v, id_ref, late_sum, scratch[adapter_shapes:]
        )
        g, s = lax.axis_index("grp"), lax.axis_index("seq")
        core, z = lax.rem(s, 2), s // 2
        far_z = [lax.rem(z + d, z_n) for d in range(1, z_n)]
        step = pl.program_id(0)

        def across(i):
            return pltpu.make_async_remote_copy(
                src_ref=term_v.at[i, 1 - core],
                dst_ref=pair_in.at[i],
                send_sem=p_send.at[i],
                recv_sem=p_recv.at[i],
                device_id=(g, z * 2 + 1 - core),
                device_id_type=MESH,
            )

        def along(i, d):
            return pltpu.make_async_remote_copy(
                src_ref=to_line.at[i, d],
                dst_ref=from_line.at[i, d],
                send_sem=l_send.at[i, d],
                recv_sem=l_recv.at[i, d],
                device_id=(g, far_z[d] * 2 + core),
                device_id_type=MESH,
            )

        def pass_on(i):
            across(i).wait()
            for d, far in enumerate(far_z):
                both = term_v[i, core, far].astype(f32) + pair_in[i, far].astype(f32)
                to_line[i, d] = both.astype(bf)
                along(i, d).start()

        load_w = pltpu.make_async_copy(w_hbm, w_v, in_sem.at[0])
        load_dh = pltpu.make_async_copy(dh_hbm, dh_v, in_sem.at[1])

        @pl.when(step == 0)
        def _():
            e_enter()
            e_core()
            load_w.start()
            load_dh.start()

        cols = pl.ds(pl.multiple_of(step * 128, 128), 128)
        attention_backward(
            sizes, q_ref, k_ref, v_ref, d_ref, ctx_ref, lse_ref, dqkv_v.at[:, cols], k_sum, v_sum
        )
        for block in range(2 * z_n):
            at = slice(block * prompt_rows, (block + 1) * prompt_rows)
            half = block % 2, block // 2
            term_v[step, half[0], half[1], :, :128] = (k_sum[at] * 0.125).astype(bf)
            term_v[step, half[0], half[1], :, 128:] = v_sum[at].astype(bf)
        across(step).start()
        for part, (total, scale) in enumerate(((k_sum, 0.125), (v_sum, 1.0))):
            to = pl.ds(pl.multiple_of(step * 128 + (part + 1) * width, 128), 128)
            dqkv_v[prompt_rows:, to] = (total[prompt_total:] * scale).astype(bf)

        @pl.when(step >= 1)
        def _():
            pass_on(step - 1)

        @pl.when(step == 1)
        def _():
            e_select()
            e_grp()

            def read(start):
                return tokens_ref[pl.ds(pl.multiple_of(start + prompt_rows, 128), 128)].astype(f32)

            def write(start, values):
                n_v[pl.ds(start, 128)] = values

            normalize_rows(read, write, CONT_LEN, gains_ref[0:1], bias_ref[:, :width])

        @pl.when(step == pairs // 2)
        def _():
            e_add()
            e_z()

        @pl.when(step == pairs - 1)
        def _():
            later = dqkv_v[prompt_rows:]
            d_low = dot_nt(later, up_ref[...]).astype(bf)
            d_turned = dot_nt(up_ref[...], later).astype(bf)
            late_v[...] = jnp.zeros(late_v.shape, bf)
            late_v[0, :, :width] = dot_nn(d_turned, n_v[...]).astype(bf)
            size = UP_SECTIONS[0] // 4
            moved = jnp.zeros((64, size), f32)
            for part in range(4):
                grads = dot_nn(inner_ref[...], dqkv_v[prompt_rows:, part * size : (part + 1) * size])
                moved += dot_nn(quarter_rows(64, 0, part, True), grads.astype(bf))
            for quarter in range(4):
                late_v[quarter, :, width:] = moved[16 * quarter : 16 * quarter + 16].astype(bf)
            l_core()
            pass_on(pairs - 1)
            load_w.wait()
            load_dh.wait()

            def pull(first, count):
                def body(start):
                    at = pl.ds(pl.multiple_of(start + first, 128), 128)
                    values = tokens_ref[at].astype(f32)
                    dn_v[at] = dh_v[at] + norm_pull(values, dn_v[at], gains_ref[0:1])

                for_blocks(count, body)
                copy = pltpu.make_async_copy(
                    dn_v.at[first : first + count], x_out.at[first : first + count],
                    out_sem.at[0 if first else 1],
                )
                copy.start()
                return copy

            def later_tile(j, carry):
                to = pl.ds(pl.multiple_of(j * TILE, TILE), TILE)
                wide = dot_nt(dqkv_v[prompt_rows:], w_v[to]) + dot_nn(d_low, down_ref[:, to])
                dn_v[prompt_rows:, to] = wide
                return carry

            lax.fori_loop(0, width // TILE, later_tile, 0)
            l_select()
            l_grp()
            later_store = pull(prompt_rows, CONT_LEN)
            e_lines()

            def arrived(i, carry):
                total = term_v[i, core, z].astype(f32) + pair_in[i, z].astype(f32)
                for d in range(z_n - 1):
                    along(i, d).wait()
                    total = total + from_line[i, d].astype(f32)
                for part in range(2):
                    to = pl.ds(pl.multiple_of(i * 128 + (part + 1) * width, 128), 128)
                    dqkv_v[:prompt_rows, to] = total[:, part * 128 : part * 128 + 128].astype(bf)
                return carry

            lax.fori_loop(0, pairs, arrived, 0)
            l_add()
            l_z()

            def prompt_tile(j, carry):
                to = pl.ds(pl.multiple_of(j * TILE, TILE), TILE)
                dn_v[:prompt_rows, to] = dot_nt(dqkv_v[:prompt_rows], w_v[to])
                return carry

            lax.fori_loop(0, width // TILE, prompt_tile, 0)
            prompt_store = pull(0, prompt_rows)
            l_lines()
            down_out[:, :width] = early_sum[:, :width] + late_sum[:, :width]
            down_out[:, width:] = early_sum[:, width:QUARTER]
            up_out[:, : UP_STARTS[1]] = late_sum[:, width:]
            up_out[:, UP_STARTS[1] :] = early_sum[:, QUARTER:]
            later_store.wait()
            prompt_store.wait()

    def pair(i):
        return (0, i)

    row_spec = pl.BlockSpec((rows, 128), pair)
    key_spec = pl.BlockSpec((keys, 128), pair)
    whole = pl.BlockSpec(memory_space=pltpu.VMEM)
    hbm = pl.BlockSpec(memory_space=pl.ANY)
    return pl.pallas_call(
        kernel,
        grid=(pairs,),
        in_specs=[
            row_spec,
            key_spec,
            pl.BlockSpec((keys, 128), lambda i: (0, pairs + i)),
            row_spec,
            row_spec,
            row_spec,
        ]
        + [whole] * 8
        + [hbm] * 2,
        out_specs=[hbm, whole, whole],
        out_shape=[
            jax.ShapeDtypeStruct((rows, width), f32),
            jax.ShapeDtypeStruct((16, QUARTER), f32),
            jax.ShapeDtypeStruct((16, UP_QUARTER), f32),
        ],
        scratch_shapes=[
            pltpu.VMEM((keys, 128), f32),
            pltpu.VMEM((keys, 128), f32),
            pltpu.VMEM((rows, 3 * width), bf),
            pltpu.VMEM((pairs, 2, z_n, prompt_rows, 256), bf),
            pltpu.VMEM((pairs, z_n, prompt_rows, 256), bf),
            pltpu.VMEM((pairs, z_n - 1, prompt_rows, 256), bf),
            pltpu.VMEM((pairs, z_n - 1, prompt_rows, 256), bf),
            pltpu.VMEM((width, 3 * width), bf),
            pltpu.VMEM((rows, width), f32),
            pltpu.VMEM((rows, width), f32),
            pltpu.VMEM((CONT_LEN, width), bf),
            pltpu.VMEM((4, 16, LATE_COLS), bf),
            pltpu.VMEM((16, EARLY_COLS), f32),
            pltpu.VMEM((16, LATE_COLS), f32),
            dma((pairs,)),
            dma((pairs,)),
            dma((pairs, z_n - 1)),
            dma((pairs, z_n - 1)),
            dma((2,)),
            dma((2,)),
        ]
        + adapter_scratch(EARLY_COLS)
        + adapter_scratch(LATE_COLS),
        compiler_params=pltpu.CompilerParams(
            collective_id=collective_id, has_side_effects=True, vmem_limit_bytes=VMEM_LIMIT
        ),
    )(
        q, kv, kv, d_ctx, ctx, lse, early, ident, tokens, gains, biases, *adapters, d_hidden, w_qkv
    )


def local_general(
    tokens,
    cotangent,
    query_key_value_weight,
    attention_out_weight,
    feedforward_in_weight,
    feedforward_out_weight,
    layer_norm_gains,
    biases,
    adapter_down_matrices,
    adapter_up_matrices,
    adapter_of_continuation,
):
    row_count = tokens.shape[0]
    prompt_rows = row_count - CONT_LEN
    prompt_total = prompt_rows * lax.axis_size("seq")
    key_count = prompt_total + CONT_LEN
    seq_index = lax.axis_index("seq")
    adapter_index = adapter_of_continuation[0, 0]
    weight_shards = (
        query_key_value_weight,
        attention_out_weight,
        feedforward_in_weight,
        feedforward_out_weight,
        adapter_down_matrices,
        adapter_up_matrices,
    )
    gathered_rows = (
        lax.all_gather(weight_shards[0], ("grp", "seq"), axis=0, tiled=True),
        lax.all_gather(weight_shards[1], ("grp", "seq"), axis=0, tiled=True),
        lax.all_gather(weight_shards[2], ("grp", "seq"), axis=0, tiled=True),
        lax.all_gather(weight_shards[3], ("grp", "seq"), axis=0, tiled=True),
        lax.all_gather(weight_shards[4], ("grp", "seq"), axis=0, tiled=True),
        lax.all_gather(weight_shards[5], ("grp", "seq"), axis=0, tiled=True),
    )
    weight_matrices, adapter_sections = unpack_sections(gathered_rows, adapter_index)
    frozen_query_key_value, frozen_attention_out, frozen_feedforward_in, frozen_feedforward_out = (
        weight_matrices
    )
    (
        down_query_key_value,
        down_attention_out,
        down_feedforward_in,
        down_feedforward_out,
        up_query_key_value,
        up_attention_out,
        up_feedforward_in,
        up_feedforward_out,
    ) = adapter_sections
    shift_one = biases[:MODEL_WIDTH]
    shift_two = biases[MODEL_WIDTH : 2 * MODEL_WIDTH]
    query_key_value_bias = jnp.concatenate(
        [
            biases[2 * MODEL_WIDTH : 3 * MODEL_WIDTH],
            jnp.zeros((MODEL_WIDTH,), jnp.float32),
            biases[3 * MODEL_WIDTH : 4 * MODEL_WIDTH],
        ]
    )
    bias_out = biases[4 * MODEL_WIDTH : 5 * MODEL_WIDTH]
    bias_proj = biases[5 * MODEL_WIDTH : 6 * MODEL_WIDTH]
    bias_fc = biases[6 * MODEL_WIDTH :]
    inputs = tokens.astype(jnp.float32)
    normed_one = layer_norm(inputs, layer_norm_gains[0], shift_one).astype(jnp.bfloat16)
    inner_one = product(normed_one[prompt_rows:], down_query_key_value).astype(jnp.bfloat16)
    mixed_query_key_value = product(normed_one, frozen_query_key_value) + query_key_value_bias
    mixed_query_key_value = mixed_query_key_value.at[prompt_rows:].add(
        product(inner_one, up_query_key_value)
    )
    qkv_rows = mixed_query_key_value.astype(jnp.bfloat16)
    prompt_keys, prompt_values = (
        lax.all_gather(
            qkv_rows[:prompt_rows, MODEL_WIDTH : 2 * MODEL_WIDTH], "seq", axis=0, tiled=True
        ),
        lax.all_gather(qkv_rows[:prompt_rows, 2 * MODEL_WIDTH :], "seq", axis=0, tiled=True),
    )
    all_keys = jnp.concatenate(
        [prompt_keys, qkv_rows[prompt_rows:, MODEL_WIDTH : 2 * MODEL_WIDTH]], 0
    )
    all_values = jnp.concatenate([prompt_values, qkv_rows[prompt_rows:, 2 * MODEL_WIDTH :]], 0)
    allowed = visible(row_count, prompt_rows, prompt_total, key_count, seq_index)
    query_heads = split_heads(qkv_rows[:, :MODEL_WIDTH])
    key_heads = split_heads(all_keys)
    value_heads = split_heads(all_values)

    def forward_head(operands):
        query_head, key_head, value_head = operands
        scores = jnp.where(allowed, product_nt(query_head, key_head) * 0.125, NEGATIVE)
        row_max = jnp.max(scores, axis=1, keepdims=True)
        exp_scores = jnp.exp(scores - row_max)
        exp_total = jnp.sum(exp_scores, axis=1, keepdims=True)
        weights = (exp_scores / exp_total).astype(jnp.bfloat16)
        return (product(weights, value_head), (row_max + jnp.log(exp_total))[:, 0])

    head_contexts, log_total = lax.map(forward_head, (query_heads, key_heads, value_heads))
    attention_context = merge_heads(head_contexts).astype(jnp.bfloat16)
    inner_two = product(attention_context[prompt_rows:], down_attention_out).astype(jnp.bfloat16)
    attention_output = product(attention_context, frozen_attention_out) + bias_out
    attention_output = attention_output.at[prompt_rows:].add(product(inner_two, up_attention_out))
    hidden = inputs + attention_output
    normed_two = layer_norm(hidden, layer_norm_gains[1], shift_two).astype(jnp.bfloat16)
    inner_three = product(normed_two[prompt_rows:], down_feedforward_in).astype(jnp.bfloat16)
    before_activation = product(normed_two, frozen_feedforward_in) + bias_fc
    before_activation = before_activation.at[prompt_rows:].add(
        product(inner_three, up_feedforward_in)
    )
    activated_hidden = jax.nn.gelu(before_activation, approximate=True).astype(jnp.bfloat16)
    inner_four = product(activated_hidden[prompt_rows:], down_feedforward_out).astype(jnp.bfloat16)
    adapter_branch = product(activated_hidden, frozen_feedforward_out) + bias_proj
    adapter_branch = adapter_branch.at[prompt_rows:].add(product(inner_four, up_feedforward_out))
    outputs = (hidden + adapter_branch).astype(jnp.bfloat16)
    weight_matrices, adapter_sections = unpack_sections(
        (
            lax.all_gather(weight_shards[0], ("grp", "seq"), axis=0, tiled=True),
            lax.all_gather(weight_shards[1], ("grp", "seq"), axis=0, tiled=True),
            lax.all_gather(weight_shards[2], ("grp", "seq"), axis=0, tiled=True),
            lax.all_gather(weight_shards[3], ("grp", "seq"), axis=0, tiled=True),
            lax.all_gather(weight_shards[4], ("grp", "seq"), axis=0, tiled=True),
            lax.all_gather(weight_shards[5], ("grp", "seq"), axis=0, tiled=True),
        ),
        adapter_index,
    )
    frozen_query_key_value, frozen_attention_out, frozen_feedforward_in, frozen_feedforward_out = (
        weight_matrices
    )
    (
        down_query_key_value,
        down_attention_out,
        down_feedforward_in,
        down_feedforward_out,
        up_query_key_value,
        up_attention_out,
        up_feedforward_in,
        up_feedforward_out,
    ) = adapter_sections
    grad_inner_four = product_nt(cotangent[prompt_rows:], up_feedforward_out).astype(jnp.bfloat16)
    grad_act = product_nt(cotangent, frozen_feedforward_out)
    grad_act = grad_act.at[prompt_rows:].add(product_nt(grad_inner_four, down_feedforward_out))
    gelu_pull = jax.vjp(lambda field: jax.nn.gelu(field, approximate=True), before_activation)[1]
    grad_pre = gelu_pull(grad_act)[0].astype(jnp.bfloat16)
    grad_inner_three = product_nt(grad_pre[prompt_rows:], up_feedforward_in).astype(jnp.bfloat16)
    grad_normed_two = product_nt(grad_pre, frozen_feedforward_in)
    grad_normed_two = grad_normed_two.at[prompt_rows:].add(
        product_nt(grad_inner_three, down_feedforward_in)
    )
    second_pull = jax.vjp(lambda field: layer_norm(field, layer_norm_gains[1], shift_two), hidden)[
        1
    ]
    grad_hidden = cotangent.astype(jnp.float32) + second_pull(grad_normed_two)[0]
    grad_attn = grad_hidden.astype(jnp.bfloat16)
    grad_inner_two = product_nt(grad_attn[prompt_rows:], up_attention_out).astype(jnp.bfloat16)
    grad_context = product_nt(grad_attn, frozen_attention_out)
    grad_context = (
        grad_context.at[prompt_rows:]
        .add(product_nt(grad_inner_two, down_attention_out))
        .astype(jnp.bfloat16)
    )

    def backward_head(operands):
        query_head, key_head, value_head, grad_head, total_head = operands
        scores = jnp.where(allowed, product_nt(query_head, key_head) * 0.125, NEGATIVE)
        prob_full = jnp.exp(scores - total_head[:, None])
        weights = prob_full.astype(jnp.bfloat16)
        grad_weights = product_nt(grad_head, value_head)
        row_delta = jnp.sum(prob_full * grad_weights, axis=1, keepdims=True)
        grad_scores = (prob_full * (grad_weights - row_delta)).astype(jnp.bfloat16)
        return (
            product(grad_scores, key_head) * 0.125,
            product_tn(grad_scores, query_head) * 0.125,
            product_tn(weights, grad_head),
        )

    grad_q, grad_k, grad_v = lax.map(
        backward_head, (query_heads, key_heads, value_heads, split_heads(grad_context), log_total)
    )
    grad_query = merge_heads(grad_q)
    grad_keys = merge_heads(grad_k)
    grad_values = merge_heads(grad_v)
    own_keys, own_values = (
        lax.psum_scatter(
            grad_keys[:prompt_total].astype(jnp.bfloat16), "seq", scatter_dimension=0, tiled=True
        ).astype(jnp.float32),
        lax.psum_scatter(
            grad_values[:prompt_total].astype(jnp.bfloat16), "seq", scatter_dimension=0, tiled=True
        ).astype(jnp.float32),
    )
    grad_qkv = jnp.concatenate(
        [
            grad_query,
            jnp.concatenate([own_keys, grad_keys[prompt_total:]], 0),
            jnp.concatenate([own_values, grad_values[prompt_total:]], 0),
        ],
        1,
    ).astype(jnp.bfloat16)
    grad_inner_one = product_nt(grad_qkv[prompt_rows:], up_query_key_value).astype(jnp.bfloat16)
    grad_normed_one = product_nt(grad_qkv, frozen_query_key_value)
    grad_normed_one = grad_normed_one.at[prompt_rows:].add(
        product_nt(grad_inner_one, down_query_key_value)
    )
    first_pull = jax.vjp(lambda field: layer_norm(field, layer_norm_gains[0], shift_one), inputs)[1]
    input_grad = grad_hidden + first_pull(grad_normed_one)[0]
    down_term = jnp.concatenate(
        [
            product_tn(normed_one[prompt_rows:], grad_inner_one),
            product_tn(attention_context[prompt_rows:], grad_inner_two),
            product_tn(normed_two[prompt_rows:], grad_inner_three),
            product_tn(activated_hidden[prompt_rows:], grad_inner_four),
        ],
        0,
    )
    up_term = jnp.concatenate(
        [
            product_tn(inner_one, grad_qkv[prompt_rows:]),
            product_tn(inner_two, grad_attn[prompt_rows:]),
            product_tn(inner_three, grad_pre[prompt_rows:]),
            product_tn(inner_four, cotangent[prompt_rows:]),
        ],
        1,
    )
    select = (jnp.arange(ADAPTER_COUNT, dtype=jnp.int32) == adapter_index).astype(jnp.float32)
    down_grad, up_grad = (
        lax.psum_scatter(
            (select[:, None, None] * down_term[None]).reshape(-1),
            ("grp", "seq"),
            scatter_dimension=0,
            tiled=True,
        ),
        lax.psum_scatter(
            (select[:, None, None] * up_term[None]).reshape(-1),
            ("grp", "seq"),
            scatter_dimension=0,
            tiled=True,
        ),
    )
    return (outputs, input_grad, down_grad, up_grad)


def fast(
    tokens,
    cotangent,
    query_key_value_weight,
    attention_out_weight,
    feedforward_in_weight,
    feedforward_out_weight,
    layer_norm_gains,
    biases,
    adapter_down_matrices,
    adapter_up_matrices,
    adapter_of_continuation,
):
    groups = (lax.axis_size("grp"), lax.axis_size("seq"))
    up_cols = 5 * MODEL_WIDTH + HIDDEN_UNITS
    ups_shard = adapter_up_matrices.reshape(4, up_cols)
    up_parts, first = [], 0
    for size in UP_SECTIONS:
        up_parts.append(ups_shard[:, first : first + size].reshape(16, size // 4))
        first += size
    (
        queries,
        keys_values,
        context,
        log_total,
        outputs,
        grad_hidden,
        grad_context,
        early_term,
        inner_one,
        down_qkv,
        up_qkv,
        _,
        _,
        _,
        w_qkv,
        _,
        _,
        _,
    ) = forward_and_gather(
        groups,
        adapter_of_continuation,
        tokens,
        cotangent,
        layer_norm_gains,
        biases.reshape(1, -1),
        [
            adapter_down_matrices.reshape(-1, ADAPTER_RANK).T,
            jnp.concatenate(up_parts, 1),
            query_key_value_weight.reshape(-1, 3 * MODEL_WIDTH),
            attention_out_weight.reshape(-1, MODEL_WIDTH),
            feedforward_in_weight.reshape(-1, HIDDEN_UNITS),
            feedforward_out_weight.reshape(-1, MODEL_WIDTH),
        ],
        1,
    )
    ident = jnp.full((16, 128), adapter_of_continuation[0, 0], jnp.int32).astype(jnp.bfloat16)
    input_grad, down_grad, up_grad = backward_tail(
        groups,
        queries,
        keys_values,
        grad_context,
        context,
        log_total,
        early_term,
        ident,
        tokens,
        grad_hidden,
        layer_norm_gains,
        biases.reshape(1, -1),
        w_qkv,
        (inner_one, down_qkv, up_qkv),
        3,
    )
    down_grad = down_grad.T.reshape(-1)
    up_pieces = []
    for start, size in zip(UP_STARTS, UP_SECTIONS):
        up_pieces.append(up_grad[:, start : start + size // 4].reshape(4, -1))
    up_grad = jnp.concatenate(up_pieces, 1).reshape(-1)
    return (outputs, input_grad, down_grad, up_grad)


def solution(mesh):
    placed = (
        P(("grp", "seq"), None),
        P(("grp", "seq"), None),
        P(("grp", "seq")),
        P(("grp", "seq")),
        P(("grp", "seq")),
        P(("grp", "seq")),
        P(),
        P(),
        P(("grp", "seq")),
        P(("grp", "seq")),
        P(("grp", "seq"), None),
    )
    fits = mesh.shape["grp"] == 4 and mesh.shape["seq"] == 8
    return jax.shard_map(
        fast if fits else local_general,
        mesh=mesh,
        in_specs=placed,
        out_specs=(
            P(("grp", "seq"), None),
            P(("grp", "seq"), None),
            P(("grp", "seq")),
            P(("grp", "seq")),
        ),
        check_vma=False,
    )
```

```python
import functools

import jax
import jax.numpy as jnp
from jax import lax
from jax.experimental import pallas as pl
from jax.experimental.pallas import tpu as pltpu
from jax.sharding import PartitionSpec as P

MODEL_WIDTH = 1024
HEADS = 16
HEAD_DIM = 64
HIDDEN_UNITS = 4096
ADAPTER_RANK = 16
ADAPTER_COUNT = 8
CONT_LEN = 512


EPSILON = 1e-05
NEGATIVE = -1e30


def product(left_side, right_side):
    return jnp.dot(left_side, right_side, preferred_element_type=jnp.float32)


def product_tn(left_side, right_side):
    return lax.dot_general(
        left_side, right_side, (((0,), (0,)), ((), ())), preferred_element_type=jnp.float32
    )


def product_nt(left_side, right_side):
    return lax.dot_general(
        left_side, right_side, (((1,), (1,)), ((), ())), preferred_element_type=jnp.float32
    )


def layer_norm(values, gain_vec, shift_vec):
    row_mean = jnp.mean(values, axis=-1, keepdims=True)
    centred = values - row_mean
    row_var = jnp.mean(centred * centred, axis=-1, keepdims=True)
    return centred * lax.rsqrt(row_var + EPSILON) * gain_vec + shift_vec


def unpack_sections(pieces, adapter_index):
    qkv_flat, out_flat, fc_flat, proj_flat, down_flat, up_flat = pieces
    every_down_matrix = down_flat.reshape(
        ADAPTER_COUNT, 3 * MODEL_WIDTH + HIDDEN_UNITS, ADAPTER_RANK
    )
    every_up_matrix = up_flat.reshape(ADAPTER_COUNT, ADAPTER_RANK, 5 * MODEL_WIDTH + HIDDEN_UNITS)
    down_rows = lax.dynamic_index_in_dim(every_down_matrix, adapter_index, 0, keepdims=False)
    up_cols = lax.dynamic_index_in_dim(every_up_matrix, adapter_index, 0, keepdims=False)
    weight_matrices = (
        qkv_flat.reshape(MODEL_WIDTH, 3 * MODEL_WIDTH),
        out_flat.reshape(MODEL_WIDTH, MODEL_WIDTH),
        fc_flat.reshape(MODEL_WIDTH, HIDDEN_UNITS),
        proj_flat.reshape(HIDDEN_UNITS, MODEL_WIDTH),
    )
    adapter_sections = (
        down_rows[:MODEL_WIDTH],
        down_rows[MODEL_WIDTH : 2 * MODEL_WIDTH],
        down_rows[2 * MODEL_WIDTH : 3 * MODEL_WIDTH],
        down_rows[3 * MODEL_WIDTH :],
        up_cols[:, : 3 * MODEL_WIDTH],
        up_cols[:, 3 * MODEL_WIDTH : 4 * MODEL_WIDTH],
        up_cols[:, 4 * MODEL_WIDTH : 4 * MODEL_WIDTH + HIDDEN_UNITS],
        up_cols[:, 4 * MODEL_WIDTH + HIDDEN_UNITS :],
    )
    return (weight_matrices, adapter_sections)


def visible(row_count, prompt_rows, prompt_total, key_count, seq_index):
    row_ids = jnp.arange(row_count, dtype=jnp.int32)[:, None]
    col_ids = jnp.arange(key_count, dtype=jnp.int32)[None, :]
    in_prompt = col_ids < prompt_total
    prompt_seen = in_prompt & (col_ids <= seq_index * prompt_rows + row_ids)
    later_seen = in_prompt | (col_ids - prompt_total <= row_ids - prompt_rows)
    return jnp.where(row_ids < prompt_rows, prompt_seen, later_seen)


def split_heads(values):
    return values.reshape(values.shape[0], HEADS, HEAD_DIM).transpose(1, 0, 2)


def merge_heads(values):
    return values.transpose(1, 0, 2).reshape(values.shape[1], HEADS * HEAD_DIM)


MESH = pl.DeviceIdType.MESH
SCALE2 = 0.125 * 1.4426950408889634
VMEM_LIMIT = 63 << 20


def gather_stages(groups, sizes, chunks, ins, outs, sems):
    grp_n, seq_n = groups
    z_n, y_n = seq_n // 2, grp_n // 2
    z_sem, x_sem, y_sem, d_sem, p_sem, s_sem, l_sem = sems
    g, s = lax.axis_index("grp"), lax.axis_index("seq")
    core, z = lax.rem(s, 2), s // 2
    gx, gy = lax.rem(g, 2), g // 2
    partner = (g, z * 2 + 1 - core)
    other_x = gy * 2 + 1 - gx
    x_next = (other_x, s)
    far_z = [lax.rem(z + d, z_n) for d in range(1, z_n)]
    far_y = [lax.rem(gy + d, y_n) for d in range(1, y_n)]
    y_next = [(y * 2 + gx, s) for y in far_y]

    def enter():
        peers = [partner, x_next] + y_next + [(g, far * 2 + core) for far in far_z]
        barrier = pltpu.get_barrier_semaphore()
        for peer in peers:
            pl.semaphore_signal(barrier, inc=1, device_id=peer, device_id_type=MESH)
        pl.semaphore_wait(barrier, len(peers))

    def place(ch, gg, ss):
        arr, row, rows, col, cols, full = chunks[ch]
        block = gg * seq_n + ss if full else ss
        at = pl.ds(pl.multiple_of(block * sizes[arr] + row, 16), rows)
        return outs[arr].at[at, pl.ds(col, cols)]

    def send(ch, src, gg, ss, sem, device):
        pltpu.make_async_remote_copy(
            src_ref=src,
            dst_ref=place(ch, gg, ss),
            send_sem=s_sem.at[ch],
            recv_sem=sem,
            device_id=device,
            device_id_type=MESH,
        ).start()

    def drain(ch, sem, count=1):
        arr, _, rows, col, cols, _ = chunks[ch]
        block = outs[arr].at[pl.ds(0, count * rows), pl.ds(col, cols)]
        pltpu.make_async_copy(block, block, sem).wait()

    def each(first, last, body):
        def step(i, carry):
            body(i)
            return carry

        lax.fori_loop(first, last, step, 0)

    def shard(ch):
        arr, row, rows, col, cols, _ = chunks[ch]
        return ins[arr].at[pl.ds(row, rows), pl.ds(col, cols)]

    def own(ch):
        src = shard(ch)

        def to_line(d):
            send(ch, src, g, s, z_sem.at[ch, z], (g, lax.rem(z + d, z_n) * 2 + core))

        each(1, z_n, to_line)
        send(ch, src, g, s, p_sem.at[ch, 0], partner)
        pltpu.make_async_copy(src, place(ch, g, s), l_sem.at[ch]).start()

    def near(ch):
        src = shard(ch)
        send(ch, src, g, s, x_sem.at[ch, z], x_next)
        for peer in y_next:
            send(ch, src, g, s, y_sem.at[ch, gy, z], peer)

    def line(ch):
        def relay(d):
            far = lax.rem(z + d, z_n)
            drain(ch, z_sem.at[ch, far])
            from_s = far * 2 + core
            src = place(ch, g, from_s)
            if chunks[ch][5]:
                send(ch, src, g, from_s, x_sem.at[ch, far], x_next)
                for peer in y_next:
                    send(ch, src, g, from_s, y_sem.at[ch, gy, far], peer)
            send(ch, src, g, from_s, p_sem.at[ch, 0], partner)

        each(1, z_n, relay)

    def side(ch):
        if not chunks[ch][5]:
            return

        def relay(half):
            for odd in range(2):
                far = half * 2 + odd
                from_s = far * 2 + core
                drain(ch, x_sem.at[ch, far])
                src = place(ch, other_x, from_s)
                if not odd:
                    for peer in y_next:
                        send(ch, src, other_x, from_s, d_sem.at[ch, gy, far], peer)
                send(ch, src, other_x, from_s, p_sem.at[ch, 1], partner)
                for y in far_y:
                    drain(ch, y_sem.at[ch, y, far])
                    from_g = y * 2 + gx
                    src = place(ch, from_g, from_s)
                    if odd:
                        send(ch, src, from_g, from_s, d_sem.at[ch, y, far], x_next)
                    send(ch, src, from_g, from_s, p_sem.at[ch, 2], partner)

        each(0, z_n // 2, relay)

    def corner(ch):
        if not chunks[ch][5]:
            return

        def relay(far):
            from_s = far * 2 + core
            for y in far_y:
                drain(ch, d_sem.at[ch, y, far])
                from_g = y * 2 + 1 - gx
                src = place(ch, from_g, from_s)
                send(ch, src, from_g, from_s, p_sem.at[ch, 3], partner)

        each(0, z_n, relay)

    def ready_kind(ch, kind):
        drain(ch, p_sem.at[ch, kind], z_n)
        pl.when(kind == 0)(lambda: drain(ch, l_sem.at[ch]))

    def ready(ch, kinds=range(4)):
        for kind in kinds if chunks[ch][5] else (0,):
            drain(ch, p_sem.at[ch, kind], z_n * (y_n - 1 if kind >= 2 else 1))
            if kind == 0:
                drain(ch, l_sem.at[ch])

    def finish(ch):
        sends = 2 * z_n - 1
        if chunks[ch][5]:
            sends += z_n * y_n
            sends += z_n * (y_n - 1)
            sends += z_n * (2 * y_n - 1)
        drain(ch, s_sem.at[ch], sends)

    steps = {"own": own, "near": near, "line": line, "side": side, "corner": corner}

    def tick(t):
        for step, which in GATHER_ORDER[t]:
            for ch in which:
                steps[step](ch)

    return enter, tick, ready, ready_kind, finish


def gather_plan(groups, shards, chunks):
    grp_n, seq_n = groups
    shapes = []
    for rows, cols, full in shards:
        total = (grp_n if full else 1) * seq_n * rows
        shapes.append(jax.ShapeDtypeStruct((total, cols), jnp.bfloat16))
    chunks = [chunk + (shards[chunk[0]][2],) for chunk in chunks]
    dma, count = pltpu.SemaphoreType.DMA, len(chunks)
    sems = [
        dma((count, seq_n // 2)),
        dma((count, seq_n // 2)),
        dma((count, grp_n // 2, seq_n // 2)),
        dma((count, grp_n // 2, seq_n // 2)),
        dma((count, 4)),
        dma((count,)),
        dma((count,)),
    ]
    return [rows for rows, _, _ in shards], chunks, shapes, sems


GATHER_ORDER = (
    (("own", (0, 1, 2, 3)), ("near", (1, 2, 3, 4, 5, 6, 7, 8))),
    (("own", (4, 5)), ("near", (9, 10, 11, 12, 13, 14)), ("line", (0,))),
    (("own", (6,)), ("line", (1,))),
    (("own", (7,)), ("line", (2,))),
    (("side", (1,)), ("line", (3,))),
    (("corner", (1,)), ("side", (2,)), ("line", (4,))),
    (("corner", (2,)), ("side", (3,)), ("line", (5,))),
    (("own", (8,)), ("corner", (3,)), ("side", (4,)), ("line", (6,))),
    (("own", (9,)), ("corner", (4,)), ("side", (5,)), ("line", (7,))),
    (("own", (10,)), ("corner", (5,)), ("side", (6,)), ("line", (8,))),
    (("own", (11,)), ("corner", (6,)), ("side", (7,))),
    (("line", (9,)),),
    (("own", (12,)), ("corner", (7,)), ("side", (8,))),
    (("line", (10,)),),
    (("own", (13,)), ("corner", (8,)), ("side", (9,))),
    (("line", (11,)),),
    (("own", (14,)), ("corner", (9,)), ("side", (10,))),
    (("line", (12,)),),
    (("corner", (10,)), ("side", (11,))),
    (("line", (13,)),),
    (("corner", (11,)), ("side", (12,))),
    (("line", (14,)),),
    (("corner", (12,)), ("side", (13,))),
    (("corner", (13,)), ("side", (14,))),
    (("corner", (14,)),),
)


def dot_nt(left, right):
    return lax.dot_general(
        left, right, (((1,), (1,)), ((), ())), preferred_element_type=jnp.float32
    )


def dot_nn(left, right):
    return lax.dot_general(
        left, right, (((1,), (0,)), ((), ())), preferred_element_type=jnp.float32
    )


def stacked_heads(pair):
    first = lax.broadcasted_iota(jnp.int32, pair.shape, 1) < HEAD_DIM
    zero = jnp.zeros_like(pair)
    return jnp.concatenate([jnp.where(first, pair, zero), jnp.where(first, zero, pair)], 0)


def row_groups(prompt_rows, prompt_total, later_rows):
    block = min(256, later_rows)
    return [(prompt_rows + i, block, prompt_total + i) for i in range(0, later_rows, block)]


def attention_forward(sizes, q_ref, k_ref, v_ref, ctx_ref, lse_ref, wide_ref):
    prompt_rows, prompt_total, later_rows = sizes
    seq = lax.axis_index("seq")
    wide_ref[:, :128] = v_ref[...]
    wide_ref[:, 128:] = jnp.ones((prompt_total + later_rows, 128), jnp.bfloat16)

    def finish(start, rows, row_max, summed):
        total = summed[:, 128:]
        mixed = summed[:, :128] / total
        log_total = row_max * SCALE2 + jnp.log2(total)
        first = lax.broadcasted_iota(jnp.int32, (rows, 128), 1) < HEAD_DIM
        ctx_ref[start : start + rows] = jnp.where(first, mixed[:rows], mixed[rows:]).astype(
            jnp.bfloat16
        )
        lse_ref[start : start + rows] = jnp.where(first, log_total[:rows], log_total[rows:])

    for start, rows, free in row_groups(prompt_rows, prompt_total, later_rows):
        queries = stacked_heads(q_ref[start : start + rows])
        open_scores = dot_nt(queries, k_ref[:free])
        edge_scores = dot_nt(queries, k_ref[free : free + rows])
        row = lax.broadcasted_iota(jnp.int32, (rows, rows), 0)
        key = lax.broadcasted_iota(jnp.int32, (rows, rows), 1)
        seen = key <= row
        edge_scores = jnp.where(jnp.concatenate([seen, seen], 0), edge_scores, NEGATIVE)
        row_max = jnp.maximum(
            jnp.max(open_scores, 1, keepdims=True), jnp.max(edge_scores, 1, keepdims=True)
        )
        scaled = row_max * SCALE2
        open_p = jnp.exp2(open_scores * SCALE2 - scaled).astype(jnp.bfloat16)
        edge_p = jnp.exp2(edge_scores * SCALE2 - scaled).astype(jnp.bfloat16)
        summed = dot_nn(open_p, wide_ref[:free]) + dot_nn(edge_p, wide_ref[free : free + rows])
        finish(start, rows, row_max, summed)
    scores = dot_nt(stacked_heads(q_ref[:prompt_rows]), k_ref[:prompt_total])
    row = lax.broadcasted_iota(jnp.int32, (prompt_rows, prompt_total), 0)
    key = lax.broadcasted_iota(jnp.int32, (prompt_rows, prompt_total), 1)
    seen = key <= row + seq * prompt_rows
    scores = jnp.where(jnp.concatenate([seen, seen], 0), scores, NEGATIVE)
    row_max = jnp.max(scores, 1, keepdims=True)
    p = jnp.exp2(scores * SCALE2 - row_max * SCALE2).astype(jnp.bfloat16)
    finish(0, prompt_rows, row_max, dot_nn(p, wide_ref[:prompt_total]))


def attention_backward(
    sizes, q_ref, k_ref, v_ref, d_ref, ctx_ref, lse_ref, dq_ref, k_sum, v_sum
):
    prompt_rows, prompt_total, later_rows = sizes
    seq = lax.axis_index("seq")
    keys_t = k_ref[...].astype(jnp.float32).T.astype(jnp.bfloat16)
    lse_t = lse_ref[...].T
    weighed_t = (d_ref[...].astype(jnp.float32) * ctx_ref[...].astype(jnp.float32)).T
    deltas = [
        jnp.sum(weighed_t[:HEAD_DIM], 0, keepdims=True),
        jnp.sum(weighed_t[HEAD_DIM:], 0, keepdims=True),
    ]
    totals = [lse_t[0:1], lse_t[HEAD_DIM : HEAD_DIM + 1]]

    def group(start, rows, count, mask):
        queries = stacked_heads(q_ref[start : start + rows])
        grads = stacked_heads(d_ref[start : start + rows])
        total = jnp.concatenate([t[:, start : start + rows] for t in totals], 1)
        delta = jnp.concatenate([t[:, start : start + rows] for t in deltas], 1)
        p = mask(jnp.exp2(dot_nt(k_ref[:count], queries) * SCALE2 - total))
        d_scores = (p * (dot_nt(v_ref[:count], grads) - delta)).astype(jnp.bfloat16)
        dq_t = dot_nn(keys_t[:, :count], d_scores)
        first = lax.broadcasted_iota(jnp.int32, (128, rows), 0) < HEAD_DIM
        dq = jnp.where(first, dq_t[:, :rows], dq_t[:, rows:]).T * 0.125
        dq_ref[start : start + rows] = dq.astype(jnp.bfloat16)
        return dot_nn(d_scores, queries), dot_nn(p.astype(jnp.bfloat16), grads)

    def causal(free, rows):
        def mask(p):
            key = lax.broadcasted_iota(jnp.int32, (rows, rows), 0)
            row = lax.broadcasted_iota(jnp.int32, (rows, rows), 1)
            seen = key <= row
            edge = jnp.where(jnp.concatenate([seen, seen], 1), p[free:], 0.0)
            return jnp.concatenate([p[:free], edge], 0)

        return mask

    def prompt_mask(p):
        key = lax.broadcasted_iota(jnp.int32, (prompt_total, prompt_rows), 0)
        row = lax.broadcasted_iota(jnp.int32, (prompt_total, prompt_rows), 1)
        seen = key <= row + seq * prompt_rows
        return jnp.where(jnp.concatenate([seen, seen], 1), p, 0.0)

    groups = row_groups(prompt_rows, prompt_total, later_rows)
    start, rows, free = groups[-1]
    k_sum[...], v_sum[...] = group(start, rows, free + rows, causal(free, rows))
    for start, rows, free in groups[:-1]:
        d_keys, d_values = group(start, rows, free + rows, causal(free, rows))
        k_sum[: free + rows] += d_keys
        v_sum[: free + rows] += d_values
    d_keys, d_values = group(0, prompt_rows, prompt_total, prompt_mask)
    k_sum[:prompt_total] += d_keys
    v_sum[:prompt_total] += d_values


UP_SECTIONS = (3 * MODEL_WIDTH, MODEL_WIDTH, HIDDEN_UNITS, MODEL_WIDTH)
UP_STARTS = (0, 768, 1024, 2048)
UP_FIRST = (0, 3 * MODEL_WIDTH, 4 * MODEL_WIDTH, 4 * MODEL_WIDTH + HIDDEN_UNITS)
QUARTER = (3 * MODEL_WIDTH + HIDDEN_UNITS) // 4
UP_QUARTER = sum(UP_SECTIONS) // 4
EARLY_COLS = QUARTER + UP_QUARTER - UP_STARTS[1]
TILE = 256
WIDE = 512


def for_blocks(count, body):
    def step(i, carry):
        body(pl.multiple_of(i * 128, 128))
        return carry

    lax.fori_loop(0, count // 128, step, 0)


def centre(values):
    centred = values - jnp.mean(values, axis=1, keepdims=True)
    var = jnp.mean(centred * centred, axis=1, keepdims=True)
    return centred, lax.rsqrt(var + EPSILON)


def normalize_rows(read, write, count, gain, shift):
    def body(start):
        centred, scale = centre(read(start))
        write(start, (centred * scale * gain + shift).astype(jnp.bfloat16))

    for_blocks(count, body)


def norm_pull(values, grads, gain):
    centred, scale = centre(values)
    unit = centred * scale
    grads = grads * gain
    along = jnp.mean(grads * unit, axis=1, keepdims=True)
    return scale * (grads - jnp.mean(grads, axis=1, keepdims=True) - unit * along)


def gelu_both(field):
    square = field * field
    bent = jnp.tanh(0.7978845608028654 * (field + 0.044715 * square * field))
    half = 0.5 * (1.0 + bent)
    slope = 0.7978845608028654 * (1.0 + 3.0 * 0.044715 * square)
    return field * half, half + 0.5 * field * (1.0 - bent * bent) * slope


def quarter_rows(rows, offset, part, across):
    rank = lax.broadcasted_iota(jnp.int32, (ADAPTER_RANK, rows), 0)
    row = lax.broadcasted_iota(jnp.int32, (ADAPTER_RANK, rows), 1)
    if across:
        rank = lax.broadcasted_iota(jnp.int32, (rows, ADAPTER_RANK), 1)
        row = lax.broadcasted_iota(jnp.int32, (rows, ADAPTER_RANK), 0)
    return (row == offset + (rank // 4) * 16 + (rank % 4) * 4 + part).astype(jnp.bfloat16)


def forward_and_gather(groups, ident, tokens, cotangent, gains, biases, shards, collective_id):
    rows = tokens.shape[0]
    prompt_rows = rows - CONT_LEN
    prompt_total = prompt_rows * groups[1]
    keys = prompt_total + CONT_LEN
    sizes = (prompt_rows, prompt_total, CONT_LEN)
    width, hidden_units = MODEL_WIDTH, HIDDEN_UNITS
    pairs = width // 128
    plan = [(prompt_rows, width, False)] + [(a.shape[0], a.shape[1], True) for a in shards]
    count = len(plan)
    whole = [(i, 0, plan[i][0], 0, plan[i][1]) for i in range(count)]
    part = plan[6][0] // 4
    cut = [whole[0], (3, 0, plan[3][0], width, width), (3, 0, plan[3][0], 2 * width, width)]
    cut += [whole[1], whole[2], (3, 0, plan[3][0], 0, width), whole[4]]
    cut += [(5, 0, plan[5][0], i * width, width) for i in range(4)]
    cut += [(6, i * part, part, 0, width) for i in range(4)]
    lengths, chunks, gathered, sems = gather_plan(groups, plan, cut)
    dma = pltpu.SemaphoreType.DMA
    bf, f32 = jnp.bfloat16, jnp.float32

    def kernel(id_ref, tokens_ref, cot_ref, gains_ref, bias_ref, *refs):
        ins = (tokens_ref,) + refs[: count - 1]
        refs = refs[count - 1 :]
        q_out, kv_out, ctx_out, lse_out, act_out, dh_out, dc_out = refs[:7]
        early_out, inner_out, down_out, up_out = refs[7:11]
        outs, refs = refs[11 : 11 + count], refs[11 + count :]
        (
            prompt_v,
            norm_v,
            weight_v,
            w_out_v,
            q_v,
            kv_v,
            wide_v,
            ctx_v,
            lse_v,
            h_v,
            n_v,
            gl_v,
            gp_v,
            dn_v,
            downs_v,
            ups_v,
            down_v,
            up_v,
            low_v,
            turned_v,
            d_low,
            d_turned,
            acc_low,
            acc_turned,
            down_e,
            up_e,
            in_sem,
            out_sem,
        ) = refs[:28]
        enter, tick, ready, ready_kind, finish = gather_stages(groups, lengths, chunks, ins, outs, refs[28:])
        adapter = id_ref[0, 0]
        seq = lax.axis_index("seq")
        grp = lax.axis_index("grp")

        def load(src, dst, sem):
            copy = pltpu.make_async_copy(src, dst, in_sem.at[sem])
            copy.start()
            return copy

        stores, store_sem = [], iter(range(8))

        def store(src, dst):
            copy = pltpu.make_async_copy(src, dst, out_sem.at[next(store_sem)])
            copy.start()
            stores.append(copy)
            return copy

        def settle(copy):
            copy.wait()
            stores[:] = [other for other in stores if other is not copy]

        def bias(start, size):
            return bias_ref[:, pl.ds(pl.multiple_of(start, 128), size)]

        def tile(i, size=TILE, first=0):
            return pl.ds(pl.multiple_of(i * size + first, 128), size)

        def read_tokens(start):
            at = pl.multiple_of(start + prompt_rows, 128)
            return tokens_ref[pl.ds(at, 128)].astype(f32)

        def write_later(start, values):
            norm_v[pl.ds(pl.multiple_of(start + prompt_total, 128), 128)] = values

        def read_prompt(start):
            return prompt_v[pl.ds(start, 128)].astype(f32)

        def write_prompt(start, values):
            norm_v[pl.ds(start, 128)] = values

        def read_hidden(start):
            return h_v[pl.ds(start, 128)]

        def write_hidden(start, values):
            n_v[pl.ds(start, 128)] = values

        def inner(which, values, down):
            low_v[which] = dot_nt(values, down).astype(bf)
            turned_v[which] = dot_nt(down, values).astype(bf)

        def d_inner(which, values, up):
            d_low[which] = dot_nt(values, up).astype(bf)
            d_turned[which] = dot_nt(up, values).astype(bf)

        enter()
        tick(0)
        shift_one = bias_ref[:, :width]
        normalize_rows(read_tokens, write_later, CONT_LEN, gains_ref[0:1], shift_one)
        tick(1)
        ready(0)
        load(outs[0], prompt_v, 0).wait()
        normalize_rows(read_prompt, write_prompt, prompt_total, gains_ref[0:1], shift_one)
        for t in range(2, 6):
            tick(t)

        def weight_part(i, sem):
            cols = slice(i * width, (i + 1) * width)
            return load(outs[3].at[:, cols], weight_v.at[:, cols], sem)

        def prompt_tile(i, carry):
            shift = jnp.where(i >= 8, bias(i * TILE + width, TILE), 0.0)
            early = dot_nn(norm_v[:prompt_total], weight_v[:, tile(i)])
            kv_v[:prompt_total, tile(i - 4)] = (early + shift).astype(bf)
            return carry

        ready(1)
        weight_part(1, 1).wait()
        lax.fori_loop(4, 8, prompt_tile, 0)
        tick(6)
        ready(2)
        weight_part(2, 2).wait()
        lax.fori_loop(8, 12, prompt_tile, 0)
        tick(7)
        ready(3)
        copy_down = load(outs[1], downs_v, 3)
        tick(8)
        ready(4)
        copy_up = load(outs[2], ups_v, 4)
        copy_down.wait()
        copy_up.wait()
        at = lax.broadcasted_iota(jnp.int32, (ADAPTER_RANK, downs_v.shape[0]), 1)
        rank = lax.broadcasted_iota(jnp.int32, (ADAPTER_RANK, downs_v.shape[0]), 0)
        for part in range(4):
            chosen = (at == rank + (adapter * 64 + part * 16)).astype(bf)
            down_v[:, part * QUARTER : (part + 1) * QUARTER] = dot_nn(chosen, downs_v[...]).astype(
                bf
            )
            chosen = quarter_rows(ups_v.shape[0], adapter * 64, part, False)
            for first, start, size in zip(UP_FIRST, UP_STARTS, UP_SECTIONS):
                size //= 4
                up_v[:, first + part * size : first + (part + 1) * size] = dot_nn(
                    chosen, ups_v[:, start : start + size]
                ).astype(bf)
        down_out[...] = down_v[:, :width]
        up_out[...] = up_v[:, : 3 * width]
        inner(0, norm_v[prompt_total:], down_v[:, :width])
        inner_out[...] = turned_v[0]
        d_inner(3, cot_ref[prompt_rows:], up_v[:, UP_FIRST[3] :])
        def later_tile(i):
            weight = weight_v[:, tile(i)]
            return dot_nn(norm_v[prompt_total:], weight) + dot_nn(low_v[0], up_v[:, tile(i)])

        def key_tile(i, carry):
            shift = jnp.where(i >= 8, bias(i * TILE + width, TILE), 0.0)
            kv_v[prompt_total:, tile(i - 4)] = (later_tile(i) + shift).astype(bf)
            return carry

        def query_tile(i, carry):
            shift = bias(i * TILE + 2 * width, TILE)
            q_v[prompt_rows:, tile(i)] = (later_tile(i) + shift).astype(bf)
            mine = norm_v[pl.ds(pl.multiple_of(seq * prompt_rows, 128), prompt_rows)]
            q_v[:prompt_rows, tile(i)] = (dot_nn(mine, weight_v[:, tile(i)]) + shift).astype(bf)
            return carry

        tick(9)
        lax.fori_loop(4, 12, key_tile, 0)
        kv_store = store(kv_v, kv_out)
        ready(5)
        weight_part(0, 5).wait()
        lax.fori_loop(0, 4, query_tile, 0)
        q_store = store(q_v, q_out)

        def attend(i, carry):
            cols = pl.ds(pl.multiple_of(i * 128, 128), 128)
            values = pl.ds(pl.multiple_of(i * 128 + width, 128), 128)

            for at in range(pairs):
                pl.when(i == at)(functools.partial(tick, 10 + at))

            attention_forward(
                sizes,
                q_v.at[:, cols],
                kv_v.at[:, cols],
                kv_v.at[:, values],
                ctx_v.at[:, cols],
                lse_v.at[:, cols],
                wide_v,
            )
            return carry

        lax.fori_loop(0, pairs, attend, 0)
        store(ctx_v, ctx_out)
        lse_store = store(lse_v, lse_out)
        tick(18)
        ready(6)
        load_out = load(outs[4], w_out_v, 6)
        ready(7)

        def hidden_part(i):
            cols = slice(i * width, (i + 1) * width)
            return load(outs[5].at[:, cols], weight_v.at[:, cols], 7 + i)

        hidden_loads = [hidden_part(0)]
        load_out.wait()
        inner(1, ctx_v[prompt_rows:], down_v[:, width : 2 * width])

        def out_tile(j, carry):
            cols = tile(j)
            mixed = dot_nn(ctx_v[...], w_out_v[:, cols]) + bias(j * TILE + 4 * width, TILE)
            mixed = tokens_ref[:, cols].astype(f32) + mixed
            extra = dot_nn(low_v[1], up_v[:, tile(j, first=UP_FIRST[1])])
            h_v[:prompt_rows, cols] = mixed[:prompt_rows]
            h_v[prompt_rows:, cols] = mixed[prompt_rows:] + extra
            return carry

        lax.fori_loop(0, 4, out_tile, 0)
        tick(19)
        normalize_rows(
            read_hidden, write_hidden, rows, gains_ref[1:2], bias_ref[:, width : 2 * width]
        )
        inner(2, n_v[prompt_rows:], down_v[:, 2 * width : 3 * width])
        settle(lse_store)
        sum_v = lse_v

        def start_sums(start):
            at = pl.ds(start, 128)
            sum_v[at] = h_v[at] + bias_ref[:, 5 * width : 6 * width]
            dn_v[at] = jnp.zeros((128, width), f32)

        for_blocks(rows, start_sums)
        tick(20)

        def hidden_tile(i, carry):
            cols = tile(i)

            wide = dot_nn(n_v[...], weight_v[:, cols]) + bias(i * TILE + 6 * width, TILE)
            extra = dot_nn(low_v[2], up_v[:, tile(i, first=UP_FIRST[2])])
            for at, field in (
                (slice(0, prompt_rows), wide[:prompt_rows]),
                (slice(prompt_rows, rows), wide[prompt_rows:] + extra),
            ):
                value, slope = gelu_both(field)
                gl_v[at, cols] = value.astype(bf)
                gp_v[at, cols] = slope.astype(bf)
            return carry

        for i in range(4):
            hidden_loads[i].wait()
            if i < 3:
                ready(8 + i)
                hidden_loads.append(hidden_part(i + 1))
            lax.fori_loop(i * 4, i * 4 + 4, hidden_tile, 0)
            if i < 2:
                tick(21 + i)
        settle(kv_store)
        tick(23)

        df_v = norm_v.at[:rows]
        part_rows = hidden_units // 4
        for which in range(2):
            acc_low[which] = jnp.zeros((CONT_LEN, ADAPTER_RANK), f32)
            acc_turned[which] = jnp.zeros((ADAPTER_RANK, CONT_LEN), f32)
        gx, gy = lax.rem(grp, 2), grp // 2

        def unit_part(kind, carry):
            pl.when(kind == 1)(functools.partial(tick, 24))
            for ch in range(11, 15):
                ready_kind(ch, kind)
            unit_x = lax.rem(gx + kind, 2)
            unit_y = lax.rem(gy + kind // 2, 2)
            base = pl.multiple_of((unit_y * 2 + unit_x) * part_rows, part_rows)
            part = pl.ds(base, part_rows)
            down_part = pl.ds(pl.multiple_of(base + 3 * width, width), part_rows)
            up_part = pl.ds(pl.multiple_of(base + UP_FIRST[2], width), part_rows)
            slot = kv_v.at[:part_rows, :width]
            load(outs[6].at[part], slot, 11).wait()

            def d_hidden(j, carry):
                cols = tile(j, WIDE, base)
                wide = dot_nt(cot_ref[...], slot[tile(j, WIDE)])
                extra = dot_nn(d_low[3], down_v[:, tile(j, WIDE, base + 3 * width)])
                slope = gp_v[:, cols].astype(f32)
                to = tile(j, WIDE)
                df_v[:prompt_rows, to] = (wide[:prompt_rows] * slope[:prompt_rows]).astype(bf)
                later = (wide[prompt_rows:] + extra) * slope[prompt_rows:]
                df_v[prompt_rows:, to] = later.astype(bf)
                return carry

            lax.fori_loop(0, part_rows // WIDE, d_hidden, 0)
            df_later = df_v[prompt_rows:]
            gl_later = gl_v[prompt_rows:, part]
            acc_low[0] += dot_nt(df_later, up_v[:, up_part])
            acc_turned[0] += dot_nt(up_v[:, up_part], df_later)
            acc_low[1] += dot_nt(gl_later, down_v[:, down_part])
            acc_turned[1] += dot_nt(down_v[:, down_part], gl_later)
            down_e[:, down_part] = dot_nn(d_turned[3], gl_later).astype(bf)
            up_e[:, up_part] = dot_nn(turned_v[2], df_later).astype(bf)

            def sums(j, carry):
                cols = tile(j, WIDE)
                sum_v[:, cols] += dot_nn(gl_v[:, part], slot[:, cols])
                dn_v[:, cols] += dot_nt(df_v[...], weight_v[cols, part])
                return carry

            lax.fori_loop(0, width // WIDE, sums, 0)
            return carry

        lax.fori_loop(0, 4, unit_part, 0)
        d_low[2] = acc_low[0].astype(bf)
        d_turned[2] = acc_turned[0].astype(bf)
        low_v[3] = acc_low[1].astype(bf)
        turned_v[3] = acc_turned[1].astype(bf)
        act_v, attn_v, dc_v = prompt_v.at[:rows], q_v, norm_v.at[:rows]

        def last_tile(j, carry):
            cols = tile(j)
            dn_v[prompt_rows:, cols] += dot_nn(d_low[2], down_v[:, tile(j, first=2 * width)])
            act_v[:prompt_rows, cols] = sum_v[:prompt_rows, cols].astype(bf)
            extra = dot_nn(low_v[3], up_v[:, tile(j, first=UP_FIRST[3])])
            act_v[prompt_rows:, cols] = (sum_v[prompt_rows:, cols] + extra).astype(bf)
            return carry

        lax.fori_loop(0, width // TILE, last_tile, 0)
        store(act_v, act_out)
        settle(q_store)

        def pull_rows(start):
            at = pl.ds(start, 128)
            grads = cot_ref[at].astype(f32) + norm_pull(h_v[at], dn_v[at], gains_ref[1:2])
            dn_v[at] = grads
            attn_v[at] = grads.astype(bf)

        for_blocks(rows, pull_rows)
        store(dn_v, dh_out)
        d_inner(1, attn_v[prompt_rows:], up_v[:, UP_FIRST[1] : UP_FIRST[2]])

        def context_tile(j, carry):
            cols = tile(j)
            wide = dot_nt(attn_v[...], w_out_v[cols])
            extra = dot_nn(d_low[1], down_v[:, tile(j, first=width)])
            dc_v[:prompt_rows, cols] = wide[:prompt_rows].astype(bf)
            dc_v[prompt_rows:, cols] = (wide[prompt_rows:] + extra).astype(bf)
            return carry

        lax.fori_loop(0, width // TILE, context_tile, 0)
        store(dc_v, dc_out)
        down_e[:, :width] = jnp.zeros((ADAPTER_RANK, width), bf)
        down_e[:, width : 2 * width] = dot_nn(d_turned[1], ctx_v[prompt_rows:]).astype(bf)
        down_e[:, 2 * width : 3 * width] = dot_nn(d_turned[2], n_v[prompt_rows:]).astype(bf)
        up_e[:, UP_FIRST[1] : UP_FIRST[2]] = dot_nn(turned_v[1], attn_v[prompt_rows:]).astype(bf)
        up_e[:, UP_FIRST[3] :] = dot_nn(turned_v[3], cot_ref[prompt_rows:]).astype(bf)
        for quarter in range(4):
            early_out[quarter, :, :QUARTER] = down_e[:, quarter * QUARTER : (quarter + 1) * QUARTER]
        for section in range(1, 4):
            size = UP_SECTIONS[section] // 4
            moved = jnp.zeros((64, size), f32)
            for part in range(4):
                first = UP_FIRST[section] + part * size
                moved += dot_nn(quarter_rows(64, 0, part, True), up_e[:, first : first + size])
            first = QUARTER + UP_STARTS[section] - UP_STARTS[1]
            for quarter in range(4):
                early_out[quarter, :, first : first + size] = moved[
                    16 * quarter : 16 * quarter + 16
                ].astype(bf)
        for ch in range(len(chunks)):
            finish(ch)
        for copy in stores:
            copy.wait()

    vmem = pl.BlockSpec(memory_space=pltpu.VMEM)
    hbm = pl.BlockSpec(memory_space=pl.ANY)
    return pl.pallas_call(
        kernel,
        in_specs=[pl.BlockSpec(memory_space=pltpu.SMEM)] + [vmem] * (3 + count),
        out_specs=[hbm] * 7 + [vmem] * 4 + [hbm] * count,
        out_shape=[
            jax.ShapeDtypeStruct((rows, width), bf),
            jax.ShapeDtypeStruct((keys, 2 * width), bf),
            jax.ShapeDtypeStruct((rows, width), bf),
            jax.ShapeDtypeStruct((rows, width), f32),
            jax.ShapeDtypeStruct((rows, width), bf),
            jax.ShapeDtypeStruct((rows, width), f32),
            jax.ShapeDtypeStruct((rows, width), bf),
            jax.ShapeDtypeStruct((4, 16, EARLY_COLS), bf),
            jax.ShapeDtypeStruct((ADAPTER_RANK, CONT_LEN), bf),
            jax.ShapeDtypeStruct((ADAPTER_RANK, width), bf),
            jax.ShapeDtypeStruct((ADAPTER_RANK, 3 * width), bf),
        ]
        + gathered,
        scratch_shapes=[
            pltpu.VMEM((prompt_total, width), bf),
            pltpu.VMEM((keys, width), bf),
            pltpu.VMEM((width, hidden_units), bf),
            pltpu.VMEM((width, width), bf),
            pltpu.VMEM((rows, width), bf),
            pltpu.VMEM((keys, 2 * width), bf),
            pltpu.VMEM((keys, 256), bf),
            pltpu.VMEM((rows, width), bf),
            pltpu.VMEM((rows, width), f32),
            pltpu.VMEM((rows, width), f32),
            pltpu.VMEM((rows, width), bf),
            pltpu.VMEM((rows, hidden_units), bf),
            pltpu.VMEM((rows, hidden_units), bf),
            pltpu.VMEM((rows, width), f32),
            pltpu.VMEM(gathered[1].shape, bf),
            pltpu.VMEM(gathered[2].shape, bf),
            pltpu.VMEM((ADAPTER_RANK, 4 * QUARTER), bf),
            pltpu.VMEM((ADAPTER_RANK, 4 * UP_QUARTER), bf),
            pltpu.VMEM((4, CONT_LEN, ADAPTER_RANK), bf),
            pltpu.VMEM((4, ADAPTER_RANK, CONT_LEN), bf),
            pltpu.VMEM((4, CONT_LEN, ADAPTER_RANK), bf),
            pltpu.VMEM((4, ADAPTER_RANK, CONT_LEN), bf),
            pltpu.VMEM((2, CONT_LEN, ADAPTER_RANK), f32),
            pltpu.VMEM((2, ADAPTER_RANK, CONT_LEN), f32),
            pltpu.VMEM((ADAPTER_RANK, 4 * QUARTER), bf),
            pltpu.VMEM((ADAPTER_RANK, 4 * UP_QUARTER), bf),
            dma((13,)),
            dma((8,)),
        ]
        + sems,
        compiler_params=pltpu.CompilerParams(
            collective_id=collective_id, has_side_effects=True, vmem_limit_bytes=VMEM_LIMIT
        ),
    )(ident, tokens, cotangent, gains, biases, *shards)


def adapter_scratch(cols):
    dma = pltpu.SemaphoreType.DMA
    return [
        pltpu.VMEM((2, 16, cols), jnp.bfloat16),
        pltpu.VMEM((16, 128), jnp.bfloat16),
        pltpu.VMEM((3, 4, 16, cols), jnp.bfloat16),
        pltpu.VMEM((3, 4, 16, cols), jnp.bfloat16),
        pltpu.VMEM((4, 16, cols), jnp.float32),
        pltpu.VMEM((3, 16, cols), jnp.bfloat16),
        pltpu.VMEM((3, 16, cols), jnp.bfloat16),
        dma((3,)),
        dma((3,)),
        dma((3,)),
        dma((3,)),
        dma((3,)),
        dma((3,)),
    ]


def adapter_stages(term_ref, id_ref, out_ref, scratch):
    from_core, other_id, to_grp, from_grp, total, to_z, from_z = scratch[:7]
    a_send, a_recv, g_send, g_recv, z_send, z_recv = scratch[7:]
    g, s = lax.axis_index("grp"), lax.axis_index("seq")
    core, z = lax.rem(s, 2), s // 2
    other = 1 - core
    partner = (g, z * 2 + other)
    grps = [lax.rem(g + d, 4) for d in range(1, 4)]
    lines = [lax.rem(z + d, 4) for d in range(1, 4)]

    def enter():
        peers = [partner] + [(far, s) for far in grps] + [(g, far * 2 + core) for far in lines]
        barrier = pltpu.get_barrier_semaphore()
        for peer in peers:
            pl.semaphore_signal(barrier, inc=1, device_id=peer, device_id_type=MESH)
        pl.semaphore_wait(barrier, len(peers))

    def remote(src, dst, send_sem, recv_sem, device):
        return pltpu.make_async_remote_copy(
            src_ref=src,
            dst_ref=dst,
            send_sem=send_sem,
            recv_sem=recv_sem,
            device_id=device,
            device_id_type=MESH,
        )

    copies_a = [
        remote(term_ref.at[i * 2 + other], from_core.at[i], a_send.at[i], a_recv.at[i], partner)
        for i in range(2)
    ] + [remote(id_ref, other_id, a_send.at[2], a_recv.at[2], partner)]
    copies_g = [
        remote(to_grp.at[d], from_grp.at[d], g_send.at[d], g_recv.at[d], (grps[d], s))
        for d in range(3)
    ]
    copies_z = [
        remote(to_z.at[d], from_z.at[d], z_send.at[d], z_recv.at[d], (g, lines[d] * 2 + core))
        for d in range(3)
    ]

    def start(copies):
        for copy in copies:
            copy.start()

    def wait(copies):
        for copy in copies:
            copy.wait()

    def select():
        wait(copies_a)
        mine = id_ref[0:1, 0:1].astype(jnp.float32)
        theirs = other_id[0:1, 0:1].astype(jnp.float32)
        for d, grp in enumerate(grps + [g]):
            for slot in range(4):
                adapter = (grp * 2 + slot // 2).astype(jnp.float32)
                own_term = term_ref[(slot % 2) * 2 + core].astype(jnp.float32)
                other_term = from_core[slot % 2].astype(jnp.float32)
                picked = jnp.where(mine == adapter, own_term, 0.0) + jnp.where(
                    theirs == adapter, other_term, 0.0
                )
                if d < 3:
                    to_grp[d, slot] = picked.astype(jnp.bfloat16)
                else:
                    total[slot] = picked

    def add_grps():
        wait(copies_g)
        for slot in range(4):
            total[slot] += sum(from_grp[d, slot].astype(jnp.float32) for d in range(3))
        for d in range(3):
            to_z[d] = total[lines[d]].astype(jnp.bfloat16)

    def add_lines():
        wait(copies_z)
        out_ref[...] = total[z] + sum(from_z[d].astype(jnp.float32) for d in range(3))

    return (
        enter,
        lambda: start(copies_a),
        select,
        lambda: start(copies_g),
        add_grps,
        lambda: start(copies_z),
        add_lines,
    )


LATE_COLS = MODEL_WIDTH + UP_STARTS[1]


def backward_tail(
    groups, q, kv, d_ctx, ctx, lse, early, ident, tokens, d_hidden, gains, biases, w_qkv, adapters,
    collective_id,
):
    rows, keys, pairs = q.shape[0], kv.shape[0], q.shape[1] // 128
    prompt_rows, prompt_total = rows - CONT_LEN, keys - CONT_LEN
    sizes = (prompt_rows, prompt_total, CONT_LEN)
    width, z_n = MODEL_WIDTH, groups[1] // 2
    bf, f32 = jnp.bfloat16, jnp.float32
    dma = pltpu.SemaphoreType.DMA
    adapter_shapes = len(adapter_scratch(128))

    def kernel(
        q_ref, k_ref, v_ref, d_ref, ctx_ref, lse_ref, early_ref, id_ref, tokens_ref, gains_ref,
        bias_ref, inner_ref, down_ref, up_ref, dh_hbm, w_hbm, *refs
    ):
        x_out, down_out, up_out = refs[:3]
        k_sum, v_sum, dqkv_v, term_v, pair_in, to_line, from_line = refs[3:10]
        w_v, dh_v, dn_v, n_v, late_v, early_sum, late_sum = refs[10:17]
        p_send, p_recv, l_send, l_recv, in_sem, out_sem = refs[17:23]
        scratch = refs[23:]
        e_enter, e_core, e_select, e_grp, e_add, e_z, e_lines = adapter_stages(
            early_ref, id_ref, early_sum, scratch[:adapter_shapes]
        )
        _, l_core, l_select, l_grp, l_add, l_z, l_lines = adapter_stages(
            late_v, id_ref, late_sum, scratch[adapter_shapes:]
        )
        g, s = lax.axis_index("grp"), lax.axis_index("seq")
        core, z = lax.rem(s, 2), s // 2
        far_z = [lax.rem(z + d, z_n) for d in range(1, z_n)]
        step = pl.program_id(0)

        def across(i):
            return pltpu.make_async_remote_copy(
                src_ref=term_v.at[i, 1 - core],
                dst_ref=pair_in.at[i],
                send_sem=p_send.at[i],
                recv_sem=p_recv.at[i],
                device_id=(g, z * 2 + 1 - core),
                device_id_type=MESH,
            )

        def along(i, d):
            return pltpu.make_async_remote_copy(
                src_ref=to_line.at[i, d],
                dst_ref=from_line.at[i, d],
                send_sem=l_send.at[i, d],
                recv_sem=l_recv.at[i, d],
                device_id=(g, far_z[d] * 2 + core),
                device_id_type=MESH,
            )

        def pass_on(i):
            across(i).wait()
            for d, far in enumerate(far_z):
                both = term_v[i, core, far].astype(f32) + pair_in[i, far].astype(f32)
                to_line[i, d] = both.astype(bf)
                along(i, d).start()

        load_w = pltpu.make_async_copy(w_hbm, w_v, in_sem.at[0])
        load_dh = pltpu.make_async_copy(dh_hbm, dh_v, in_sem.at[1])

        @pl.when(step == 0)
        def _():
            e_enter()
            e_core()
            load_w.start()
            load_dh.start()

        cols = pl.ds(pl.multiple_of(step * 128, 128), 128)
        attention_backward(
            sizes, q_ref, k_ref, v_ref, d_ref, ctx_ref, lse_ref, dqkv_v.at[:, cols], k_sum, v_sum
        )
        for block in range(2 * z_n):
            at = slice(block * prompt_rows, (block + 1) * prompt_rows)
            half = block % 2, block // 2
            term_v[step, half[0], half[1], :, :128] = (k_sum[at] * 0.125).astype(bf)
            term_v[step, half[0], half[1], :, 128:] = v_sum[at].astype(bf)
        across(step).start()
        for part, (total, scale) in enumerate(((k_sum, 0.125), (v_sum, 1.0))):
            to = pl.ds(pl.multiple_of(step * 128 + (part + 1) * width, 128), 128)
            dqkv_v[prompt_rows:, to] = (total[prompt_total:] * scale).astype(bf)

        @pl.when(step >= 1)
        def _():
            pass_on(step - 1)

        @pl.when(step == 1)
        def _():
            e_select()
            e_grp()

            def read(start):
                return tokens_ref[pl.ds(pl.multiple_of(start + prompt_rows, 128), 128)].astype(f32)

            def write(start, values):
                n_v[pl.ds(start, 128)] = values

            normalize_rows(read, write, CONT_LEN, gains_ref[0:1], bias_ref[:, :width])

        @pl.when(step == pairs // 2)
        def _():
            e_add()
            e_z()

        @pl.when(step == pairs - 1)
        def _():
            later = dqkv_v[prompt_rows:]
            d_low = dot_nt(later, up_ref[...]).astype(bf)
            d_turned = dot_nt(up_ref[...], later).astype(bf)
            late_v[...] = jnp.zeros(late_v.shape, bf)
            late_v[0, :, :width] = dot_nn(d_turned, n_v[...]).astype(bf)
            size = UP_SECTIONS[0] // 4
            moved = jnp.zeros((64, size), f32)
            for part in range(4):
                grads = dot_nn(inner_ref[...], dqkv_v[prompt_rows:, part * size : (part + 1) * size])
                moved += dot_nn(quarter_rows(64, 0, part, True), grads.astype(bf))
            for quarter in range(4):
                late_v[quarter, :, width:] = moved[16 * quarter : 16 * quarter + 16].astype(bf)
            l_core()
            pass_on(pairs - 1)
            l_select()
            l_grp()
            load_w.wait()
            load_dh.wait()

            def pull(first, count):
                def body(start):
                    at = pl.ds(pl.multiple_of(start + first, 128), 128)
                    values = tokens_ref[at].astype(f32)
                    dn_v[at] = dh_v[at] + norm_pull(values, dn_v[at], gains_ref[0:1])

                for_blocks(count, body)
                copy = pltpu.make_async_copy(
                    dn_v.at[first : first + count], x_out.at[first : first + count],
                    out_sem.at[0 if first else 1],
                )
                copy.start()
                return copy

            def later_tile(j, carry):
                to = pl.ds(pl.multiple_of(j * TILE, TILE), TILE)
                wide = dot_nt(dqkv_v[prompt_rows:], w_v[to]) + dot_nn(d_low, down_ref[:, to])
                dn_v[prompt_rows:, to] = wide
                return carry

            lax.fori_loop(0, width // TILE, later_tile, 0)
            later_store = pull(prompt_rows, CONT_LEN)
            l_add()
            l_z()
            e_lines()

            def arrived(i, carry):
                total = term_v[i, core, z].astype(f32) + pair_in[i, z].astype(f32)
                for d in range(z_n - 1):
                    along(i, d).wait()
                    total = total + from_line[i, d].astype(f32)
                for part in range(2):
                    to = pl.ds(pl.multiple_of(i * 128 + (part + 1) * width, 128), 128)
                    dqkv_v[:prompt_rows, to] = total[:, part * 128 : part * 128 + 128].astype(bf)
                return carry

            lax.fori_loop(0, pairs, arrived, 0)

            def prompt_tile(j, carry):
                to = pl.ds(pl.multiple_of(j * TILE, TILE), TILE)
                dn_v[:prompt_rows, to] = dot_nt(dqkv_v[:prompt_rows], w_v[to])
                return carry

            lax.fori_loop(0, width // TILE, prompt_tile, 0)
            prompt_store = pull(0, prompt_rows)
            l_lines()
            down_out[:, :width] = early_sum[:, :width] + late_sum[:, :width]
            down_out[:, width:] = early_sum[:, width:QUARTER]
            up_out[:, : UP_STARTS[1]] = late_sum[:, width:]
            up_out[:, UP_STARTS[1] :] = early_sum[:, QUARTER:]
            later_store.wait()
            prompt_store.wait()

    def pair(i):
        return (0, i)

    row_spec = pl.BlockSpec((rows, 128), pair)
    key_spec = pl.BlockSpec((keys, 128), pair)
    whole = pl.BlockSpec(memory_space=pltpu.VMEM)
    hbm = pl.BlockSpec(memory_space=pl.ANY)
    return pl.pallas_call(
        kernel,
        grid=(pairs,),
        in_specs=[
            row_spec,
            key_spec,
            pl.BlockSpec((keys, 128), lambda i: (0, pairs + i)),
            row_spec,
            row_spec,
            row_spec,
        ]
        + [whole] * 8
        + [hbm] * 2,
        out_specs=[hbm, whole, whole],
        out_shape=[
            jax.ShapeDtypeStruct((rows, width), f32),
            jax.ShapeDtypeStruct((16, QUARTER), f32),
            jax.ShapeDtypeStruct((16, UP_QUARTER), f32),
        ],
        scratch_shapes=[
            pltpu.VMEM((keys, 128), f32),
            pltpu.VMEM((keys, 128), f32),
            pltpu.VMEM((rows, 3 * width), bf),
            pltpu.VMEM((pairs, 2, z_n, prompt_rows, 256), bf),
            pltpu.VMEM((pairs, z_n, prompt_rows, 256), bf),
            pltpu.VMEM((pairs, z_n - 1, prompt_rows, 256), bf),
            pltpu.VMEM((pairs, z_n - 1, prompt_rows, 256), bf),
            pltpu.VMEM((width, 3 * width), bf),
            pltpu.VMEM((rows, width), f32),
            pltpu.VMEM((rows, width), f32),
            pltpu.VMEM((CONT_LEN, width), bf),
            pltpu.VMEM((4, 16, LATE_COLS), bf),
            pltpu.VMEM((16, EARLY_COLS), f32),
            pltpu.VMEM((16, LATE_COLS), f32),
            dma((pairs,)),
            dma((pairs,)),
            dma((pairs, z_n - 1)),
            dma((pairs, z_n - 1)),
            dma((2,)),
            dma((2,)),
        ]
        + adapter_scratch(EARLY_COLS)
        + adapter_scratch(LATE_COLS),
        compiler_params=pltpu.CompilerParams(
            collective_id=collective_id, has_side_effects=True, vmem_limit_bytes=VMEM_LIMIT
        ),
    )(
        q, kv, kv, d_ctx, ctx, lse, early, ident, tokens, gains, biases, *adapters, d_hidden, w_qkv
    )


def local_general(
    tokens,
    cotangent,
    query_key_value_weight,
    attention_out_weight,
    feedforward_in_weight,
    feedforward_out_weight,
    layer_norm_gains,
    biases,
    adapter_down_matrices,
    adapter_up_matrices,
    adapter_of_continuation,
):
    row_count = tokens.shape[0]
    prompt_rows = row_count - CONT_LEN
    prompt_total = prompt_rows * lax.axis_size("seq")
    key_count = prompt_total + CONT_LEN
    seq_index = lax.axis_index("seq")
    adapter_index = adapter_of_continuation[0, 0]
    weight_shards = (
        query_key_value_weight,
        attention_out_weight,
        feedforward_in_weight,
        feedforward_out_weight,
        adapter_down_matrices,
        adapter_up_matrices,
    )
    gathered_rows = (
        lax.all_gather(weight_shards[0], ("grp", "seq"), axis=0, tiled=True),
        lax.all_gather(weight_shards[1], ("grp", "seq"), axis=0, tiled=True),
        lax.all_gather(weight_shards[2], ("grp", "seq"), axis=0, tiled=True),
        lax.all_gather(weight_shards[3], ("grp", "seq"), axis=0, tiled=True),
        lax.all_gather(weight_shards[4], ("grp", "seq"), axis=0, tiled=True),
        lax.all_gather(weight_shards[5], ("grp", "seq"), axis=0, tiled=True),
    )
    weight_matrices, adapter_sections = unpack_sections(gathered_rows, adapter_index)
    frozen_query_key_value, frozen_attention_out, frozen_feedforward_in, frozen_feedforward_out = (
        weight_matrices
    )
    (
        down_query_key_value,
        down_attention_out,
        down_feedforward_in,
        down_feedforward_out,
        up_query_key_value,
        up_attention_out,
        up_feedforward_in,
        up_feedforward_out,
    ) = adapter_sections
    shift_one = biases[:MODEL_WIDTH]
    shift_two = biases[MODEL_WIDTH : 2 * MODEL_WIDTH]
    query_key_value_bias = jnp.concatenate(
        [
            biases[2 * MODEL_WIDTH : 3 * MODEL_WIDTH],
            jnp.zeros((MODEL_WIDTH,), jnp.float32),
            biases[3 * MODEL_WIDTH : 4 * MODEL_WIDTH],
        ]
    )
    bias_out = biases[4 * MODEL_WIDTH : 5 * MODEL_WIDTH]
    bias_proj = biases[5 * MODEL_WIDTH : 6 * MODEL_WIDTH]
    bias_fc = biases[6 * MODEL_WIDTH :]
    inputs = tokens.astype(jnp.float32)
    normed_one = layer_norm(inputs, layer_norm_gains[0], shift_one).astype(jnp.bfloat16)
    inner_one = product(normed_one[prompt_rows:], down_query_key_value).astype(jnp.bfloat16)
    mixed_query_key_value = product(normed_one, frozen_query_key_value) + query_key_value_bias
    mixed_query_key_value = mixed_query_key_value.at[prompt_rows:].add(
        product(inner_one, up_query_key_value)
    )
    qkv_rows = mixed_query_key_value.astype(jnp.bfloat16)
    prompt_keys, prompt_values = (
        lax.all_gather(
            qkv_rows[:prompt_rows, MODEL_WIDTH : 2 * MODEL_WIDTH], "seq", axis=0, tiled=True
        ),
        lax.all_gather(qkv_rows[:prompt_rows, 2 * MODEL_WIDTH :], "seq", axis=0, tiled=True),
    )
    all_keys = jnp.concatenate(
        [prompt_keys, qkv_rows[prompt_rows:, MODEL_WIDTH : 2 * MODEL_WIDTH]], 0
    )
    all_values = jnp.concatenate([prompt_values, qkv_rows[prompt_rows:, 2 * MODEL_WIDTH :]], 0)
    allowed = visible(row_count, prompt_rows, prompt_total, key_count, seq_index)
    query_heads = split_heads(qkv_rows[:, :MODEL_WIDTH])
    key_heads = split_heads(all_keys)
    value_heads = split_heads(all_values)

    def forward_head(operands):
        query_head, key_head, value_head = operands
        scores = jnp.where(allowed, product_nt(query_head, key_head) * 0.125, NEGATIVE)
        row_max = jnp.max(scores, axis=1, keepdims=True)
        exp_scores = jnp.exp(scores - row_max)
        exp_total = jnp.sum(exp_scores, axis=1, keepdims=True)
        weights = (exp_scores / exp_total).astype(jnp.bfloat16)
        return (product(weights, value_head), (row_max + jnp.log(exp_total))[:, 0])

    head_contexts, log_total = lax.map(forward_head, (query_heads, key_heads, value_heads))
    attention_context = merge_heads(head_contexts).astype(jnp.bfloat16)
    inner_two = product(attention_context[prompt_rows:], down_attention_out).astype(jnp.bfloat16)
    attention_output = product(attention_context, frozen_attention_out) + bias_out
    attention_output = attention_output.at[prompt_rows:].add(product(inner_two, up_attention_out))
    hidden = inputs + attention_output
    normed_two = layer_norm(hidden, layer_norm_gains[1], shift_two).astype(jnp.bfloat16)
    inner_three = product(normed_two[prompt_rows:], down_feedforward_in).astype(jnp.bfloat16)
    before_activation = product(normed_two, frozen_feedforward_in) + bias_fc
    before_activation = before_activation.at[prompt_rows:].add(
        product(inner_three, up_feedforward_in)
    )
    activated_hidden = jax.nn.gelu(before_activation, approximate=True).astype(jnp.bfloat16)
    inner_four = product(activated_hidden[prompt_rows:], down_feedforward_out).astype(jnp.bfloat16)
    adapter_branch = product(activated_hidden, frozen_feedforward_out) + bias_proj
    adapter_branch = adapter_branch.at[prompt_rows:].add(product(inner_four, up_feedforward_out))
    outputs = (hidden + adapter_branch).astype(jnp.bfloat16)
    weight_matrices, adapter_sections = unpack_sections(
        (
            lax.all_gather(weight_shards[0], ("grp", "seq"), axis=0, tiled=True),
            lax.all_gather(weight_shards[1], ("grp", "seq"), axis=0, tiled=True),
            lax.all_gather(weight_shards[2], ("grp", "seq"), axis=0, tiled=True),
            lax.all_gather(weight_shards[3], ("grp", "seq"), axis=0, tiled=True),
            lax.all_gather(weight_shards[4], ("grp", "seq"), axis=0, tiled=True),
            lax.all_gather(weight_shards[5], ("grp", "seq"), axis=0, tiled=True),
        ),
        adapter_index,
    )
    frozen_query_key_value, frozen_attention_out, frozen_feedforward_in, frozen_feedforward_out = (
        weight_matrices
    )
    (
        down_query_key_value,
        down_attention_out,
        down_feedforward_in,
        down_feedforward_out,
        up_query_key_value,
        up_attention_out,
        up_feedforward_in,
        up_feedforward_out,
    ) = adapter_sections
    grad_inner_four = product_nt(cotangent[prompt_rows:], up_feedforward_out).astype(jnp.bfloat16)
    grad_act = product_nt(cotangent, frozen_feedforward_out)
    grad_act = grad_act.at[prompt_rows:].add(product_nt(grad_inner_four, down_feedforward_out))
    gelu_pull = jax.vjp(lambda field: jax.nn.gelu(field, approximate=True), before_activation)[1]
    grad_pre = gelu_pull(grad_act)[0].astype(jnp.bfloat16)
    grad_inner_three = product_nt(grad_pre[prompt_rows:], up_feedforward_in).astype(jnp.bfloat16)
    grad_normed_two = product_nt(grad_pre, frozen_feedforward_in)
    grad_normed_two = grad_normed_two.at[prompt_rows:].add(
        product_nt(grad_inner_three, down_feedforward_in)
    )
    second_pull = jax.vjp(lambda field: layer_norm(field, layer_norm_gains[1], shift_two), hidden)[
        1
    ]
    grad_hidden = cotangent.astype(jnp.float32) + second_pull(grad_normed_two)[0]
    grad_attn = grad_hidden.astype(jnp.bfloat16)
    grad_inner_two = product_nt(grad_attn[prompt_rows:], up_attention_out).astype(jnp.bfloat16)
    grad_context = product_nt(grad_attn, frozen_attention_out)
    grad_context = (
        grad_context.at[prompt_rows:]
        .add(product_nt(grad_inner_two, down_attention_out))
        .astype(jnp.bfloat16)
    )

    def backward_head(operands):
        query_head, key_head, value_head, grad_head, total_head = operands
        scores = jnp.where(allowed, product_nt(query_head, key_head) * 0.125, NEGATIVE)
        prob_full = jnp.exp(scores - total_head[:, None])
        weights = prob_full.astype(jnp.bfloat16)
        grad_weights = product_nt(grad_head, value_head)
        row_delta = jnp.sum(prob_full * grad_weights, axis=1, keepdims=True)
        grad_scores = (prob_full * (grad_weights - row_delta)).astype(jnp.bfloat16)
        return (
            product(grad_scores, key_head) * 0.125,
            product_tn(grad_scores, query_head) * 0.125,
            product_tn(weights, grad_head),
        )

    grad_q, grad_k, grad_v = lax.map(
        backward_head, (query_heads, key_heads, value_heads, split_heads(grad_context), log_total)
    )
    grad_query = merge_heads(grad_q)
    grad_keys = merge_heads(grad_k)
    grad_values = merge_heads(grad_v)
    own_keys, own_values = (
        lax.psum_scatter(
            grad_keys[:prompt_total].astype(jnp.bfloat16), "seq", scatter_dimension=0, tiled=True
        ).astype(jnp.float32),
        lax.psum_scatter(
            grad_values[:prompt_total].astype(jnp.bfloat16), "seq", scatter_dimension=0, tiled=True
        ).astype(jnp.float32),
    )
    grad_qkv = jnp.concatenate(
        [
            grad_query,
            jnp.concatenate([own_keys, grad_keys[prompt_total:]], 0),
            jnp.concatenate([own_values, grad_values[prompt_total:]], 0),
        ],
        1,
    ).astype(jnp.bfloat16)
    grad_inner_one = product_nt(grad_qkv[prompt_rows:], up_query_key_value).astype(jnp.bfloat16)
    grad_normed_one = product_nt(grad_qkv, frozen_query_key_value)
    grad_normed_one = grad_normed_one.at[prompt_rows:].add(
        product_nt(grad_inner_one, down_query_key_value)
    )
    first_pull = jax.vjp(lambda field: layer_norm(field, layer_norm_gains[0], shift_one), inputs)[1]
    input_grad = grad_hidden + first_pull(grad_normed_one)[0]
    down_term = jnp.concatenate(
        [
            product_tn(normed_one[prompt_rows:], grad_inner_one),
            product_tn(attention_context[prompt_rows:], grad_inner_two),
            product_tn(normed_two[prompt_rows:], grad_inner_three),
            product_tn(activated_hidden[prompt_rows:], grad_inner_four),
        ],
        0,
    )
    up_term = jnp.concatenate(
        [
            product_tn(inner_one, grad_qkv[prompt_rows:]),
            product_tn(inner_two, grad_attn[prompt_rows:]),
            product_tn(inner_three, grad_pre[prompt_rows:]),
            product_tn(inner_four, cotangent[prompt_rows:]),
        ],
        1,
    )
    select = (jnp.arange(ADAPTER_COUNT, dtype=jnp.int32) == adapter_index).astype(jnp.float32)
    down_grad, up_grad = (
        lax.psum_scatter(
            (select[:, None, None] * down_term[None]).reshape(-1),
            ("grp", "seq"),
            scatter_dimension=0,
            tiled=True,
        ),
        lax.psum_scatter(
            (select[:, None, None] * up_term[None]).reshape(-1),
            ("grp", "seq"),
            scatter_dimension=0,
            tiled=True,
        ),
    )
    return (outputs, input_grad, down_grad, up_grad)


def fast(
    tokens,
    cotangent,
    query_key_value_weight,
    attention_out_weight,
    feedforward_in_weight,
    feedforward_out_weight,
    layer_norm_gains,
    biases,
    adapter_down_matrices,
    adapter_up_matrices,
    adapter_of_continuation,
):
    groups = (lax.axis_size("grp"), lax.axis_size("seq"))
    up_cols = 5 * MODEL_WIDTH + HIDDEN_UNITS
    ups_shard = adapter_up_matrices.reshape(4, up_cols)
    up_parts, first = [], 0
    for size in UP_SECTIONS:
        up_parts.append(ups_shard[:, first : first + size].reshape(16, size // 4))
        first += size
    (
        queries,
        keys_values,
        context,
        log_total,
        outputs,
        grad_hidden,
        grad_context,
        early_term,
        inner_one,
        down_qkv,
        up_qkv,
        _,
        _,
        _,
        w_qkv,
        _,
        _,
        _,
    ) = forward_and_gather(
        groups,
        adapter_of_continuation,
        tokens,
        cotangent,
        layer_norm_gains,
        biases.reshape(1, -1),
        [
            adapter_down_matrices.reshape(-1, ADAPTER_RANK).T,
            jnp.concatenate(up_parts, 1),
            query_key_value_weight.reshape(-1, 3 * MODEL_WIDTH),
            attention_out_weight.reshape(-1, MODEL_WIDTH),
            feedforward_in_weight.reshape(-1, HIDDEN_UNITS),
            feedforward_out_weight.reshape(-1, MODEL_WIDTH),
        ],
        1,
    )
    ident = jnp.full((16, 128), adapter_of_continuation[0, 0], jnp.int32).astype(jnp.bfloat16)
    input_grad, down_grad, up_grad = backward_tail(
        groups,
        queries,
        keys_values,
        grad_context,
        context,
        log_total,
        early_term,
        ident,
        tokens,
        grad_hidden,
        layer_norm_gains,
        biases.reshape(1, -1),
        w_qkv,
        (inner_one, down_qkv, up_qkv),
        3,
    )
    down_grad = down_grad.T.reshape(-1)
    up_pieces = []
    for start, size in zip(UP_STARTS, UP_SECTIONS):
        up_pieces.append(up_grad[:, start : start + size // 4].reshape(4, -1))
    up_grad = jnp.concatenate(up_pieces, 1).reshape(-1)
    return (outputs, input_grad, down_grad, up_grad)


def solution(mesh):
    placed = (
        P(("grp", "seq"), None),
        P(("grp", "seq"), None),
        P(("grp", "seq")),
        P(("grp", "seq")),
        P(("grp", "seq")),
        P(("grp", "seq")),
        P(),
        P(),
        P(("grp", "seq")),
        P(("grp", "seq")),
        P(("grp", "seq"), None),
    )
    fits = mesh.shape["grp"] == 4 and mesh.shape["seq"] == 8
    return jax.shard_map(
        fast if fits else local_general,
        mesh=mesh,
        in_specs=placed,
        out_specs=(
            P(("grp", "seq"), None),
            P(("grp", "seq"), None),
            P(("grp", "seq")),
            P(("grp", "seq")),
        ),
        check_vma=False,
    )
```
